32 devices in a mesh: dp: 16 (over z, x, core), tensor: 2 (over y).
Axes of the slice: x: 2, y: 2, z: 4, core: 2. Of those that a mesh axis runs over, the one named last changes fastest.
Arguments:
- activations: bfloat16 [73856, 1024], P(('dp', 'tensor')), may hold values from -6 to 6
- first_gain: bfloat16 [1024], P('dp'), may hold values from 0.25 to 1.75
- first_shift: bfloat16 [1024], P('dp'), may hold values from -4 to 4
- heads_weight: bfloat16 [3, 1024, 1024], P(None, 'dp', 'tensor'), may hold values from -0.1875 to 0.1875
- heads_bias: bfloat16 [2, 16, 64], P(None, 'tensor', 'dp'), may hold values from -4 to 4
- merge_weight: bfloat16 [1024, 1024], P('tensor', 'dp'), may hold values from -2 to 2
- merge_bias: bfloat16 [1024], P('dp'), may hold values from -4 to 4
- second_gain: bfloat16 [1024], P('dp'), may hold values from 0.25 to 1.75
- second_shift: bfloat16 [1024], P('dp'), may hold values from -4 to 4
- expand_weight: bfloat16 [1024, 4096], P('dp', 'tensor'), may hold values from -0.1875 to 0.1875
- expand_bias: bfloat16 [32, 128], P('tensor', 'dp'), may hold values from -6 to 6
- reduce_weight: bfloat16 [4096, 1024], P('tensor', 'dp'), may hold values from -0.125 to 0.125
- reduce_bias: bfloat16 [1024], P('dp'), may hold values from -4 to 4
- output_grad: bfloat16 [73856, 1024], P(('dp', 'tensor')), may hold values from -6 to 6
- real_images: int32 [16], P('dp'), may hold values from 1 to 8, as said below
Outputs:
- block_output: bfloat16 [73856, 1024], P(('dp', 'tensor'))
- input_grad: bfloat16 [73856, 1024], P(('dp', 'tensor'))
- first_gain_grad: float32 [1024], P('dp')
- first_shift_grad: float32 [1024], P('dp')
- heads_weight_grad: float32 [3, 1024, 1024], P(None, 'dp', 'tensor')
- heads_bias_grad: float32 [2, 16, 64], P(None, 'tensor', 'dp')
- merge_weight_grad: float32 [1024, 1024], P('tensor', 'dp')
- merge_bias_grad: float32 [1024], P('dp')
- second_gain_grad: float32 [1024], P('dp')
- second_shift_grad: float32 [1024], P('dp')
- expand_weight_grad: float32 [1024, 4096], P('dp', 'tensor')
- expand_bias_grad: float32 [32, 128], P('tensor', 'dp')
- reduce_weight_grad: float32 [4096, 1024], P('tensor', 'dp')
- reduce_bias_grad: float32 [1024], P('dp')
The draws below stay inside these ranges and needn't reach their ends.
Inputs may be any that keep to these rules, and one draw needn't show every extreme that they name: `real_images`: entry s counts the live images among the 8 slots of dp index s, which come first; some entry equals 8.
All inputs are finite; a program needn't handle non-finite values.
Results may differ from the reference program's by a relative error of at most 0.02.
Values may be sent and summed in bfloat16 or wider, within the bound.
A program may use at most 320 MiB of HBM per device.

```python
import jax
import jax.numpy as jnp
from jax import lax

D = 1024
HEADS = 16
HEAD_DIM = 64
FF = 4096
SEQ = 577
IMAGES_DEV = 8
IMAGES = 128
TOKENS = 73856
SHARDS = 16


def draw_real_images(key, part):
    first, second = jax.random.split(jax.random.fold_in(key, 7))
    counts = jax.random.randint(first, (SHARDS,), 1, IMAGES_DEV + 1, dtype=jnp.int32)
    chosen = jax.random.randint(second, (), 0, SHARDS, dtype=jnp.int32)
    return jnp.where(lax.iota(jnp.int32, SHARDS) == chosen, jnp.int32(IMAGES_DEV), counts)


def shard_levels(rng, shape, cuts, least, top_value):
    level, own = 1.0, jax.random.fold_in(rng, 6)
    for dim, parts in cuts:
        heights = jnp.exp(jax.random.uniform(jax.random.fold_in(own, dim), (parts,), jnp.float32, least / len(cuts), top_value / len(cuts)))
        level = level * jnp.repeat(heights, shape[dim] // parts).reshape([-1 if axis == dim else 1 for axis in range(len(shape))])
    return level


def normal_values(own_key, extent, deviation, reach, cuts=(), held_as=jnp.bfloat16):
    loudness = shard_levels(own_key, extent, cuts, -0.22, 0.18) if cuts else 1.0
    drawn = jax.random.normal(own_key, extent, jnp.float32) * deviation * loudness
    return jnp.minimum(jnp.maximum(drawn, -reach), reach).astype(held_as)


def setup_inputs(seed: int = 0) -> dict:
    arg_keys = jax.random.split(jax.random.key(seed), 16)
    return {
        "activations": normal_values(arg_keys[0], (TOKENS, D), 1.0, 6.0, ((0, 32),)),
        "first_gain": jnp.clip(1.0 + 0.15 * jax.random.normal(arg_keys[1], (D,), jnp.float32), 0.25, 1.75).astype(jnp.bfloat16),
        "first_shift": normal_values(arg_keys[2], (D,), 0.3, 4.0, ((0, 16),)),
        "heads_weight": normal_values(arg_keys[3], (3, D, D), D ** -0.5, 0.1875, ((1, 16), (2, 2))),
        "heads_bias": normal_values(arg_keys[4], (2, HEADS, HEAD_DIM), 0.3, 4.0, ((1, 2), (2, 16))),
        "merge_weight": normal_values(arg_keys[5], (D, D), (max(4 * D // SEQ, 1)) ** -0.5, 2.0, ((0, 2), (1, 16))),
        "merge_bias": normal_values(arg_keys[6], (D,), 0.3, 4.0, ((0, 16),)),
        "second_gain": jnp.clip(1.0 + 0.15 * jax.random.normal(arg_keys[7], (D,), jnp.float32), 0.25, 1.75).astype(jnp.bfloat16),
        "second_shift": normal_values(arg_keys[8], (D,), 0.3, 4.0, ((0, 16),)),
        "expand_weight": normal_values(arg_keys[9], (D, FF), D ** -0.5, 0.1875, ((0, 16), (1, 2))),
        "expand_bias": normal_values(arg_keys[10], (FF // 128, 128), 0.5, 6.0, ((0, 2), (1, 16))),
        "reduce_weight": normal_values(arg_keys[11], (FF, D), (FF // 2) ** -0.5, 0.125, ((0, 2), (1, 16))),
        "reduce_bias": normal_values(arg_keys[12], (D,), 0.3, 4.0, ((0, 16),)),
        "output_grad": normal_values(arg_keys[13], (TOKENS, D), 1.0, 6.0, ((0, 32),)),
        "real_images": draw_real_images(jax.random.fold_in(arg_keys[15], 71), 0),
    }


EPSILON = 1e-06
HIGH = lax.Precision.HIGHEST

@jax.custom_vjp
def low(v):
    return lax.optimization_barrier(v.astype(jnp.bfloat16)).astype(jnp.float32)

@jax.custom_vjp
def low_back(v):
    return v

def low_keep(v):
    return (low(v), None)

def low_pass(kept, grad):
    return (grad,)

def back_keep(v):
    return (v, None)

def back_low(kept, grad):
    return (low(grad),)
low.defvjp(low_keep, low_pass)
low_back.defvjp(back_keep, back_low)

def normalize(values, gain, shift):
    center = values - lax.optimization_barrier(jnp.mean(values, axis=-1, keepdims=True))
    second = lax.optimization_barrier(jnp.mean(center * center, axis=-1, keepdims=True))
    return center * lax.rsqrt(second + EPSILON) * gain + shift

def product(left, right):
    return jnp.dot(left, right, precision=HIGH)

def layer(params, image):
    gain_one, shift_one, heads_weight, heads_bias, merge_weight, merge_bias, gain_two, shift_two, expand_weight, expand_bias, reduce_weight, reduce_bias = params
    normed_one = low(normalize(image, gain_one, shift_one))
    pair = heads_bias.reshape(2, D)
    triple = jnp.stack([product(normed_one, heads_weight[0]) + pair[0], product(normed_one, heads_weight[1]), product(normed_one, heads_weight[2]) + pair[1]])
    triple = low_back(low(triple))
    query = triple[0].reshape(SEQ, HEADS, HEAD_DIM)
    keys = triple[1].reshape(SEQ, HEADS, HEAD_DIM)
    values = triple[2].reshape(SEQ, HEADS, HEAD_DIM)
    raw = low_back(jnp.einsum('qhd,khd->hqk', query, keys, precision=HIGH))
    probs = low(jax.nn.softmax(raw * HEAD_DIM ** (-0.5), axis=-1))
    context = jnp.einsum('hqk,khd->qhd', probs, values, precision=HIGH).reshape(SEQ, D)
    context = low_back(low(context))
    resid = image + (low_back(product(context, merge_weight)) + merge_bias)
    normed_two = low(normalize(resid, gain_two, shift_two))
    hidden_pre = low_back(product(normed_two, expand_weight) + expand_bias.reshape(FF))
    active = low(jax.nn.gelu(hidden_pre, approximate=False))
    return resid + (low_back(product(active, reduce_weight)) + reduce_bias)

def reference(activations, first_gain, first_shift, heads_weight, heads_bias, merge_weight, merge_bias, second_gain, second_shift, expand_weight, expand_bias, reduce_weight, reduce_bias, output_grad, real_images):
    params = tuple((item.astype(jnp.float32) for item in (first_gain, first_shift, heads_weight, heads_bias, merge_weight, merge_bias, second_gain, second_shift, expand_weight, expand_bias, reduce_weight, reduce_bias)))
    images = activations.astype(jnp.float32).reshape(IMAGES, SEQ, D)
    slots = lax.iota(jnp.int32, IMAGES)
    owners = (slots // IMAGES_DEV).astype(jnp.int32)
    live = (slots % IMAGES_DEV < real_images[owners]).astype(jnp.float32)
    cotangent = output_grad.astype(jnp.float32).reshape(IMAGES, SEQ, D) * live[:, None, None]
    stepper = jax.checkpoint(layer)

    def whole(weights, inputs):
        return lax.map(lambda image: stepper(weights, image), inputs)
    outputs, pull = jax.vjp(whole, params, images)
    grads, image_grads = pull(cotangent)
    return (outputs.reshape(TOKENS, D).astype(jnp.bfloat16), image_grads.reshape(TOKENS, D).astype(jnp.bfloat16), grads[0], grads[1], grads[2], grads[3], grads[4], grads[5], grads[6], grads[7], grads[8], grads[9], grads[10], grads[11])
```

```python
import functools

import jax
import jax.numpy as jnp
from jax import lax
from jax.experimental import pallas as pl
from jax.experimental.pallas import tpu as pltpu
from jax.sharding import PartitionSpec as P

HEAD_DIM = 64
SEQ = 577
PAD = 592
EPSILON = 1e-06
LOG_SCALE = 0.125
bf16 = jnp.bfloat16
f32 = jnp.float32
NN = (((1,), (0,)), ((), ()))
NT = (((1,), (1,)), ((), ()))
TN = (((0,), (0,)), ((), ()))
VMEM_BYTES = 60 * 2**20
AXES = ("tensor", "dp")


def matmul(left, right, dims=NN):
    return lax.dot_general(left, right, dims, preferred_element_type=f32)


def norm_parts(values):
    center = values - jnp.mean(values, axis=-1, keepdims=True)
    second = jnp.mean(center * center, axis=-1, keepdims=True)
    inv = lax.rsqrt(second + EPSILON)
    return center * inv, inv


def gelu_and_slope(pre):
    size = jnp.abs(pre)
    bell = jnp.exp(pre * pre * -0.5)
    t = 1.0 / (1.0 + size * (0.3275911 * 0.7071067811865476))
    poly = t * (
        0.254829592
        + t * (-0.284496736 + t * (1.421413741 + t * (-1.453152027 + t * 1.061405429)))
    )
    tail = (0.5 * poly) * bell
    phi = jnp.where(pre >= 0, 1.0 - tail, tail)
    return pre * phi, phi + pre * (bell * 0.3989422804014327)


def full(shape):
    return pl.BlockSpec(shape, lambda *_: (0,) * len(shape), pipeline_mode=pl.Buffered(1))


def call(kernel, name, grid, in_specs, out_specs, out_shape, args, scratch=()):
    return pl.pallas_call(
        kernel,
        grid=grid,
        in_specs=in_specs,
        out_specs=out_specs,
        out_shape=[jax.ShapeDtypeStruct(s, d) for s, d in out_shape],
        scratch_shapes=list(scratch),
        compiler_params=pltpu.CompilerParams(vmem_limit_bytes=VMEM_BYTES),
        name=name,
    )(*args)


def qkv_kernel(x_ref, gain_ref, shift_ref, bias_ref, w_ref, normed_ref, triple_ref):
    hat, _ = norm_parts(x_ref[...].astype(f32))
    normed = (hat * gain_ref[...] + shift_ref[...]).astype(bf16)
    normed_ref[...] = normed
    tensor, dp, rows, _ = w_ref.shape
    width = w_ref.shape[3] // 3
    for s in range(3):
        for t in range(tensor):
            cols = slice(t * width, (t + 1) * width)
            w = w_ref[t, :, :, s * width : (s + 1) * width].reshape(dp * rows, width)
            out = matmul(normed, w)
            if s != 1:
                out = out + bias_ref[s // 2 : s // 2 + 1, cols]
            triple_ref[s, :, cols] = out.astype(bf16)


def attend_kernel(triple_ref, context_ref, stat_ref):
    rows = lax.broadcasted_iota(jnp.int32, (PAD, 1), 0)
    mask = jnp.where(rows < SEQ, 0.0, -1e30)
    for h in range(triple_ref.shape[2] // HEAD_DIM):
        cols = slice(HEAD_DIM * h, HEAD_DIM * (h + 1))
        query = triple_ref[0, :, cols] * bf16(LOG_SCALE)
        scores = matmul(triple_ref[1, :, cols], query, NT) + mask
        top = jnp.max(scores, axis=0, keepdims=True)
        expo = jnp.exp(scores - top)
        total = jnp.sum(expo, axis=0, keepdims=True)
        probs = (expo * (1.0 / total)).astype(bf16)
        context_ref[:, cols] = matmul(probs, triple_ref[2, :, cols], TN).astype(bf16)
        stat_ref[0, h : h + 1, :] = top + jnp.log(total)


def attend_back_kernel(triple_ref, stat_ref, grad_ref, out_ref):
    rows = lax.broadcasted_iota(jnp.int32, (PAD, 1), 0)
    mask = jnp.where(rows < SEQ, 0.0, -1e30)
    for h in range(triple_ref.shape[2] // HEAD_DIM):
        cols = slice(HEAD_DIM * h, HEAD_DIM * (h + 1))
        query = triple_ref[0, :, cols]
        keys = triple_ref[1, :, cols]
        grad = grad_ref[:, cols]
        scores = matmul(keys, query * bf16(LOG_SCALE), NT) + mask
        probs = jnp.exp(scores - stat_ref[0, h : h + 1, :])
        grad_probs = matmul(triple_ref[2, :, cols], grad, NT)
        inner = jnp.sum(probs * grad_probs, axis=0, keepdims=True)
        grad_scores = (probs * (grad_probs - inner) * LOG_SCALE).astype(bf16)
        out_ref[2, :, cols] = matmul(probs.astype(bf16), grad).astype(bf16)
        out_ref[1, :, cols] = matmul(grad_scores, query).astype(bf16)
        out_ref[0, :, cols] = matmul(grad_scores, keys, TN).astype(bf16)


def merge_kernel(ctx_ref, x_ref, bias_ref, gain_ref, shift_ref, w_ref, resid_ref, normed_ref):
    tensor, dp, rows, width = w_ref.shape
    total = x_ref[...].astype(f32) + bias_ref[...]
    for t in range(tensor):
        w = w_ref[t].reshape(dp * rows, width)
        total = total + matmul(ctx_ref[:, t * width : (t + 1) * width], w, NT)
    resid_ref[...] = total
    hat, _ = norm_parts(total)
    normed_ref[...] = (hat * gain_ref[...] + shift_ref[...]).astype(bf16)


def mlp_kernel(chunk, normed_ref, resid_ref, ebias_ref, rbias_ref, e_ref, r_ref, out_ref, act_ref, slope_ref):
    tensor, dp, rows, width = e_ref.shape
    normed = normed_ref[...]
    total = resid_ref[...] + rbias_ref[...]
    for t in range(tensor):
        for c in range(width // chunk):
            local = slice(c * chunk, (c + 1) * chunk)
            cols = slice(t * width + c * chunk, t * width + (c + 1) * chunk)
            e = e_ref[t, :, :, local].reshape(dp * rows, chunk)
            active, slope = gelu_and_slope(matmul(normed, e) + ebias_ref[:, cols])
            active = active.astype(bf16)
            act_ref[:, cols] = active
            slope_ref[:, cols] = slope.astype(bf16)
            r = r_ref[t, :, :, local].reshape(dp * rows, chunk)
            total = total + matmul(active, r, NT)
    out_ref[...] = total.astype(bf16)


def accumulate(first, ref, value):
    @pl.when(first)
    def _():
        ref[...] = value

    @pl.when(jnp.logical_not(first))
    def _():
        ref[...] += value


def norm_back(values, gain, grad):
    hat, inv = norm_parts(values)
    scaled = grad * gain
    back = (
        scaled
        - jnp.mean(scaled, axis=-1, keepdims=True)
        - hat * jnp.mean(scaled * hat, axis=-1, keepdims=True)
    ) * inv
    return back, jnp.sum(grad * hat, axis=0, keepdims=True), jnp.sum(grad, axis=0, keepdims=True)


def mlp_back_kernel(
    chunk, grad_ref, slope_ref, resid_ref, gain_ref, e_ref, r_ref, m_ref,
    pre_ref, low_ref, ctx_ref, sums_ref, esum_ref,
):
    tensor, dp, rows, width = e_ref.shape
    first = pl.program_id(0) == 0
    grad = grad_ref[...]
    total = jnp.zeros(grad.shape, f32)
    parts = []
    for t in range(tensor):
        for c in range(width // chunk):
            local = slice(c * chunk, (c + 1) * chunk)
            cols = slice(t * width + c * chunk, t * width + (c + 1) * chunk)
            r = r_ref[t, :, :, local].reshape(dp * rows, chunk)
            pre = (matmul(grad, r) * slope_ref[:, cols].astype(f32)).astype(bf16)
            pre_ref[:, cols] = pre
            parts.append(jnp.sum(pre.astype(f32), axis=0, keepdims=True))
            e = e_ref[t, :, :, local].reshape(dp * rows, chunk)
            total = total + matmul(pre, e, NT)
    grad = grad.astype(f32)
    back, gain_sum, shift_sum = norm_back(resid_ref[...], gain_ref[...], total)
    resid_grad = grad + back
    low = resid_grad.astype(bf16)
    low_ref[...] = low
    wide = m_ref.shape[3]
    for t in range(tensor):
        m = m_ref[t].reshape(dp * rows, wide)
        ctx_ref[:, t * wide : (t + 1) * wide] = matmul(low, m).astype(bf16)
    sums = jnp.concatenate(
        [
            jnp.sum(grad, axis=0, keepdims=True),
            gain_sum,
            shift_sum,
            jnp.sum(resid_grad, axis=0, keepdims=True),
        ],
        axis=0,
    )
    accumulate(first, sums_ref, sums)
    accumulate(first, esum_ref, jnp.concatenate(parts, axis=1))


def qkv_back_kernel(x_ref, low_ref, gain_ref, grad_ref, w_ref, out_ref, sums_ref, bsum_ref):
    tensor, dp, rows, _ = w_ref.shape
    width = w_ref.shape[3] // 3
    first = pl.program_id(0) == 0
    total = jnp.zeros(x_ref.shape, f32)
    for s in range(3):
        for t in range(tensor):
            w = w_ref[t, :, :, s * width : (s + 1) * width].reshape(dp * rows, width)
            total = total + matmul(grad_ref[s, :, t * width : (t + 1) * width], w, NT)
    back, gain_sum, shift_sum = norm_back(x_ref[...].astype(f32), gain_ref[...], total)
    out_ref[...] = (low_ref[...].astype(f32) + back).astype(bf16)
    accumulate(first, sums_ref, jnp.concatenate([gain_sum, shift_sum], axis=0))
    bias = [jnp.sum(grad_ref[s].astype(f32), axis=0, keepdims=True) for s in (0, 2)]
    accumulate(first, bsum_ref, jnp.concatenate(bias, axis=0))


def weight_grad_kernel(left_ref, right_ref, out_ref, turned):
    @pl.when(pl.program_id(0) == 0)
    def _():
        turned[...] = left_ref[...].T

    out = matmul(turned[...], right_ref[...].reshape(right_ref.shape[-2:]))
    out_ref[...] = out.astype(bf16).reshape(out_ref.shape)


def weight_grad(name, left, right, tensor, dp, block):
    count, rows, width = right.shape
    deep = left.shape[1]
    local = width // tensor
    block = min(block, local)
    per = local // block
    steps = count * tensor * per

    def where(i):
        return i // (tensor * per), (i // per) % tensor, i % per

    def right_map(i):
        s, t, b = where(i)
        return (s, 0, t * per + b)

    def out_map(i):
        s, t, b = where(i)
        return (t, 0, 0, s * per + b)

    return call(
        weight_grad_kernel,
        name,
        (steps,),
        [full((rows, deep)), pl.BlockSpec((1, rows, block), right_map)],
        [pl.BlockSpec((1, dp, deep // dp, block), out_map)],
        [((tensor, dp, deep // dp, count * local), bf16)],
        (left, right),
        [pltpu.VMEM((deep, rows), bf16)],
    )[0]


def shards(
    tensor,
    dp,
    activations,
    first_gain,
    first_shift,
    heads_weight,
    heads_bias,
    merge_weight,
    merge_bias,
    second_gain,
    second_shift,
    expand_weight,
    expand_bias,
    reduce_weight,
    reduce_bias,
    output_grad,
    real_images,
):
    rows, deep = activations.shape
    images = rows // SEQ
    part = deep // dp
    own = heads_weight.shape[2]
    hidden_own = expand_weight.shape[1]
    hidden = hidden_own * tensor
    heads = deep // HEAD_DIM

    def gather(shard):
        out = lax.all_gather(shard, AXES, axis=0, tiled=True)
        return out.reshape(tensor, dp, *shard.shape)

    small_parts = [
        first_gain, first_shift, merge_bias, second_gain, second_shift, reduce_bias,
        heads_bias.reshape(-1), expand_bias.reshape(-1),
    ]
    small = gather(jnp.concatenate(small_parts)[None, :])[:, :, 0]
    wide_heads = gather(heads_weight.transpose(1, 0, 2).reshape(part, 3 * own))
    wide_merge = gather(merge_weight.T)
    wide_expand = gather(expand_weight)
    wide_reduce = gather(reduce_weight.T)

    vectors = small[0, :, : 6 * part].astype(f32).reshape(dp, 6, part)
    vectors = vectors.transpose(1, 0, 2).reshape(6, 1, deep)
    gain_one, shift_one, merge_shift, gain_two, shift_two, reduce_shift = vectors
    hb = small[:, :, 6 * part : 6 * part + heads_bias.size].astype(f32)
    hb = hb.reshape((tensor, dp) + heads_bias.shape).transpose(2, 0, 3, 1, 4).reshape(2, deep)
    eb = small[:, :, 6 * part + heads_bias.size :].astype(f32)
    eb = eb.reshape((tensor, dp) + expand_bias.shape).transpose(0, 2, 1, 3).reshape(1, hidden)

    def padded(values):
        values = values.reshape(images, SEQ, deep)
        return jnp.pad(values, ((0, 0), (0, PAD - SEQ), (0, 0))).reshape(images * PAD, deep)

    def unpadded(values):
        return values.reshape(images, PAD, deep)[:, :SEQ].reshape(rows, deep)

    full_rows = images * PAD
    inputs = padded(activations)
    ids = lax.axis_index("tensor") * images + lax.iota(jnp.int32, images)
    live = (ids < real_images[0]).astype(bf16)
    grad = padded((output_grad.reshape(images, SEQ, deep) * live[:, None, None]).reshape(rows, deep))

    def by_rows(width, block=PAD):
        return pl.BlockSpec((block, width), lambda i: (i, 0))

    vec = full((1, deep))
    triple_spec = pl.BlockSpec((3, PAD, deep), lambda i: (0, i, 0))
    normed_one, triple = call(
        qkv_kernel,
        "qkv",
        (images,),
        [by_rows(deep), vec, vec, full((2, deep)), full(wide_heads.shape)],
        [by_rows(deep), triple_spec],
        [((full_rows, deep), bf16), ((3, full_rows, deep), bf16)],
        (inputs, gain_one, shift_one, hb, wide_heads),
    )

    group = 4
    groups = heads // group
    head_spec = pl.BlockSpec((3, PAD, group * HEAD_DIM), lambda i, g: (0, i, g))
    ctx_spec = pl.BlockSpec((PAD, group * HEAD_DIM), lambda i, g: (i, g))
    stat_spec = pl.BlockSpec((1, group, PAD), lambda i, g: (i * groups + g, 0, 0))
    context, stat = call(
        attend_kernel,
        "attend",
        (images, groups),
        [head_spec],
        [ctx_spec, stat_spec],
        [((full_rows, deep), bf16), ((images * groups, group, PAD), f32)],
        (triple,),
    )

    resid, normed_two = call(
        merge_kernel,
        "merge",
        (images,),
        [by_rows(deep), by_rows(deep), vec, vec, vec, full(wide_merge.shape)],
        [by_rows(deep), by_rows(deep)],
        [((full_rows, deep), f32), ((full_rows, deep), bf16)],
        (context, inputs, merge_shift, gain_two, shift_two, wide_merge),
    )

    chunk = min(512, hidden_own)
    half = PAD // 2
    output, active, slope = call(
        functools.partial(mlp_kernel, chunk),
        "mlp",
        (full_rows // half,),
        [
            by_rows(deep, half), by_rows(deep, half), full((1, hidden)), vec,
            full(wide_expand.shape), full(wide_reduce.shape),
        ],
        [by_rows(deep, half), by_rows(hidden, half), by_rows(hidden, half)],
        [((full_rows, deep), bf16), ((full_rows, hidden), bf16), ((full_rows, hidden), bf16)],
        (normed_two, resid, eb, reduce_shift, wide_expand, wide_reduce),
    )

    def scatter(grads):
        grads = grads.reshape(tensor * dp * grads.shape[2], grads.shape[3])
        return lax.psum_scatter(grads, AXES, scatter_dimension=0, tiled=True)

    def gradient(name, left, right, block=512):
        return scatter(weight_grad(name, left, right, tensor, dp, block))

    grad_reduce = gradient("grad_reduce", grad, active[None])

    pre_grad, resid_low, grad_context, sums_two, esum = call(
        functools.partial(mlp_back_kernel, chunk),
        "mlp_back",
        (full_rows // half,),
        [
            by_rows(deep, half), by_rows(hidden, half), by_rows(deep, half), vec,
            full(wide_expand.shape), full(wide_reduce.shape), full(wide_merge.shape),
        ],
        [
            by_rows(hidden, half), by_rows(deep, half), by_rows(deep, half),
            pl.BlockSpec((4, deep), lambda i: (0, 0)), pl.BlockSpec((1, hidden), lambda i: (0, 0)),
        ],
        [
            ((full_rows, hidden), bf16), ((full_rows, deep), bf16), ((full_rows, deep), bf16),
            ((4, deep), f32), ((1, hidden), f32),
        ],
        (grad, slope, resid, gain_two, wide_expand, wide_reduce, wide_merge),
    )
    grad_expand = gradient("grad_expand", normed_two, pre_grad[None])
    grad_merge = gradient("grad_merge", resid_low, context[None])

    grad_triple = call(
        attend_back_kernel,
        "attend_back",
        (images, groups),
        [head_spec, stat_spec, ctx_spec],
        [head_spec],
        [((3, full_rows, deep), bf16)],
        (triple, stat, grad_context),
    )[0]
    grad_heads = gradient("grad_heads", normed_one, grad_triple)

    input_grad, sums_one, bsum = call(
        qkv_back_kernel,
        "qkv_back",
        (images,),
        [by_rows(deep), by_rows(deep), vec, triple_spec, full(wide_heads.shape)],
        [by_rows(deep), pl.BlockSpec((2, deep), lambda i: (0, 0)), pl.BlockSpec((2, deep), lambda i: (0, 0))],
        [((full_rows, deep), bf16), ((2, deep), f32), ((2, deep), f32)],
        (inputs, resid_low, gain_one, grad_triple, wide_heads),
    )

    shared = jnp.concatenate([sums_one, sums_two[3:], sums_two[1:3], sums_two[:1]], axis=0)
    shared = shared.reshape(6, dp, part).transpose(1, 0, 2).reshape(1, dp, 6 * part)
    shared = jnp.broadcast_to(shared, (tensor, dp, 6 * part))
    hbs = heads_bias.shape
    bsum = bsum.reshape(2, tensor, hbs[1], dp, hbs[2]).transpose(1, 3, 0, 2, 4)
    ebs = expand_bias.shape
    esum = esum.reshape(tensor, ebs[0], dp, ebs[1]).transpose(0, 2, 1, 3)
    packed = jnp.concatenate(
        [shared, bsum.reshape(tensor, dp, -1), esum.reshape(tensor, dp, -1)], axis=2
    )
    packed = lax.psum_scatter(
        packed.reshape(tensor * dp, -1), AXES, scatter_dimension=0, tiled=True
    )[0]
    vector = packed[: 6 * part].reshape(6, part)
    hb_grad = packed[6 * part : 6 * part + heads_bias.size].reshape(hbs)
    eb_grad = packed[6 * part + heads_bias.size :].reshape(ebs)

    return (
        unpadded(output),
        unpadded(input_grad),
        vector[0],
        vector[1],
        grad_heads.astype(f32).reshape(part, 3, own).transpose(1, 0, 2),
        hb_grad,
        grad_merge.astype(f32).T,
        vector[2],
        vector[3],
        vector[4],
        grad_expand.astype(f32),
        eb_grad,
        grad_reduce.astype(f32).T,
        vector[5],
    )


def solution(mesh):
    rows = P(("dp", "tensor"), None)
    specs = (
        P("dp"),
        P("dp"),
        P(None, "dp", "tensor"),
        P(None, "tensor", "dp"),
        P("tensor", "dp"),
        P("dp"),
        P("dp"),
        P("dp"),
        P("dp", "tensor"),
        P("tensor", "dp"),
        P("tensor", "dp"),
        P("dp"),
    )
    return jax.shard_map(
        functools.partial(shards, mesh.shape["tensor"], mesh.shape["dp"]),
        mesh=mesh,
        in_specs=(rows,) + specs + (rows, P("dp")),
        out_specs=(rows, rows) + specs,
        check_vma=False,
    )
```

```python
import functools
import math

import jax
import jax.numpy as jnp
from jax import lax
from jax.experimental import pallas as pl
from jax.experimental.pallas import tpu as pltpu
from jax.sharding import PartitionSpec as P

HEAD_DIM = 64
SEQ = 577
STRIDE = 576
WINDOW = 592
EPSILON = 1e-06
LOG_SCALE = 0.125
bf16 = jnp.bfloat16
f32 = jnp.float32
NN = (((1,), (0,)), ((), ()))
NT = (((1,), (1,)), ((), ()))
TN = (((0,), (0,)), ((), ()))
VMEM_BYTES = 60 * 2**20
AXES = ("tensor", "dp")


def matmul(left, right, dims=NN):
    return lax.dot_general(left, right, dims, preferred_element_type=f32)


def norm_parts(values):
    center = values - jnp.mean(values, axis=-1, keepdims=True)
    second = jnp.mean(center * center, axis=-1, keepdims=True)
    inv = lax.rsqrt(second + EPSILON)
    return center * inv, inv


def gelu_and_slope(pre):
    phi = 0.5 + 0.5 * lax.erf(pre * 0.7071067811865476)
    bell = jnp.exp(pre * pre * -0.5)
    return pre * phi, phi + pre * (bell * 0.3989422804014327)


def full(shape):
    return pl.BlockSpec(shape, lambda *_: (0,) * len(shape), pipeline_mode=pl.Buffered(1))


def call(kernel, name, grid, in_specs, out_specs, out_shape, args, scratch=(), flops=0, prefetch=0, aliases={}, **params):
    moved = 0
    if flops:
        moved = sum(a.size * a.dtype.itemsize for a in args)
        moved += sum(math.prod(shape) * jnp.dtype(dtype).itemsize for shape, dtype in out_shape)
    return pl.pallas_call(
        kernel,
        grid_spec=pltpu.PrefetchScalarGridSpec(
            num_scalar_prefetch=prefetch,
            grid=grid,
            in_specs=in_specs,
            out_specs=out_specs,
            scratch_shapes=list(scratch),
        ),
        out_shape=[jax.ShapeDtypeStruct(shape, dtype) for shape, dtype in out_shape],
        input_output_aliases=aliases,
        compiler_params=pltpu.CompilerParams(vmem_limit_bytes=VMEM_BYTES, **params),
        cost_estimate=pl.CostEstimate(flops=2 * flops, bytes_accessed=moved, transcendentals=0),
        name=name,
    )(*args)


def before(ref, count):
    height = ref.shape[0]
    rows = pl.program_id(0) * height + lax.broadcasted_iota(jnp.int32, (height, 1), 0)
    return jnp.where(rows < count, ref[...].astype(f32), 0.0)


def qkv_kernel(part, count, x_ref, vec_ref, bias_ref, w_ref, normed_ref, triple_ref):
    hat, _ = norm_parts(before(x_ref, count))
    normed = (hat * vec_ref[0:1] + vec_ref[1:2]).astype(bf16)
    normed_ref[...] = normed
    tensor, dp = w_ref.shape[:2]
    width = w_ref.shape[3] // 3
    for s in range(3):
        for t in range(tensor):
            cols = slice(t * width, (t + 1) * width)
            w = w_ref[t, :, :part, s * width : (s + 1) * width].reshape(dp * part, width)
            out = matmul(normed, w)
            if s != 1:
                out = out + bias_ref[s // 2 : s // 2 + 1, cols]
            triple_ref[s, :, cols] = out.astype(bf16)


def window(image):
    start = pl.multiple_of(image * STRIDE, 16)
    return pl.ds(start, WINDOW)


def keep_before(image, ref, index, value):
    edge = pl.ds(pl.multiple_of(image * STRIDE, 16), 16)
    rest = pl.ds(pl.multiple_of(image * STRIDE + 16, 16), WINDOW - 16)
    rows = lax.broadcasted_iota(jnp.int32, (16, 1), 0)
    head = jnp.where(rows < image, ref[(*index[:-1], edge, index[-1])].astype(f32), value[:16])
    ref[(*index[:-1], edge, index[-1])] = head.astype(ref.dtype)
    ref[(*index[:-1], rest, index[-1])] = value[16:].astype(ref.dtype)


def attend_kernel(triple_ref, context_ref, stat_ref):
    image = pl.program_id(1)
    lanes = lax.broadcasted_iota(jnp.int32, (1, WINDOW), 1)
    mask = jnp.where((lanes >= image) & (lanes < image + SEQ), 0.0, -1e30)
    own = window(image)
    stats = []
    for h in range(triple_ref.shape[2] // HEAD_DIM):
        cols = slice(HEAD_DIM * h, HEAD_DIM * (h + 1))
        query = triple_ref[0, own, cols] * bf16(LOG_SCALE)
        scores = matmul(query, triple_ref[1, own, cols], NT) + mask
        top = jnp.max(scores, axis=1, keepdims=True)
        expo = jnp.exp(scores - top)
        total = jnp.sum(expo, axis=1, keepdims=True)
        context = matmul(expo.astype(bf16), triple_ref[2, own, cols]) * (1.0 / total)
        keep_before(image, context_ref, (cols,), context)
        stats.append(top + jnp.log(total))
    stat_ref[0] = jnp.concatenate(stats, axis=1).T


def attend_back_kernel(triple_ref, stat_ref, grad_ref, *refs):
    out_ref = refs[-1]
    image = pl.program_id(1)
    rows = lax.broadcasted_iota(jnp.int32, (WINDOW, 1), 0)
    mask = jnp.where((rows >= image) & (rows < image + SEQ), 0.0, -1e30)
    lanes = lax.broadcasted_iota(jnp.int32, (1, WINDOW), 1)
    real = (lanes >= image) & (lanes < image + SEQ)
    own = window(image)
    for h in range(triple_ref.shape[2] // HEAD_DIM):
        cols = slice(HEAD_DIM * h, HEAD_DIM * (h + 1))
        query = triple_ref[0, own, cols]
        keys = triple_ref[1, own, cols]
        grad = grad_ref[own, cols]
        scores = matmul(keys, query * bf16(LOG_SCALE), NT) + mask
        probs = jnp.exp(scores - jnp.where(real, stat_ref[0, h : h + 1, :], 1e30))
        grad_probs = matmul(triple_ref[2, own, cols], grad, NT)
        inner = jnp.sum(probs * grad_probs, axis=0, keepdims=True)
        grad_scores = (probs * (grad_probs - inner)).astype(bf16)
        keep_before(image, out_ref, (2, cols), matmul(probs.astype(bf16), grad))
        keep_before(image, out_ref, (1, cols), matmul(grad_scores, query) * LOG_SCALE)
        keep_before(image, out_ref, (0, cols), (matmul(keys.T, grad_scores) * LOG_SCALE).T)


def merge_kernel(count, ctx_ref, x_ref, vec_ref, w_ref, resid_ref, normed_ref):
    tensor, dp, rows, width = w_ref.shape
    total = before(x_ref, count) + vec_ref[2:3]
    for t in range(tensor):
        w = w_ref[t].reshape(dp * rows, width)
        total = total + matmul(ctx_ref[:, t * width : (t + 1) * width], w, NT)
    resid_ref[...] = total
    hat, _ = norm_parts(total)
    normed_ref[...] = (hat * vec_ref[3:4] + vec_ref[4:5]).astype(bf16)


def mlp_kernel(
    chunk, live_ref, normed_ref, resid_ref, ebias_ref, vec_ref, e_ref, r_ref, given_ref,
    out_ref, act_ref, slope_ref, grad_ref,
):
    grad_ref[...] = before(given_ref, live_ref[0]).astype(bf16)
    tensor, dp, rows, width = e_ref.shape
    normed = normed_ref[...]
    total = resid_ref[...] + vec_ref[5:6]
    for t in range(tensor):
        for c in range(width // chunk):
            local = slice(c * chunk, (c + 1) * chunk)
            cols = slice(t * width + c * chunk, t * width + (c + 1) * chunk)
            e = e_ref[t, :, :, local].reshape(dp * rows, chunk)
            active, slope = gelu_and_slope(matmul(normed, e) + ebias_ref[:, cols])
            active = active.astype(bf16)
            act_ref[:, cols] = active
            slope_ref[:, cols] = slope.astype(bf16)
            r = r_ref[t, :, :, local].reshape(dp * rows, chunk)
            total = total + matmul(active, r, NT)
    out_ref[...] = total.astype(bf16)


def accumulate(first, ref, value):
    @pl.when(first)
    def _():
        ref[...] = value

    @pl.when(jnp.logical_not(first))
    def _():
        ref[...] += value


def norm_back(values, gain, grad):
    hat, inv = norm_parts(values)
    scaled = grad * gain
    back = (
        scaled
        - jnp.mean(scaled, axis=-1, keepdims=True)
        - hat * jnp.mean(scaled * hat, axis=-1, keepdims=True)
    ) * inv
    return back, jnp.sum(grad * hat, axis=0, keepdims=True), jnp.sum(grad, axis=0, keepdims=True)


def mlp_back_kernel(
    chunk, grad_ref, slope_ref, resid_ref, vec_ref, e_ref, r_ref, m_ref,
    pre_ref, low_ref, ctx_ref, sums_ref, esum_ref,
):
    tensor, dp, rows, width = e_ref.shape
    first = pl.program_id(0) == 0
    grad = grad_ref[...]
    total = jnp.zeros(grad.shape, f32)
    parts = []
    for t in range(tensor):
        for c in range(width // chunk):
            local = slice(c * chunk, (c + 1) * chunk)
            cols = slice(t * width + c * chunk, t * width + (c + 1) * chunk)
            r = r_ref[t, :, :, local].reshape(dp * rows, chunk)
            pre = (matmul(grad, r) * slope_ref[:, cols].astype(f32)).astype(bf16)
            pre_ref[:, cols] = pre
            parts.append(jnp.sum(pre.astype(f32), axis=0, keepdims=True))
            e = e_ref[t, :, :, local].reshape(dp * rows, chunk)
            total = total + matmul(pre, e, NT)
    grad = grad.astype(f32)
    back, gain_sum, shift_sum = norm_back(resid_ref[...], vec_ref[3:4], total)
    resid_grad = grad + back
    low = resid_grad.astype(bf16)
    low_ref[...] = low
    wide = m_ref.shape[3]
    for t in range(tensor):
        m = m_ref[t].reshape(dp * rows, wide)
        ctx_ref[:, t * wide : (t + 1) * wide] = matmul(low, m).astype(bf16)
    sums = jnp.concatenate(
        [
            jnp.sum(grad, axis=0, keepdims=True),
            gain_sum,
            shift_sum,
            jnp.sum(resid_grad, axis=0, keepdims=True),
        ],
        axis=0,
    )
    accumulate(first, sums_ref, sums)
    parts = jnp.concatenate(parts, axis=1)
    lines = [parts[:, k * 128 : (k + 1) * 128] for k in range(esum_ref.shape[0])]
    accumulate(first, esum_ref, jnp.concatenate(lines, axis=0))


def qkv_back_kernel(part, count, x_ref, low_ref, vec_ref, grad_ref, w_ref, out_ref, sums_ref, bsum_ref):
    tensor, dp = w_ref.shape[:2]
    width = w_ref.shape[3] // 3
    first = pl.program_id(0) == 0
    total = jnp.zeros(x_ref.shape, f32)
    for s in range(3):
        for t in range(tensor):
            w = w_ref[t, :, :part, s * width : (s + 1) * width].reshape(dp * part, width)
            total = total + matmul(grad_ref[s, :, t * width : (t + 1) * width], w, NT)
    back, gain_sum, shift_sum = norm_back(before(x_ref, count), vec_ref[0:1], total)
    out_ref[...] = (low_ref[...].astype(f32) + back).astype(bf16)
    accumulate(first, sums_ref, jnp.concatenate([gain_sum, shift_sum], axis=0))
    bias = [jnp.sum(grad_ref[s].astype(f32), axis=0, keepdims=True) for s in (0, 2)]
    accumulate(first, bsum_ref, jnp.concatenate(bias, axis=0))


def weight_grad_kernel(starts, *refs):
    count = len(starts) - 1
    lefts, rights, out_ref, turned = refs[:count], refs[count : 2 * count], refs[-2], refs[-1]
    step = pl.program_id(0)
    for j in range(count):
        @pl.when((step >= starts[j]) & (step < starts[j + 1]))
        def _():
            @pl.when(step == starts[j])
            def _():
                turned[...] = lefts[j][...].T

            out = matmul(turned[...], rights[j][0])
            out_ref[...] = out.astype(bf16).reshape(out_ref.shape)


def weight_grads(name, pairs, tensor, dp, block):
    rows, deep = pairs[0][0].shape
    locals_ = [right.shape[1] // tensor for _, right in pairs]
    block = min([block] + locals_)
    pers = [local // block for local in locals_]
    starts = [0]
    for per in pers:
        starts.append(starts[-1] + tensor * per)

    def right_map(j, i):
        i = jnp.clip(i - starts[j], 0, tensor * pers[j] - 1)
        return (0, 0, i)

    def out_map(i):
        where, column, t = 0, 0, 0
        for j, per in enumerate(pers):
            inside = (i >= starts[j]) & (i < starts[j + 1])
            t = t + jnp.where(inside, (i - starts[j]) // per, 0)
            column = column + jnp.where(inside, where + (i - starts[j]) % per, 0)
            where += per
        return (t, 0, 0, column)

    return call(
        functools.partial(weight_grad_kernel, starts),
        name,
        (starts[-1],),
        [full((rows, deep))] * len(pairs)
        + [pl.BlockSpec((1, rows, block), functools.partial(right_map, j)) for j in range(len(pairs))],
        [pl.BlockSpec((1, dp, deep // dp, block), out_map)],
        [((tensor, dp, deep // dp, sum(locals_)), bf16)],
        [left for left, _ in pairs] + [right[None] for _, right in pairs],
        [pltpu.VMEM((deep, rows), bf16)],
        flops=rows * deep * tensor * sum(locals_),
    )[0]


def slot_grad_kernel(tensor, dp, starts, me_ref, *refs):
    count = len(starts) - 1
    lefts, rights = refs[:count], refs[count : 2 * count]
    keep_ref, send_ref, turned, total = refs[2 * count :]
    step, t = pl.program_id(0), pl.program_id(1)
    for j in range(count):
        @pl.when((step >= starts[j]) & (step < starts[j + 1]))
        def _():
            @pl.when((step == starts[j]) & (t == 0))
            def _():
                turned[...] = lefts[j][...].T

            total[...] = matmul(turned[...], rights[j][0])
    part = total.shape[0] // dp
    depth = dp // 4
    column = t ^ me_ref[1]
    for r in range(dp):
        owner = me_ref[0] ^ r
        slot = (((r >> 1) & 1) * tensor + column) * depth + (r >> 2)
        half = send_ref if r & 1 else keep_ref
        half[slot] = total[pl.ds(pl.multiple_of(owner * part, part), part), :].astype(bf16)


def slot_grads(name, pairs, tensor, dp, me, block):
    rows, deep = pairs[0][0].shape
    block = min([block] + [right.shape[2] // tensor for _, right in pairs])
    pers = [right.shape[2] // tensor // block for _, right in pairs]
    starts = [0]
    for (_, right), per in zip(pairs, pers):
        starts.append(starts[-1] + right.shape[0] * per)
    half = tensor * dp // 2

    def right_map(j, i, t, me):
        i = jnp.clip(i - starts[j], 0, starts[j + 1] - starts[j] - 1)
        return (i // pers[j], 0, t * pers[j] + i % pers[j])

    left_spec = pl.BlockSpec((rows, deep), lambda i, t, me: (0, 0), pipeline_mode=pl.Buffered(1))
    spec = pl.BlockSpec((half, deep // dp, block), lambda i, t, me: (0, 0, i))
    return call(
        functools.partial(slot_grad_kernel, tensor, dp, starts),
        name,
        (starts[-1], tensor),
        [left_spec] * len(pairs)
        + [pl.BlockSpec((1, rows, block), functools.partial(right_map, j)) for j in range(len(pairs))],
        [spec, spec],
        [((half, deep // dp, starts[-1] * block), bf16)] * 2,
        [me] + [left for left, _ in pairs] + [right for _, right in pairs],
        [pltpu.VMEM((deep, rows), bf16), pltpu.VMEM((deep, block), f32)],
        prefetch=1,
    )


def swap(values, d, t, tensor, dp):
    moves = []
    for p in range(dp):
        for q in range(tensor):
            moves.append((p * tensor + q, (p ^ d) * tensor + (q ^ t)))
    return lax.ppermute(values, ("dp", "tensor"), moves)


def sum_cores(keep, other, tensor, dp):
    depth = dp // 4
    parts = []
    for k in range(2 * tensor):
        own = slice(k * depth, (k + 1) * depth)
        parts.append((keep[own].astype(f32) + other[own].astype(f32)).astype(bf16))
    return parts


def send_plane(parts, tensor, dp):
    return [swap(parts[k], 2 * (k // tensor), k % tensor, tensor, dp) for k in range(1, 2 * tensor)]


def sum_plane(part, landed, dp):
    planes = []
    for z in range(dp // 4):
        total = part[z].astype(f32)
        for piece in landed:
            total = total + piece[z].astype(f32)
        planes.append(total.astype(bf16))
    return planes


def send_line(planes, tensor, dp):
    return [swap(planes[z], 4 * z, 0, tensor, dp) for z in range(1, dp // 4)]


def sum_line(plane, landed):
    total = plane.astype(f32)
    for piece in landed:
        total = total + piece.astype(f32)
    return total


def pack_kernel(
    heads_ref, merge_ref, expand_ref, reduce_ref, hb_ref, eb_ref, *refs
):
    small, (first_ref, later_ref) = refs[:-2], refs[-2:]
    _, part, own = heads_ref.shape
    for s in range(3):
        first_ref[:part, s * own : (s + 1) * own] = heads_ref[s]
    lines = [ref[...].astype(f32) for ref in small] + [jnp.zeros((8 - len(small), part), f32)]
    hb = hb_ref[...].astype(f32)
    hb = hb.reshape(hb.shape[0] * hb.shape[1], hb.shape[2])
    eb = eb_ref[...].astype(f32)
    pieces = []
    for piece in (jnp.concatenate(lines, axis=0), eb, hb):
        height, width = piece.shape
        if height < 8:
            piece = jnp.concatenate([piece, jnp.zeros((8 - height, width), f32)], axis=0)
        pieces.append(piece)
    used = sum(piece.shape[1] for piece in pieces)
    pieces.append(jnp.zeros((8, 128 - used), f32))
    first_ref[part:, :128] = jnp.concatenate(pieces, axis=1).astype(bf16)
    first_ref[part:, 128:] = jnp.zeros((8, 3 * own - 128), bf16)
    hidden = expand_ref.shape[1]
    later_ref[:, :hidden] = expand_ref[...]
    later_ref[:, hidden : 2 * hidden] = reduce_ref[...]
    later_ref[:, 2 * hidden :] = merge_ref[...]


def gather_kernel(in_ref, out_ref, own_sem, send_sem, recv_sem):
    d, y = lax.axis_index("dp"), lax.axis_index("tensor")
    z, x, c = lax.div(d, 4), lax.rem(lax.div(d, 2), 2), lax.rem(d, 2)
    far_x, far_y, far_c = 1 - x, 1 - y, 1 - c
    barrier = pltpu.get_barrier_semaphore()

    def index(place):
        pz, px, pc, py = place
        return (pz * 2 + px) * 2 + pc, py

    lines = [lax.rem(z + k, 4) for k in range(1, 4)]
    peers = [(other, x, c, y) for other in lines] + [(z, far_x, c, y), (z, x, c, far_y), (z, x, far_c, y)]
    to_x, to_y, to_c = peers[3:]
    for peer in peers:
        pl.semaphore_signal(barrier, inc=1, device_id=index(peer), device_id_type=pl.DeviceIdType.MESH)
    pl.semaphore_wait(barrier, len(peers))

    sent = []

    def copy(owner, peer, slot, source=None):
        p, q = index(owner)
        return pltpu.make_async_remote_copy(
            src_ref=out_ref.at[q, p] if source is None else source,
            dst_ref=out_ref.at[q, p],
            send_sem=send_sem.at[slot],
            recv_sem=recv_sem.at[p * 2 + q],
            device_id=index(peer),
            device_id_type=pl.DeviceIdType.MESH,
        )

    def send(owner, peer, source=None):
        out = copy(owner, peer, len(sent), source)
        out.start()
        sent.append(out)

    def arrive(owner):
        copy(owner, to_c, 0).wait_recv()

    own = (z, x, c, y)
    for peer in peers:
        send(own, peer, in_ref)
    keep = pltpu.make_async_copy(in_ref, out_ref.at[y, d], own_sem)
    keep.start()
    for other in lines:
        block = (other, x, c, y)
        arrive(block)
        for peer in (to_x, to_y, to_c):
            send(block, peer)
    for level in range(4):
        block = (level, far_x, c, y)
        arrive(block)
        if level % 2 == 0:
            send(block, to_y)
        send(block, to_c)
        block = (level, x, c, far_y)
        arrive(block)
        if level % 2 == 1:
            send(block, to_x)
        send(block, to_c)
    for level in range(4):
        block = (level, far_x, c, far_y)
        arrive(block)
        send(block, to_c)
    for level in range(4):
        for px in range(2):
            for py in range(2):
                arrive((level, px, far_c, py))
    for out in sent:
        out.wait_send()
    keep.wait()


def gather_first(shard, tensor, dp):
    shape = (tensor, dp) + shard.shape
    if (tensor, dp) != (2, 16):
        return lax.all_gather(shard, AXES, axis=0, tiled=True).reshape(shape)
    return call(
        gather_kernel,
        "gather",
        (),
        [pl.BlockSpec(memory_space=pltpu.VMEM)],
        [pl.BlockSpec(memory_space=pl.ANY)],
        [(shape, bf16)],
        (shard,),
        [pltpu.SemaphoreType.DMA, pltpu.SemaphoreType.DMA((31,)), pltpu.SemaphoreType.DMA((32,))],
        collective_id=1,
        has_side_effects=True,
    )[0]


def tail_kernel(dp, tensor, *refs):
    count, depth = dp * tensor, dp // 4
    own_ref, refs = refs[0], refs[1:]
    others, refs = refs[: 2 * tensor - 1], refs[2 * tensor - 1 :]
    one_ref, two_ref, hb_ref, eb_ref, out_ref, sums_ref = refs[:6]
    packed, landed, line, arrived, send_sem, recv_sem, line_send, line_recv = refs[6:]
    d, y = lax.axis_index("dp"), lax.axis_index("tensor")
    me = d * tensor + y
    part = own_ref.shape[1]
    barrier = pltpu.get_barrier_semaphore()

    def place(k):
        other = lax.rem(me + k, count)
        return other, (lax.div(other, tensor), lax.rem(other, tensor))

    def greet(k, carry):
        _, where = place(k)
        pl.semaphore_signal(barrier, inc=1, device_id=where, device_id_type=pl.DeviceIdType.MESH)
        return carry

    lax.fori_loop(1, count, greet, 0)

    def plane(z):
        total = own_ref[z].astype(f32)
        for ref in others:
            total = total + ref[z].astype(f32)
        return total

    for z in range(1, depth):
        line[z - 1] = plane(z).astype(bf16)
    heads = hb_ref.shape[1] // HEAD_DIM
    own_heads, hb_wide = heads // tensor, HEAD_DIM // dp
    eb_tall, eb_wide = eb_ref.shape[0] // tensor, eb_ref.shape[1] // dp
    hb = [
        hb_ref[k : k + 1, h * HEAD_DIM : (h + 1) * HEAD_DIM] for k in range(2) for h in range(heads)
    ]
    hb = jnp.concatenate(hb, axis=0).T
    eb = eb_ref[...].T
    sums = jnp.concatenate([one_ref[...], two_ref[3:4], two_ref[1:3], two_ref[0:1]], axis=0)
    for p in range(dp):
        piece = sums[:, p * part : (p + 1) * part]
        for q in range(tensor):
            packed[p * tensor + q, 0:6, 0:part] = piece
            lane = part
            packed[p * tensor + q, 0:eb_wide, lane : lane + eb_tall] = eb[
                p * eb_wide : (p + 1) * eb_wide, q * eb_tall : (q + 1) * eb_tall
            ]
            for k in range(2):
                lane = part + eb_tall + k * own_heads
                packed[p * tensor + q, 0:hb_wide, lane : lane + own_heads] = hb[
                    p * hb_wide : (p + 1) * hb_wide,
                    k * heads + q * own_heads : k * heads + (q + 1) * own_heads,
                ]
    pl.semaphore_wait(barrier, count - 1)

    copies = []
    for z in range(1, depth):
        far = d
        for bit in range(depth.bit_length() - 1):
            if (z >> bit) & 1:
                unit = 4 << bit
                far = far + unit - 2 * unit * lax.rem(lax.div(far, unit), 2)
        copies.append(pltpu.make_async_remote_copy(
            src_ref=line.at[z - 1],
            dst_ref=arrived.at[z - 1],
            send_sem=line_send.at[z - 1],
            recv_sem=line_recv.at[z - 1],
            device_id=(far, y),
            device_id_type=pl.DeviceIdType.MESH,
        ))

    def copy(k):
        other, where = place(k)
        return pltpu.make_async_remote_copy(
            src_ref=packed.at[other],
            dst_ref=landed.at[k],
            send_sem=send_sem.at[k],
            recv_sem=recv_sem.at[k],
            device_id=where,
            device_id_type=pl.DeviceIdType.MESH,
        )

    def start(k, carry):
        copy(k).start()
        return carry

    lax.fori_loop(1, count, start, 0)
    for item in copies:
        item.start()
    total = plane(0)

    def finish(k, sums):
        copy(k).wait()
        return sums + landed[k]

    sums = lax.fori_loop(1, count, finish, packed[me])
    sums_ref[...] = sums
    for item, z in zip(copies, range(1, depth)):
        item.wait()
        total = total + arrived[z - 1].astype(f32)
    own = out_ref.shape[2]
    for s in range(3):
        out_ref[s] = total[:, s * own : (s + 1) * own]


def tail(part_own, landed, sums, hb, eb, tensor, dp):
    depth, part, lanes = part_own.shape
    count = tensor * dp
    arrays = [part_own, *landed, *sums, hb, eb]
    vmem = pl.BlockSpec(memory_space=pltpu.VMEM)
    out = [((3, part, lanes // 3), f32), ((8, 128), f32)]
    return call(
        functools.partial(tail_kernel, dp, tensor),
        "tail",
        (),
        [vmem] * len(arrays),
        [vmem] * len(out),
        out,
        arrays,
        [
            pltpu.VMEM((count, 8, 128), f32), pltpu.VMEM((count, 8, 128), f32),
            pltpu.VMEM((depth - 1, part, lanes), bf16), pltpu.VMEM((depth - 1, part, lanes), bf16),
            pltpu.SemaphoreType.DMA((count,)), pltpu.SemaphoreType.DMA((count,)),
            pltpu.SemaphoreType.DMA((depth - 1,)), pltpu.SemaphoreType.DMA((depth - 1,)),
        ],
        collective_id=0,
        has_side_effects=True,
    )


def finish_kernel(sums_ref, heads_ref, out_ref, hb_ref, eb_ref, *vectors):
    out_ref[...] = heads_ref[...]
    part = vectors[0].shape[1]
    for r, ref in enumerate(vectors):
        ref[...] = sums_ref[r : r + 1, :part]
    wide, tall = eb_ref.shape
    eb_ref[...] = sums_ref[:wide, part : part + tall]
    wide, count = hb_ref.shape[1:]
    for k in range(2):
        lane = part + tall + k * count
        hb_ref[k] = sums_ref[:wide, lane : lane + count]


def shards(
    tensor,
    dp,
    activations,
    first_gain,
    first_shift,
    heads_weight,
    heads_bias,
    merge_weight,
    merge_bias,
    second_gain,
    second_shift,
    expand_weight,
    expand_bias,
    reduce_weight,
    reduce_bias,
    output_grad,
    real_images,
):
    rows, deep = activations.shape
    images = rows // SEQ
    part = deep // dp
    own = heads_weight.shape[2]
    hidden_own = expand_weight.shape[1]
    hidden = hidden_own * tensor
    heads = deep // HEAD_DIM
    least = (images - 1) * STRIDE + WINDOW
    blocks = -(-least // 512)
    block = -(-least // blocks // 16) * 16
    total_rows = block * blocks

    def gather(shard):
        out = lax.all_gather(shard, AXES, axis=0, tiled=True)
        return out.reshape(tensor, dp, *shard.shape)

    small = [first_gain, first_shift, merge_bias, second_gain, second_shift, reduce_bias]
    arrays = [
        heads_weight, merge_weight.T, expand_weight, reduce_weight.T,
        heads_bias.transpose(0, 2, 1), expand_bias.T,
    ] + [v.reshape(1, part) for v in small]
    vmem = pl.BlockSpec(memory_space=pltpu.VMEM)
    first, later = call(
        pack_kernel, "pack", (), [vmem] * len(arrays), [vmem] * 2,
        [((part + 8, 3 * own), bf16), ((part, 2 * hidden_own + own), bf16)], arrays,
    )
    wide = gather(later)
    wide_heads = gather_first(first, tensor, dp)

    hbs, ebs = heads_bias.shape, expand_bias.shape
    small = wide_heads[:, :, part:, :128].astype(f32)
    vectors = small[0, :, :6, :part].transpose(1, 0, 2).reshape(6, deep)
    eb = small[:, :, : ebs[1], part : part + ebs[0]].transpose(0, 3, 1, 2).reshape(1, hidden)
    hb = small[:, :, : 2 * hbs[2], part + ebs[0] : part + ebs[0] + hbs[1]]
    hb = hb.reshape(tensor, dp, 2, hbs[2], hbs[1]).transpose(2, 0, 4, 1, 3).reshape(2, deep)
    live = jnp.clip(real_images - lax.axis_index("tensor") * images, 0, images) * SEQ

    def by_rows(width):
        return pl.BlockSpec((block, width), lambda i, *_: (i, 0))

    def column(index, width):
        shape = (tensor, dp, part, width)
        return pl.BlockSpec(shape, lambda *_: (0, 0, 0, index), pipeline_mode=pl.Buffered(1))

    vec = full((6, deep))
    triple_spec = pl.BlockSpec((3, block, deep), lambda i: (0, i, 0))
    normed_one, triple = call(
        functools.partial(qkv_kernel, part, rows),
        "qkv",
        (blocks,),
        [by_rows(deep), vec, full((2, deep)), full(wide_heads.shape)],
        [by_rows(deep), triple_spec],
        [((total_rows, deep), bf16), ((3, total_rows, deep), bf16)],
        (activations, vectors, hb, wide_heads),
        flops=total_rows * deep * deep * 3,
    )

    group = 4
    groups = heads // group
    panel = group * HEAD_DIM
    head_spec = pl.BlockSpec((3, total_rows, panel), lambda g, i: (0, 0, g))
    ctx_spec = pl.BlockSpec((total_rows, panel), lambda g, i: (0, g))
    stat_spec = pl.BlockSpec((1, group, WINDOW), lambda g, i: (g * images + i, 0, 0))
    attend_flops = images * heads * WINDOW * 768 * 256 * 2
    context, stat = call(
        attend_kernel,
        "attend",
        (groups, images),
        [head_spec],
        [ctx_spec, stat_spec],
        [((total_rows, deep), bf16), ((images * groups, group, WINDOW), f32)],
        (triple,),
        flops=attend_flops,
    )

    merge_width, expand_width = merge_weight.shape[0], hidden_own
    expand_spec = column(0, expand_width)
    reduce_spec = column(1, expand_width)
    merge_spec = column(2 * expand_width // merge_width, merge_width)
    resid, normed_two = call(
        functools.partial(merge_kernel, rows),
        "merge",
        (blocks,),
        [by_rows(deep), by_rows(deep), vec, merge_spec],
        [by_rows(deep), by_rows(deep)],
        [((total_rows, deep), f32), ((total_rows, deep), bf16)],
        (context, activations, vectors, wide),
        flops=total_rows * deep * deep,
    )

    chunk = min(1024, hidden_own)
    output, active, slope, grad = call(
        functools.partial(mlp_kernel, chunk),
        "mlp",
        (blocks,),
        [
            by_rows(deep), by_rows(deep), full((1, hidden)), vec, expand_spec, reduce_spec, by_rows(deep),
        ],
        [by_rows(deep), by_rows(hidden), by_rows(hidden), by_rows(deep)],
        [
            ((rows, deep), bf16), ((total_rows, hidden), bf16), ((total_rows, hidden), bf16),
            ((total_rows, deep), bf16),
        ],
        (live, normed_two, resid, eb, vectors, wide, wide, output_grad),
        prefetch=1,
        flops=total_rows * deep * hidden * 2,
    )

    def scatter(grads):
        grads = grads.reshape(tensor * dp * part, grads.shape[3])
        return lax.psum_scatter(grads, AXES, scatter_dimension=0, tiled=True)

    grad_reduce = weight_grads("reduce_grad", [(grad, active)], tensor, dp, 512)
    grad, slope, grad_reduce = lax.optimization_barrier((grad, slope, grad_reduce))
    grad_reduce = scatter(grad_reduce)

    back_chunk = min(512, hidden_own)
    pre_grad, resid_low, grad_context, sums_two, esum = call(
        functools.partial(mlp_back_kernel, back_chunk),
        "mlp_back",
        (blocks,),
        [
            by_rows(deep), by_rows(hidden), by_rows(deep), vec,
            expand_spec, reduce_spec, merge_spec,
        ],
        [
            by_rows(hidden), by_rows(deep), by_rows(deep),
            pl.BlockSpec((4, deep), lambda i: (0, 0)), pl.BlockSpec((hidden // 128, 128), lambda i: (0, 0)),
        ],
        [
            ((total_rows, hidden), bf16), ((total_rows, deep), bf16), ((total_rows, deep), bf16),
            ((4, deep), f32), ((hidden // 128, 128), f32),
        ],
        (grad, slope, resid, vectors, wide, wide, wide),
    )
    me = jnp.stack([lax.axis_index("dp"), lax.axis_index("tensor")]).astype(jnp.int32)
    keep, send = slot_grads(
        "middle_grad", [(normed_two, pre_grad[None]), (resid_low, context[None])], tensor, dp, me, 512
    )
    grad_context, keep, send = lax.optimization_barrier((grad_context, keep, send))
    other = swap(send, 1, 0, tensor, dp)

    def attend_back(first, before, grad_context):
        count = groups // 2
        return call(
            attend_back_kernel,
            "attend_back",
            (count, images),
            [
                pl.BlockSpec((3, total_rows, panel), lambda g, i: (0, 0, first + g)),
                pl.BlockSpec((1, group, WINDOW), lambda g, i: ((first + g) * images + i, 0, 0)),
                pl.BlockSpec((total_rows, panel), lambda g, i: (0, first + g)),
            ] + [pl.BlockSpec(memory_space=pl.ANY)] * len(before),
            [pl.BlockSpec((3, total_rows, panel), lambda g, i: (0, 0, first + g))],
            [((3, total_rows, deep), bf16)],
            (triple, stat, grad_context) + before,
            aliases={3: 0} if before else {},
        )[0]

    grad_triple = attend_back(0, (), grad_context)
    keep, other, grad_triple = lax.optimization_barrier((keep, other, grad_triple))
    parts = sum_cores(keep, other, tensor, dp)
    *parts, grad_context = lax.optimization_barrier((*parts, grad_context))
    landed = send_plane(parts, tensor, dp)
    grad_triple = attend_back(groups // 2, (grad_triple,), grad_context)
    *landed, part_own, grad_triple = lax.optimization_barrier((*landed, parts[0], grad_triple))
    planes = sum_plane(part_own, landed, dp)
    *planes, grad_triple = lax.optimization_barrier((*planes, grad_triple))
    landed = send_line(planes, tensor, dp)
    keep, send = slot_grads("heads_grad", [(normed_one, grad_triple)], tensor, dp, me, 512)
    resid_low, keep, send, *landed = lax.optimization_barrier((resid_low, keep, send, *landed))
    grad_middle = sum_line(planes[0], landed)

    other = swap(send, 1, 0, tensor, dp)
    parts = sum_cores(keep, other, tensor, dp)
    *parts, resid_low = lax.optimization_barrier((*parts, resid_low))
    landed = send_plane(parts, tensor, dp)
    input_grad, sums_one, bsum = call(
        functools.partial(qkv_back_kernel, part, rows),
        "qkv_back",
        (blocks,),
        [by_rows(deep), by_rows(deep), vec, triple_spec, full(wide_heads.shape)],
        [by_rows(deep), pl.BlockSpec((2, deep), lambda i: (0, 0)), pl.BlockSpec((2, deep), lambda i: (0, 0))],
        [((rows, deep), bf16), ((2, deep), f32), ((2, deep), f32)],
        (activations, resid_low, vectors, grad_triple, wide_heads),
        flops=total_rows * deep * deep * 3,
    )

    heads_sum, sums = tail(parts[0], landed, (sums_one, sums_two), bsum, esum, tensor, dp)
    grad_heads, hb_grad, eb_grad, *vector = call(
        finish_kernel, "finish", (), [vmem] * 2, [vmem] * 9,
        [(heads_sum.shape, f32), ((2, hbs[2], hbs[1]), f32), (ebs[::-1], f32)] + [((1, part), f32)] * 6,
        (sums, heads_sum),
    )
    vector = [v.reshape(part) for v in vector]

    return (
        output,
        input_grad,
        vector[0],
        vector[1],
        grad_heads,
        hb_grad.transpose(0, 2, 1),
        grad_middle[:, expand_width:].T,
        vector[2],
        vector[3],
        vector[4],
        grad_middle[:, :expand_width],
        eb_grad.T,
        grad_reduce.astype(f32).T,
        vector[5],
    )


def solution(mesh):
    rows = P(("dp", "tensor"), None)
    specs = (
        P("dp"),
        P("dp"),
        P(None, "dp", "tensor"),
        P(None, "tensor", "dp"),
        P("tensor", "dp"),
        P("dp"),
        P("dp"),
        P("dp"),
        P("dp", "tensor"),
        P("tensor", "dp"),
        P("tensor", "dp"),
        P("dp"),
    )
    return jax.shard_map(
        functools.partial(shards, mesh.shape["tensor"], mesh.shape["dp"]),
        mesh=mesh,
        in_specs=(rows,) + specs + (rows, P("dp")),
        out_specs=(rows, rows) + specs,
        check_vma=False,
    )
```

```python
import functools
import math

import jax
import jax.numpy as jnp
from jax import lax
from jax.experimental import pallas as pl
from jax.experimental.pallas import tpu as pltpu
from jax.sharding import PartitionSpec as P

HEAD_DIM = 64
SEQ = 577
STRIDE = 576
WINDOW = 592
EPSILON = 1e-06
LOG_SCALE = 0.125
bf16 = jnp.bfloat16
f32 = jnp.float32
NN = (((1,), (0,)), ((), ()))
NT = (((1,), (1,)), ((), ()))
TN = (((0,), (0,)), ((), ()))
MIB = 2**20
AXES = ("tensor", "dp")


def matmul(left, right, dims=NN):
    return lax.dot_general(left, right, dims, preferred_element_type=f32)


def norm_parts(values):
    center = values - jnp.mean(values, axis=-1, keepdims=True)
    second = jnp.mean(center * center, axis=-1, keepdims=True)
    inv = lax.rsqrt(second + EPSILON)
    return center * inv, inv


def gelu_and_slope(pre):
    phi = 0.5 + 0.5 * lax.erf(pre * 0.7071067811865476)
    bell = jnp.exp(pre * pre * -0.5)
    return pre * phi, phi + pre * (bell * 0.3989422804014327)


def full(shape):
    return pl.BlockSpec(shape, lambda *_: (0,) * len(shape), pipeline_mode=pl.Buffered(1))


def call(kernel, name, grid, in_specs, out_specs, out_shape, args, scratch=(), flops=0, prefetch=0, vmem=40, **params):
    moved = 0
    if flops:
        moved = sum(a.size * a.dtype.itemsize for a in args)
        moved += sum(math.prod(shape) * jnp.dtype(dtype).itemsize for shape, dtype in out_shape)
    return pl.pallas_call(
        kernel,
        grid_spec=pltpu.PrefetchScalarGridSpec(
            num_scalar_prefetch=prefetch,
            grid=grid,
            in_specs=in_specs,
            out_specs=out_specs,
            scratch_shapes=list(scratch),
        ),
        out_shape=[jax.ShapeDtypeStruct(shape, dtype) for shape, dtype in out_shape],
        compiler_params=pltpu.CompilerParams(vmem_limit_bytes=vmem * MIB, **params),
        cost_estimate=pl.CostEstimate(flops=2 * flops, bytes_accessed=moved, transcendentals=0),
        name=name,
    )(*args)


def before(ref, count):
    height = ref.shape[0]
    rows = pl.program_id(0) * height + lax.broadcasted_iota(jnp.int32, (height, 1), 0)
    return jnp.where(rows < count, ref[...].astype(f32), 0.0)


def qkv_kernel(part, count, x_ref, vec_ref, bias_ref, w_ref, normed_ref, triple_ref):
    hat, _ = norm_parts(before(x_ref, count))
    normed = (hat * vec_ref[0:1] + vec_ref[1:2]).astype(bf16)
    normed_ref[...] = normed
    tensor, dp = w_ref.shape[:2]
    width = w_ref.shape[3] // 4
    for s in range(3):
        for t in range(tensor):
            cols = slice(t * width, (t + 1) * width)
            w = w_ref[t, :, :part, s * width : (s + 1) * width].reshape(dp * part, width)
            out = matmul(normed, w)
            if s != 1:
                out = out + bias_ref[s // 2 : s // 2 + 1, cols]
            triple_ref[s, :, cols] = out.astype(bf16)


def window(image):
    start = pl.multiple_of(image * STRIDE, 16)
    return pl.ds(start, WINDOW)


def keep_before(image, ref, index, value):
    edge = pl.ds(pl.multiple_of(image * STRIDE, 16), 16)
    rest = pl.ds(pl.multiple_of(image * STRIDE + 16, 16), WINDOW - 16)
    rows = lax.broadcasted_iota(jnp.int32, (16, 1), 0)
    head = jnp.where(rows < image, ref[(*index[:-1], edge, index[-1])].astype(f32), value[:16])
    ref[(*index[:-1], edge, index[-1])] = head.astype(ref.dtype)
    ref[(*index[:-1], rest, index[-1])] = value[16:].astype(ref.dtype)


def attend_kernel(triple_ref, context_ref, stat_ref):
    image = pl.program_id(1)
    lanes = lax.broadcasted_iota(jnp.int32, (1, WINDOW), 1)
    mask = jnp.where((lanes >= image) & (lanes < image + SEQ), 0.0, -1e30)
    own = window(image)
    stats = []
    for h in range(triple_ref.shape[2] // HEAD_DIM):
        cols = slice(HEAD_DIM * h, HEAD_DIM * (h + 1))
        query = triple_ref[0, own, cols] * bf16(LOG_SCALE)
        scores = matmul(query, triple_ref[1, own, cols], NT) + mask
        top = jnp.max(scores, axis=1, keepdims=True)
        expo = jnp.exp(scores - top)
        total = jnp.sum(expo, axis=1, keepdims=True)
        context = matmul(expo.astype(bf16), triple_ref[2, own, cols]) * (1.0 / total)
        keep_before(image, context_ref, (cols,), context)
        stats.append(top + jnp.log(total))
    stat_ref[0] = jnp.concatenate(stats, axis=1).T


def attend_back_kernel(triple_ref, stat_ref, grad_ref, out_ref):
    image = pl.program_id(1)
    rows = lax.broadcasted_iota(jnp.int32, (WINDOW, 1), 0)
    mask = jnp.where((rows >= image) & (rows < image + SEQ), 0.0, -1e30)
    lanes = lax.broadcasted_iota(jnp.int32, (1, WINDOW), 1)
    real = (lanes >= image) & (lanes < image + SEQ)
    own = window(image)
    for h in range(triple_ref.shape[2] // HEAD_DIM):
        cols = slice(HEAD_DIM * h, HEAD_DIM * (h + 1))
        query = triple_ref[0, own, cols]
        keys = triple_ref[1, own, cols]
        grad = grad_ref[own, cols]
        scores = matmul(keys, query * bf16(LOG_SCALE), NT) + mask
        probs = jnp.exp(scores - jnp.where(real, stat_ref[0, h : h + 1, :], 1e30))
        grad_probs = matmul(triple_ref[2, own, cols], grad, NT)
        inner = jnp.sum(probs * grad_probs, axis=0, keepdims=True)
        grad_scores = (probs * (grad_probs - inner)).astype(bf16)
        blank = jnp.zeros_like(grad)
        left = jnp.concatenate([probs.astype(bf16), grad_scores], axis=1)
        right = jnp.concatenate(
            [jnp.concatenate([grad, blank], axis=1), jnp.concatenate([blank, query], axis=1)], axis=0
        )
        pair = matmul(left, right)
        keep_before(image, out_ref, (2, cols), pair[:, :HEAD_DIM])
        keep_before(image, out_ref, (1, cols), pair[:, HEAD_DIM:] * LOG_SCALE)
        keep_before(image, out_ref, (0, cols), (matmul(keys.T, grad_scores) * LOG_SCALE).T)


def merge_kernel(part, count, ctx_ref, x_ref, vec_ref, w_ref, resid_ref, normed_ref):
    tensor, dp = w_ref.shape[:2]
    width = w_ref.shape[3] // 4
    total = before(x_ref, count) + vec_ref[2:3]
    for t in range(tensor):
        w = w_ref[t, :, :part, 3 * width :].reshape(dp * part, width)
        total = total + matmul(ctx_ref[:, t * width : (t + 1) * width], w, NT)
    resid_ref[...] = total
    hat, _ = norm_parts(total)
    normed_ref[...] = (hat * vec_ref[3:4] + vec_ref[4:5]).astype(bf16)


def mlp_kernel(
    chunk, live_ref, normed_ref, resid_ref, ebias_ref, vec_ref, w_ref, given_ref,
    out_ref, act_ref, slope_ref, grad_ref,
):
    grad_ref[...] = before(given_ref, live_ref[0]).astype(bf16)
    tensor, dp, rows, width = w_ref.shape
    width = width // 2
    normed = normed_ref[...]
    total = resid_ref[...] + vec_ref[5:6]
    for t in range(tensor):
        for c in range(width // chunk):
            local = slice(c * chunk, (c + 1) * chunk)
            other = slice(width + c * chunk, width + (c + 1) * chunk)
            cols = slice(t * width + c * chunk, t * width + (c + 1) * chunk)
            e = w_ref[t, :, :, local].reshape(dp * rows, chunk)
            active, slope = gelu_and_slope(matmul(normed, e) + ebias_ref[:, cols])
            active = active.astype(bf16)
            act_ref[:, cols] = active
            slope_ref[:, cols] = slope.astype(bf16)
            r = w_ref[t, :, :, other].reshape(dp * rows, chunk)
            total = total + matmul(active, r, NT)
    out_ref[...] = total.astype(bf16)


def accumulate(first, ref, value):
    @pl.when(first)
    def _():
        ref[...] = value

    @pl.when(jnp.logical_not(first))
    def _():
        ref[...] += value


def norm_back(values, gain, grad):
    hat, inv = norm_parts(values)
    scaled = grad * gain
    back = (
        scaled
        - jnp.mean(scaled, axis=-1, keepdims=True)
        - hat * jnp.mean(scaled * hat, axis=-1, keepdims=True)
    ) * inv
    return back, jnp.sum(grad * hat, axis=0, keepdims=True), jnp.sum(grad, axis=0, keepdims=True)


def mlp_back_kernel(
    part, chunk, grad_ref, slope_ref, resid_ref, vec_ref, w_ref, m_ref,
    pre_ref, low_ref, ctx_ref, sums_ref, esum_ref,
):
    tensor, dp, rows, width = w_ref.shape
    width = width // 2
    first = pl.program_id(0) == 0
    grad = grad_ref[...]
    total = jnp.zeros(grad.shape, f32)
    parts = []
    for t in range(tensor):
        for c in range(width // chunk):
            local = slice(c * chunk, (c + 1) * chunk)
            other = slice(width + c * chunk, width + (c + 1) * chunk)
            cols = slice(t * width + c * chunk, t * width + (c + 1) * chunk)
            r = w_ref[t, :, :, other].reshape(dp * rows, chunk)
            pre = (matmul(grad, r) * slope_ref[:, cols].astype(f32)).astype(bf16)
            pre_ref[:, cols] = pre
            parts.append(jnp.sum(pre.astype(f32), axis=0, keepdims=True))
            e = w_ref[t, :, :, local].reshape(dp * rows, chunk)
            total = total + matmul(pre, e, NT)
    sums = 0
    half = grad.shape[0] // 2
    for rows_half in (slice(0, half), slice(half, 2 * half)):
        own = grad_ref[rows_half].astype(f32)
        back, gain_sum, shift_sum = norm_back(resid_ref[rows_half], vec_ref[3:4], total[rows_half])
        resid_grad = own + back
        low_ref[rows_half] = resid_grad.astype(bf16)
        lines = [jnp.sum(own, axis=0, keepdims=True), gain_sum, shift_sum]
        sums = sums + jnp.concatenate(lines + [jnp.sum(resid_grad, axis=0, keepdims=True)], axis=0)
    low = low_ref[...]
    wide = m_ref.shape[3]
    for t in range(tensor):
        m = m_ref[t, :, :part].reshape(dp * part, wide)
        ctx_ref[:, t * wide : (t + 1) * wide] = matmul(low, m).astype(bf16)
    accumulate(first, sums_ref, sums)
    parts = jnp.concatenate(parts, axis=1)
    lines = [parts[:, k * 128 : (k + 1) * 128] for k in range(esum_ref.shape[0])]
    accumulate(first, esum_ref, jnp.concatenate(lines, axis=0))


def qkv_back_kernel(part, count, x_ref, low_ref, vec_ref, grad_ref, w_ref, out_ref, sums_ref, bsum_ref):
    tensor, dp = w_ref.shape[:2]
    width = w_ref.shape[3] // 4
    first = pl.program_id(0) == 0
    total = jnp.zeros(x_ref.shape, f32)
    for s in range(3):
        for t in range(tensor):
            w = w_ref[t, :, :part, s * width : (s + 1) * width].reshape(dp * part, width)
            total = total + matmul(grad_ref[s, :, t * width : (t + 1) * width], w, NT)
    back, gain_sum, shift_sum = norm_back(before(x_ref, count), vec_ref[0:1], total)
    out_ref[...] = (low_ref[...].astype(f32) + back).astype(bf16)
    accumulate(first, sums_ref, jnp.concatenate([gain_sum, shift_sum], axis=0))
    bias = [jnp.sum(grad_ref[s].astype(f32), axis=0, keepdims=True) for s in (0, 2)]
    accumulate(first, bsum_ref, jnp.concatenate(bias, axis=0))


def weight_grad_kernel(starts, *refs):
    count = len(starts) - 1
    lefts, rights, out_ref = refs[:count], refs[count : 2 * count], refs[-1]
    step = pl.program_id(0)
    for j in range(count):
        @pl.when((step >= starts[j]) & (step < starts[j + 1]))
        def _():
            out = matmul(lefts[j][...], rights[j][0], TN)
            out_ref[...] = out.astype(bf16).reshape(out_ref.shape)


def weight_grads(name, pairs, tensor, dp, block):
    rows, deep = pairs[0][0].shape
    locals_ = [right.shape[1] // tensor for _, right in pairs]
    block = min([block] + locals_)
    pers = [local // block for local in locals_]
    starts = [0]
    for per in pers:
        starts.append(starts[-1] + tensor * per)

    def right_map(j, i):
        i = jnp.clip(i - starts[j], 0, tensor * pers[j] - 1)
        return (0, 0, i)

    def out_map(i):
        where, column, t = 0, 0, 0
        for j, per in enumerate(pers):
            inside = (i >= starts[j]) & (i < starts[j + 1])
            t = t + jnp.where(inside, (i - starts[j]) // per, 0)
            column = column + jnp.where(inside, where + (i - starts[j]) % per, 0)
            where += per
        return (t, 0, 0, column)

    return call(
        functools.partial(weight_grad_kernel, starts),
        name,
        (starts[-1],),
        [full((rows, deep))] * len(pairs)
        + [pl.BlockSpec((1, rows, block), functools.partial(right_map, j)) for j in range(len(pairs))],
        [pl.BlockSpec((1, dp, deep // dp, block), out_map)],
        [((tensor, dp, deep // dp, sum(locals_)), bf16)],
        [left for left, _ in pairs] + [right[None] for _, right in pairs],
        flops=rows * deep * tensor * sum(locals_),
    )[0]


def flip(value, mask):
    unit = 1
    while unit <= mask:
        if mask & unit:
            value = value + unit - 2 * unit * lax.rem(lax.div(value, unit), 2)
        unit *= 2
    return value


def differ(left, right, size):
    total, unit = 0, 1
    while unit < size:
        p, q = lax.rem(lax.div(left, unit), 2), lax.rem(lax.div(right, unit), 2)
        total = total + unit * (p + q - 2 * p * q)
        unit *= 2
    return total


def slot_grad_kernel(tensor, dp, starts, *refs):
    count, steps, depth = len(starts) - 1, starts[-1], dp // 4
    lefts, rights, outs = refs[:count], refs[count : 2 * count], refs[2 * count : 2 * count + 2 * tensor]
    total, keep, send, landed, send_sem, recv_sem = refs[2 * count + 2 * tensor :]
    step, t = pl.program_id(0), pl.program_id(1)
    d, y = lax.axis_index("dp"), lax.axis_index("tensor")
    part, block = total.shape[0] // dp, total.shape[1]
    column = differ(t, y, tensor)
    slots = pl.ds(column * (2 * depth), 2 * depth)

    def copy(step):
        cols = pl.ds(pl.multiple_of(step * block, block), block)
        return pltpu.make_async_remote_copy(
            src_ref=send.at[slots, :, cols],
            dst_ref=landed.at[slots, :, cols],
            send_sem=send_sem.at[step * tensor + t],
            recv_sem=recv_sem.at[step * tensor + t],
            device_id=(flip(d, 1), y),
            device_id_type=pl.DeviceIdType.MESH,
        )

    @pl.when((step == 0) & (t == 0))
    def _():
        barrier = pltpu.get_barrier_semaphore()
        pl.semaphore_signal(
            barrier, inc=1, device_id=(flip(d, 1), y), device_id_type=pl.DeviceIdType.MESH
        )
        pl.semaphore_wait(barrier, 1)

    for j in range(count):
        @pl.when((step >= starts[j]) & (step < starts[j + 1]))
        def _():
            total[...] = matmul(lefts[j][...], rights[j][0], TN)

    @pl.when(step < steps)
    def _():
        cols = pl.ds(pl.multiple_of(step * block, block), block)
        for r in range(dp):
            owner = pl.multiple_of(flip(d, r) * part, part)
            half = send if r & 1 else keep
            slot = column * (2 * depth) + ((r >> 1) & 1) * depth + (r >> 2)
            half[slot, :, cols] = total[pl.ds(owner, part), :].astype(bf16)
        copy(step).start()

    @pl.when(step > 0)
    def _():
        copy(step - 1).wait()
        cols = pl.ds(pl.multiple_of((step - 1) * block, block), block)
        for k in range(2 * tensor):
            @pl.when(column == k // 2)
            def _():
                own = pl.ds(k * depth, depth)
                both = keep[own, :, cols].astype(f32) + landed[own, :, cols].astype(f32)
                outs[k][...] = both.astype(bf16)


def slot_grads(name, pairs, tensor, dp, block, collective_id):
    rows, deep = pairs[0][0].shape
    part, depth = deep // dp, dp // 4
    block = min([block] + [right.shape[2] // tensor for _, right in pairs])
    pers = [right.shape[2] // tensor // block for _, right in pairs]
    starts = [0]
    for (_, right), per in zip(pairs, pers):
        starts.append(starts[-1] + right.shape[0] * per)
    wide = starts[-1] * block
    half = tensor * dp // 2

    def right_map(j, i, t):
        t = jnp.where(i < starts[j], 0, jnp.where(i >= starts[j + 1], tensor - 1, t))
        i = jnp.clip(i - starts[j], 0, starts[j + 1] - starts[j] - 1)
        return (i // pers[j], 0, t * pers[j] + i % pers[j])

    spec = pl.BlockSpec((depth, part, block), lambda i, t: (0, 0, jnp.maximum(i - 1, 0)))
    return call(
        functools.partial(slot_grad_kernel, tensor, dp, starts),
        name,
        (starts[-1] + 1, tensor),
        [full((rows, deep))] * len(pairs)
        + [pl.BlockSpec((1, rows, block), functools.partial(right_map, j)) for j in range(len(pairs))],
        [spec] * (2 * tensor),
        [((depth, part, wide), bf16)] * (2 * tensor),
        [left for left, _ in pairs] + [right for _, right in pairs],
        [pltpu.VMEM((deep, block), f32)]
        + [pltpu.VMEM((half, part, wide), bf16)] * 3
        + [pltpu.SemaphoreType.DMA((starts[-1] * tensor,))] * 2,
        vmem=56,
        collective_id=collective_id,
        has_side_effects=True,
    )


def swap(values, d, t, tensor, dp):
    moves = []
    for p in range(dp):
        for q in range(tensor):
            moves.append((p * tensor + q, (p ^ d) * tensor + (q ^ t)))
    return lax.ppermute(values, ("dp", "tensor"), moves)


def send_plane(parts, tensor, dp):
    return [swap(parts[k], 2 * (k % 2), k // 2, tensor, dp) for k in range(1, 2 * tensor)]


def sum_plane(part, landed, dp):
    planes = []
    for z in range(dp // 4):
        total = part[z].astype(f32)
        for piece in landed:
            total = total + piece[z].astype(f32)
        planes.append(total.astype(bf16))
    return planes


def send_line(planes, tensor, dp):
    return [swap(planes[z], 4 * z, 0, tensor, dp) for z in range(1, dp // 4)]


def sum_line(plane, landed):
    total = plane.astype(f32)
    for piece in landed:
        total = total + piece.astype(f32)
    return total


def pack_kernel(
    heads_ref, merge_ref, expand_ref, reduce_ref, hb_ref, eb_ref, *refs
):
    small, (first_ref, later_ref) = refs[:-2], refs[-2:]
    _, part, own = heads_ref.shape
    for s in range(3):
        first_ref[:part, s * own : (s + 1) * own] = heads_ref[s]
    lines = [ref[...].astype(f32) for ref in small] + [jnp.zeros((8 - len(small), part), f32)]
    hb = hb_ref[...].astype(f32)
    hb = hb.reshape(hb.shape[0] * hb.shape[1], hb.shape[2])
    eb = eb_ref[...].astype(f32)
    pieces = []
    for piece in (jnp.concatenate(lines, axis=0), eb, hb):
        height, width = piece.shape
        if height < 8:
            piece = jnp.concatenate([piece, jnp.zeros((8 - height, width), f32)], axis=0)
        pieces.append(piece)
    used = sum(piece.shape[1] for piece in pieces)
    pieces.append(jnp.zeros((8, 128 - used), f32))
    first_ref[part:, :128] = jnp.concatenate(pieces, axis=1).astype(bf16)
    first_ref[:part, 3 * own :] = merge_ref[...]
    first_ref[part:, 128:] = jnp.zeros((8, 4 * own - 128), bf16)
    hidden = expand_ref.shape[1]
    later_ref[:, :hidden] = expand_ref[...]
    later_ref[:, hidden:] = reduce_ref[...]


def gather_kernel(in_ref, out_ref, own_sem, send_sem, recv_sem):
    d, y = lax.axis_index("dp"), lax.axis_index("tensor")
    z, x, c = lax.div(d, 4), lax.rem(lax.div(d, 2), 2), lax.rem(d, 2)
    far_x, far_y, far_c = 1 - x, 1 - y, 1 - c
    barrier = pltpu.get_barrier_semaphore()

    def index(place):
        pz, px, pc, py = place
        return (pz * 2 + px) * 2 + pc, py

    lower, upper = (z - 1, x, c, y), (z + 1, x, c, y)
    to_x, to_y, to_c = (z, far_x, c, y), (z, x, c, far_y), (z, x, far_c, y)

    def greet(peer):
        pl.semaphore_signal(barrier, inc=1, device_id=index(peer), device_id_type=pl.DeviceIdType.MESH)

    for peer in (to_x, to_y, to_c):
        greet(peer)
    pl.when(z > 0)(lambda: greet(lower))
    pl.when(z < 3)(lambda: greet(upper))
    pl.semaphore_wait(barrier, 4 + lax.rem(lax.div(z + 1, 2), 2))

    sent = []

    def copy(owner, peer, slot, source=None):
        p, q = index(owner)
        return pltpu.make_async_remote_copy(
            src_ref=out_ref.at[q, p] if source is None else source,
            dst_ref=out_ref.at[q, p],
            send_sem=send_sem.at[slot],
            recv_sem=recv_sem.at[p * 2 + q],
            device_id=index(peer),
            device_id_type=pl.DeviceIdType.MESH,
        )

    def send(owner, peer, there, source=None):
        slot = len(sent)
        sent.append((owner, peer, slot, there))

        @pl.when(there)
        def _():
            copy(owner, peer, slot, source).start()

    def arrive(owner, there):
        @pl.when(there)
        def _():
            copy(owner, to_c, 0).wait_recv()

    own = (z, x, c, y)
    keep = pltpu.make_async_copy(in_ref, out_ref.at[y, d], own_sem)
    send(own, upper, z < 3, in_ref)
    send(own, lower, z > 0, in_ref)
    for peer in (to_x, to_y, to_c):
        send(own, peer, z >= 0, in_ref)
    keep.start()
    for far in range(1, 4):
        for sign, after, onward in ((-1, upper, z < 3), (1, lower, z > 0)):
            level = z + sign * far
            there = (level >= 0) & (level <= 3)
            block = (level, x, c, y)
            arrive(block, there)
            send(block, after, there & onward)
            for peer in (to_x, to_y, to_c):
                send(block, peer, there)
    for far in range(4):
        for sign in (-1, 1) if far else (1,):
            level = z + sign * far
            there = (level >= 0) & (level <= 3)
            odd = lax.rem(level + 4, 2)
            block = (level, far_x, c, y)
            arrive(block, there)
            send(block, to_y, there & (odd == 0))
            send(block, to_c, there)
            block = (level, x, c, far_y)
            arrive(block, there)
            send(block, to_x, there & (odd == 1))
            send(block, to_c, there)
    for far in range(4):
        for sign in (-1, 1) if far else (1,):
            level = z + sign * far
            there = (level >= 0) & (level <= 3)
            block = (level, far_x, c, far_y)
            arrive(block, there)
            send(block, to_c, there)
    for level in range(4):
        for px in range(2):
            for py in range(2):
                arrive((level, px, far_c, py), z >= 0)
    for owner, peer, slot, there in sent:
        pl.when(there)(lambda: copy(owner, peer, slot).wait_send())
    keep.wait()


def gather_first(shard, tensor, dp):
    shape = (tensor, dp) + shard.shape
    if (tensor, dp) != (2, 16):
        return lax.all_gather(shard, AXES, axis=0, tiled=True).reshape(shape)
    return call(
        gather_kernel,
        "gather",
        (),
        [pl.BlockSpec(memory_space=pltpu.VMEM)],
        [pl.BlockSpec(memory_space=pl.ANY)],
        [(shape, bf16)],
        (shard,),
        [pltpu.SemaphoreType.DMA, pltpu.SemaphoreType.DMA((64,)), pltpu.SemaphoreType.DMA((32,))],
        collective_id=1,
        has_side_effects=True,
    )[0]


def tail_kernel(dp, tensor, *refs):
    count, depth = dp * tensor, dp // 4
    own_ref, refs = refs[0], refs[1:]
    others, refs = refs[: 2 * tensor - 1], refs[2 * tensor - 1 :]
    one_ref, two_ref, hb_ref, eb_ref, out_ref, sums_ref = refs[:6]
    packed, landed, line, arrived, send_sem, recv_sem, line_send, line_recv = refs[6:]
    d, y = lax.axis_index("dp"), lax.axis_index("tensor")
    me = d * tensor + y
    part = own_ref.shape[1]
    barrier = pltpu.get_barrier_semaphore()

    def place(k):
        other = lax.rem(me + k, count)
        return other, (lax.div(other, tensor), lax.rem(other, tensor))

    def greet(k, carry):
        _, where = place(k)
        pl.semaphore_signal(barrier, inc=1, device_id=where, device_id_type=pl.DeviceIdType.MESH)
        return carry

    lax.fori_loop(1, count, greet, 0)

    def plane(z):
        total = own_ref[z].astype(f32)
        for ref in others:
            total = total + ref[z].astype(f32)
        return total

    for z in range(1, depth):
        line[z - 1] = plane(z).astype(bf16)
    heads = hb_ref.shape[1] // HEAD_DIM
    own_heads, hb_wide = heads // tensor, HEAD_DIM // dp
    eb_tall, eb_wide = eb_ref.shape[0] // tensor, eb_ref.shape[1] // dp
    hb = [
        hb_ref[k : k + 1, h * HEAD_DIM : (h + 1) * HEAD_DIM] for k in range(2) for h in range(heads)
    ]
    hb = jnp.concatenate(hb, axis=0).T
    eb = eb_ref[...].T
    sums = jnp.concatenate([one_ref[...], two_ref[3:4], two_ref[1:3], two_ref[0:1]], axis=0)
    for p in range(dp):
        piece = sums[:, p * part : (p + 1) * part]
        for q in range(tensor):
            packed[p * tensor + q, 0:6, 0:part] = piece
            lane = part
            packed[p * tensor + q, 0:eb_wide, lane : lane + eb_tall] = eb[
                p * eb_wide : (p + 1) * eb_wide, q * eb_tall : (q + 1) * eb_tall
            ]
            for k in range(2):
                lane = part + eb_tall + k * own_heads
                packed[p * tensor + q, 0:hb_wide, lane : lane + own_heads] = hb[
                    p * hb_wide : (p + 1) * hb_wide,
                    k * heads + q * own_heads : k * heads + (q + 1) * own_heads,
                ]
    pl.semaphore_wait(barrier, count - 1)

    copies = []
    for z in range(1, depth):
        far = d
        for bit in range(depth.bit_length() - 1):
            if (z >> bit) & 1:
                unit = 4 << bit
                far = far + unit - 2 * unit * lax.rem(lax.div(far, unit), 2)
        copies.append(pltpu.make_async_remote_copy(
            src_ref=line.at[z - 1],
            dst_ref=arrived.at[z - 1],
            send_sem=line_send.at[z - 1],
            recv_sem=line_recv.at[z - 1],
            device_id=(far, y),
            device_id_type=pl.DeviceIdType.MESH,
        ))

    def copy(k):
        other, where = place(k)
        return pltpu.make_async_remote_copy(
            src_ref=packed.at[other],
            dst_ref=landed.at[k],
            send_sem=send_sem.at[k],
            recv_sem=recv_sem.at[k],
            device_id=where,
            device_id_type=pl.DeviceIdType.MESH,
        )

    def start(k, carry):
        copy(k).start()
        return carry

    lax.fori_loop(1, count, start, 0)
    for item in copies:
        item.start()
    total = plane(0)

    def finish(k, sums):
        copy(k).wait()
        return sums + landed[k]

    sums = lax.fori_loop(1, count, finish, packed[me])
    sums_ref[...] = sums
    for item, z in zip(copies, range(1, depth)):
        item.wait()
        total = total + arrived[z - 1].astype(f32)
    own = out_ref.shape[2]
    for s in range(3):
        out_ref[s] = total[:, s * own : (s + 1) * own]


def tail(part_own, landed, sums, hb, eb, tensor, dp):
    depth, part, lanes = part_own.shape
    count = tensor * dp
    arrays = [part_own, *landed, *sums, hb, eb]
    vmem = pl.BlockSpec(memory_space=pltpu.VMEM)
    out = [((3, part, lanes // 3), f32), ((8, 128), f32)]
    return call(
        functools.partial(tail_kernel, dp, tensor),
        "tail",
        (),
        [vmem] * len(arrays),
        [vmem] * len(out),
        out,
        arrays,
        [
            pltpu.VMEM((count, 8, 128), f32), pltpu.VMEM((count, 8, 128), f32),
            pltpu.VMEM((depth - 1, part, lanes), bf16), pltpu.VMEM((depth - 1, part, lanes), bf16),
            pltpu.SemaphoreType.DMA((count,)), pltpu.SemaphoreType.DMA((count,)),
            pltpu.SemaphoreType.DMA((depth - 1,)), pltpu.SemaphoreType.DMA((depth - 1,)),
        ],
        collective_id=0,
        has_side_effects=True,
    )


def finish_kernel(sums_ref, heads_ref, out_ref, hb_ref, eb_ref, *vectors):
    out_ref[...] = heads_ref[...]
    part = vectors[0].shape[1]
    for r, ref in enumerate(vectors):
        ref[...] = sums_ref[r : r + 1, :part]
    wide, tall = eb_ref.shape
    eb_ref[...] = sums_ref[:wide, part : part + tall]
    wide, count = hb_ref.shape[1:]
    for k in range(2):
        lane = part + tall + k * count
        hb_ref[k] = sums_ref[:wide, lane : lane + count]


def shards(
    tensor,
    dp,
    activations,
    first_gain,
    first_shift,
    heads_weight,
    heads_bias,
    merge_weight,
    merge_bias,
    second_gain,
    second_shift,
    expand_weight,
    expand_bias,
    reduce_weight,
    reduce_bias,
    output_grad,
    real_images,
):
    rows, deep = activations.shape
    images = rows // SEQ
    part = deep // dp
    own = heads_weight.shape[2]
    hidden_own = expand_weight.shape[1]
    hidden = hidden_own * tensor
    heads = deep // HEAD_DIM
    least = (images - 1) * STRIDE + WINDOW
    blocks = -(-least // 512)
    block = -(-least // blocks // 16) * 16
    total_rows = block * blocks

    def gather(shard):
        out = lax.all_gather(shard, AXES, axis=0, tiled=True)
        return out.reshape(tensor, dp, *shard.shape)

    small = [first_gain, first_shift, merge_bias, second_gain, second_shift, reduce_bias]
    arrays = [
        heads_weight, merge_weight.T, expand_weight, reduce_weight.T,
        heads_bias.transpose(0, 2, 1), expand_bias.T,
    ] + [v.reshape(1, part) for v in small]
    vmem = pl.BlockSpec(memory_space=pltpu.VMEM)
    first, later = call(
        pack_kernel, "pack", (), [vmem] * len(arrays), [vmem] * 2,
        [((part + 8, 4 * own), bf16), ((part, 2 * hidden_own), bf16)], arrays,
    )
    wide = gather(later)
    wide_heads = gather_first(first, tensor, dp)

    hbs, ebs = heads_bias.shape, expand_bias.shape
    small = wide_heads[:, :, part:, :128].astype(f32)
    vectors = small[0, :, :6, :part].transpose(1, 0, 2).reshape(6, deep)
    eb = small[:, :, : ebs[1], part : part + ebs[0]].transpose(0, 3, 1, 2).reshape(1, hidden)
    hb = small[:, :, : 2 * hbs[2], part + ebs[0] : part + ebs[0] + hbs[1]]
    hb = hb.reshape(tensor, dp, 2, hbs[2], hbs[1]).transpose(2, 0, 4, 1, 3).reshape(2, deep)
    live = jnp.clip(real_images - lax.axis_index("tensor") * images, 0, images) * SEQ

    def by_rows(width):
        return pl.BlockSpec((block, width), lambda i, *_: (i, 0))

    vec = full((6, deep))
    triple_spec = pl.BlockSpec((3, block, deep), lambda i: (0, i, 0))
    normed_one, triple = call(
        functools.partial(qkv_kernel, part, rows),
        "qkv",
        (blocks,),
        [by_rows(deep), vec, full((2, deep)), vmem],
        [by_rows(deep), triple_spec],
        [((total_rows, deep), bf16), ((3, total_rows, deep), bf16)],
        (activations, vectors, hb, wide_heads),
        flops=total_rows * deep * deep * 3,
    )

    group = 4
    groups = heads // group
    panel = group * HEAD_DIM
    head_spec = pl.BlockSpec((3, total_rows, panel), lambda g, i: (0, 0, g))
    ctx_spec = pl.BlockSpec((total_rows, panel), lambda g, i: (0, g))
    stat_spec = pl.BlockSpec((1, group, WINDOW), lambda g, i: (g * images + i, 0, 0))
    attend_flops = images * heads * WINDOW * 768 * 256 * 2
    context, stat = call(
        attend_kernel,
        "attend",
        (groups, images),
        [head_spec],
        [ctx_spec, stat_spec],
        [((total_rows, deep), bf16), ((images * groups, group, WINDOW), f32)],
        (triple,),
        flops=attend_flops,
    )

    resid, normed_two = call(
        functools.partial(merge_kernel, part, rows),
        "merge",
        (blocks,),
        [by_rows(deep), by_rows(deep), vec, vmem],
        [by_rows(deep), by_rows(deep)],
        [((total_rows, deep), f32), ((total_rows, deep), bf16)],
        (context, activations, vectors, wide_heads),
        flops=total_rows * deep * deep,
    )

    chunk = min(1024, hidden_own)
    output, active, slope, grad = call(
        functools.partial(mlp_kernel, chunk),
        "mlp",
        (blocks,),
        [
            by_rows(deep), by_rows(deep), full((1, hidden)), vec, vmem, by_rows(deep),
        ],
        [by_rows(deep), by_rows(hidden), by_rows(hidden), by_rows(deep)],
        [
            ((rows, deep), bf16), ((total_rows, hidden), bf16), ((total_rows, hidden), bf16),
            ((total_rows, deep), bf16),
        ],
        (live, normed_two, resid, eb, vectors, wide, output_grad),
        prefetch=1,
        flops=total_rows * deep * hidden * 2,
        vmem=44,
    )

    def scatter(grads):
        grads = grads.reshape(tensor * dp * part, grads.shape[3])
        return lax.psum_scatter(grads, AXES, scatter_dimension=0, tiled=True)

    grad_reduce = weight_grads("reduce_grad", [(grad, active)], tensor, dp, 512)
    grad, slope, grad_reduce = lax.optimization_barrier((grad, slope, grad_reduce))
    grad_reduce = scatter(grad_reduce)

    back_chunk = min(512, hidden_own)
    pre_grad, resid_low, grad_context, sums_two, esum = call(
        functools.partial(mlp_back_kernel, part, back_chunk),
        "mlp_back",
        (blocks,),
        [
            by_rows(deep), by_rows(hidden), by_rows(deep), vec,
            vmem,
            pl.BlockSpec(
                (tensor, dp, part + 8, own), lambda i: (0, 0, 0, 3), pipeline_mode=pl.Buffered(1)
            ),
        ],
        [
            by_rows(hidden), by_rows(deep), by_rows(deep),
            pl.BlockSpec((4, deep), lambda i: (0, 0)), pl.BlockSpec((hidden // 128, 128), lambda i: (0, 0)),
        ],
        [
            ((total_rows, hidden), bf16), ((total_rows, deep), bf16), ((total_rows, deep), bf16),
            ((4, deep), f32), ((hidden // 128, 128), f32),
        ],
        (grad, slope, resid, vectors, wide, wide_heads),
        vmem=44,
    )
    parts = slot_grads(
        "middle_grad", [(normed_two, pre_grad[None]), (resid_low, context[None])], tensor, dp, 512, 2
    )
    *parts, grad_context = lax.optimization_barrier((*parts, grad_context))
    landed = send_plane(parts, tensor, dp)
    grad_triple = call(
        attend_back_kernel,
        "attend_back",
        (groups, images),
        [head_spec, stat_spec, ctx_spec],
        [head_spec],
        [((3, total_rows, deep), bf16)],
        (triple, stat, grad_context),
    )[0]
    *landed, part_own, grad_triple = lax.optimization_barrier((*landed, parts[0], grad_triple))
    planes = sum_plane(part_own, landed, dp)
    *planes, grad_triple = lax.optimization_barrier((*planes, grad_triple))
    landed = send_line(planes, tensor, dp)
    parts = slot_grads("heads_grad", [(normed_one, grad_triple)], tensor, dp, 512, 3)
    held = (tuple(parts), tuple(landed), planes[0], resid_low)
    parts, landed, plane_own, resid_low = lax.optimization_barrier(held)
    last = send_plane(parts, tensor, dp)
    grad_middle = sum_line(plane_own, landed)
    input_grad, sums_one, bsum = call(
        functools.partial(qkv_back_kernel, part, rows),
        "qkv_back",
        (blocks,),
        [by_rows(deep), by_rows(deep), vec, triple_spec, vmem],
        [by_rows(deep), pl.BlockSpec((2, deep), lambda i: (0, 0)), pl.BlockSpec((2, deep), lambda i: (0, 0))],
        [((rows, deep), bf16), ((2, deep), f32), ((2, deep), f32)],
        (activations, resid_low, vectors, grad_triple, wide_heads),
        flops=total_rows * deep * deep * 3,
    )

    heads_sum, sums = tail(parts[0], last, (sums_one, sums_two), bsum, esum, tensor, dp)
    grad_heads, hb_grad, eb_grad, *vector = call(
        finish_kernel, "finish", (), [vmem] * 2, [vmem] * 9,
        [(heads_sum.shape, f32), ((2, hbs[2], hbs[1]), f32), (ebs[::-1], f32)] + [((1, part), f32)] * 6,
        (sums, heads_sum),
    )
    vector = [v.reshape(part) for v in vector]

    return (
        output,
        input_grad,
        vector[0],
        vector[1],
        grad_heads,
        hb_grad.transpose(0, 2, 1),
        grad_middle[:, hidden_own:].T,
        vector[2],
        vector[3],
        vector[4],
        grad_middle[:, :hidden_own],
        eb_grad.T,
        grad_reduce.astype(f32).T,
        vector[5],
    )


def solution(mesh):
    rows = P(("dp", "tensor"), None)
    specs = (
        P("dp"),
        P("dp"),
        P(None, "dp", "tensor"),
        P(None, "tensor", "dp"),
        P("tensor", "dp"),
        P("dp"),
        P("dp"),
        P("dp"),
        P("dp", "tensor"),
        P("tensor", "dp"),
        P("tensor", "dp"),
        P("dp"),
    )
    return jax.shard_map(
        functools.partial(shards, mesh.shape["tensor"], mesh.shape["dp"]),
        mesh=mesh,
        in_specs=(rows,) + specs + (rows, P("dp")),
        out_specs=(rows, rows) + specs,
        check_vma=False,
    )
```

```python
import functools
import math

import jax
import jax.numpy as jnp
from jax import lax
from jax.experimental import pallas as pl
from jax.experimental.pallas import tpu as pltpu
from jax.sharding import PartitionSpec as P

HEAD_DIM = 64
SEQ = 577
STRIDE = 576
WINDOW = 592
LANES = 640
EPSILON = 1e-06
LOG_SCALE = 0.125
bf16 = jnp.bfloat16
f32 = jnp.float32
NN = (((1,), (0,)), ((), ()))
NT = (((1,), (1,)), ((), ()))
TN = (((0,), (0,)), ((), ()))
AXES = ("tensor", "dp")


def matmul(left, right, dims=NN):
    return lax.dot_general(left, right, dims, preferred_element_type=f32)


def norm_parts(values):
    center = values - jnp.mean(values, axis=-1, keepdims=True)
    second = jnp.mean(center * center, axis=-1, keepdims=True)
    inv = lax.rsqrt(second + EPSILON)
    return center * inv, inv


def gelu_and_slope(pre):
    phi = 0.5 + 0.5 * lax.erf(pre * 0.7071067811865476)
    bell = jnp.exp(pre * pre * -0.5)
    return pre * phi, phi + pre * (bell * 0.3989422804014327)


def full(shape):
    return pl.BlockSpec(shape, lambda *_: (0,) * len(shape), pipeline_mode=pl.Buffered(1))


def call(kernel, name, grid, in_specs, out_specs, out_shape, args, scratch=(), flops=0, prefetch=0, **params):
    moved = 0
    if flops:
        moved = sum(a.size * a.dtype.itemsize for a in args)
        moved += sum(math.prod(shape) * jnp.dtype(dtype).itemsize for shape, dtype in out_shape)
    return pl.pallas_call(
        kernel,
        grid_spec=pltpu.PrefetchScalarGridSpec(
            num_scalar_prefetch=prefetch,
            grid=grid,
            in_specs=in_specs,
            out_specs=out_specs,
            scratch_shapes=list(scratch),
        ),
        out_shape=[jax.ShapeDtypeStruct(shape, dtype) for shape, dtype in out_shape],
        compiler_params=pltpu.CompilerParams(vmem_limit_bytes=60 * 2**20, **params),
        cost_estimate=pl.CostEstimate(flops=2 * flops, bytes_accessed=moved, transcendentals=0),
        name=name,
    )(*args)


def before(ref, count):
    height = ref.shape[0]
    rows = pl.program_id(0) * height + lax.broadcasted_iota(jnp.int32, (height, 1), 0)
    return jnp.where(rows < count, ref[...].astype(f32), 0.0)


def qkv_kernel(part, count, x_ref, vec_ref, bias_ref, w_ref, normed_ref, triple_ref):
    hat, _ = norm_parts(before(x_ref, count))
    normed = (hat * vec_ref[0:1] + vec_ref[1:2]).astype(bf16)
    normed_ref[...] = normed
    tensor, dp = w_ref.shape[:2]
    width = w_ref.shape[3] // 4
    for s in range(3):
        for t in range(tensor):
            cols = slice(t * width, (t + 1) * width)
            w = w_ref[t, :, :part, s * width : (s + 1) * width].reshape(dp * part, width)
            out = matmul(normed, w)
            if s != 1:
                out = out + bias_ref[s // 2 : s // 2 + 1, cols]
            triple_ref[s, :, cols] = out.astype(bf16)


def window(image):
    start = pl.multiple_of(image * STRIDE, 16)
    return pl.ds(start, WINDOW)


def keep_before(image, ref, index, value):
    edge = pl.ds(pl.multiple_of(image * STRIDE, 16), 16)
    rest = pl.ds(pl.multiple_of(image * STRIDE + 16, 16), WINDOW - 16)
    rows = lax.broadcasted_iota(jnp.int32, (16, 1), 0)
    head = jnp.where(rows < image, ref[(*index[:-1], edge, index[-1])].astype(f32), value[:16])
    ref[(*index[:-1], edge, index[-1])] = head.astype(ref.dtype)
    ref[(*index[:-1], rest, index[-1])] = value[16:].astype(ref.dtype)


def two_heads(first, second):
    blank, below = jnp.zeros_like(first), jnp.zeros((LANES - WINDOW, 2 * HEAD_DIM), first.dtype)
    return jnp.concatenate(
        [
            jnp.concatenate([first, blank], axis=1), below,
            jnp.concatenate([blank, second], axis=1), below,
        ],
        axis=0,
    )


def head_columns(h):
    return (
        slice(HEAD_DIM * h, HEAD_DIM * (h + 2)),
        (slice(HEAD_DIM * h, HEAD_DIM * (h + 1)), slice(HEAD_DIM * (h + 1), HEAD_DIM * (h + 2))),
    )


def attend_kernel(triple_ref, context_ref, stat_ref):
    image = pl.program_id(1)
    lanes = lax.broadcasted_iota(jnp.int32, (1, LANES), 1)
    mask = jnp.where((lanes >= image) & (lanes < image + SEQ), 0.0, -1e30)
    own = window(image)
    left = lax.broadcasted_iota(jnp.int32, (1, 2 * HEAD_DIM), 1) < HEAD_DIM
    stats = []
    for h in range(0, triple_ref.shape[2] // HEAD_DIM, 2):
        pair, single = head_columns(h)
        keys = two_heads(*(triple_ref[1, own, cols] for cols in single))
        both = matmul(triple_ref[0, own, pair] * bf16(LOG_SCALE), keys, NT)
        probs, scale = [], []
        for u in range(2):
            scores = both[:, u * LANES : (u + 1) * LANES] + mask
            top = jnp.max(scores, axis=1, keepdims=True)
            expo = jnp.exp(scores - top)
            total = jnp.sum(expo, axis=1, keepdims=True)
            probs.append(expo.astype(bf16))
            scale.append(1.0 / total)
            stats.append(top + jnp.log(total))
        values = two_heads(*(triple_ref[2, own, cols] for cols in single))
        context = matmul(jnp.concatenate(probs, axis=1), values)
        keep_before(image, context_ref, (pair,), context * jnp.where(left, *scale))
    stat_ref[0] = jnp.concatenate(stats, axis=1).T


def attend_back_kernel(triple_ref, stat_ref, grad_ref, out_ref):
    image = pl.program_id(1)
    rows = lax.broadcasted_iota(jnp.int32, (WINDOW, 1), 0)
    mask = jnp.where((rows >= image) & (rows < image + SEQ), 0.0, -1e30)
    lanes = lax.broadcasted_iota(jnp.int32, (1, LANES), 1)
    real = (lanes >= image) & (lanes < image + SEQ)
    own = window(image)
    for h in range(0, triple_ref.shape[2] // HEAD_DIM, 2):
        pair, single = head_columns(h)
        keys = triple_ref[1, own, pair]
        queries = [triple_ref[0, own, cols] for cols in single]
        grads = [grad_ref[own, cols] for cols in single]
        both = matmul(keys, two_heads(*queries) * bf16(LOG_SCALE), NT)
        both_grad = matmul(triple_ref[2, own, pair], two_heads(*grads), NT)
        turned = keys.T
        value_grad, key_grad, query_grad = [], [], []
        for u in range(2):
            side = slice(u * LANES, (u + 1) * LANES)
            stat = jnp.concatenate(
                [stat_ref[0, h + u : h + u + 1, :], jnp.zeros((1, LANES - WINDOW), f32)], axis=1
            )
            probs = jnp.exp(both[:, side] + mask - jnp.where(real, stat, 1e30))
            grad_probs = both_grad[:, side]
            inner = jnp.sum(probs * grad_probs, axis=0, keepdims=True)
            grad_scores = (probs * (grad_probs - inner)).astype(bf16)
            out = matmul(
                jnp.concatenate([probs.astype(bf16), grad_scores], axis=1),
                two_heads(grads[u], queries[u]),
            )
            value_grad.append(out[:, :HEAD_DIM])
            key_grad.append(out[:, HEAD_DIM:])
            query_grad.append(matmul(turned[u * HEAD_DIM : (u + 1) * HEAD_DIM], grad_scores))
        keep_before(image, out_ref, (2, pair), jnp.concatenate(value_grad, axis=1))
        keep_before(image, out_ref, (1, pair), jnp.concatenate(key_grad, axis=1) * LOG_SCALE)
        query_grad = jnp.concatenate(query_grad, axis=0).T[:WINDOW]
        keep_before(image, out_ref, (0, pair), query_grad * LOG_SCALE)


def merge_kernel(part, count, ctx_ref, x_ref, vec_ref, w_ref, resid_ref, normed_ref):
    tensor, dp, _, width = w_ref.shape
    total = before(x_ref, count) + vec_ref[2:3]
    for t in range(tensor):
        w = w_ref[t, :, :part].reshape(dp * part, width)
        total = total + matmul(ctx_ref[:, t * width : (t + 1) * width], w, NT)
    resid_ref[...] = total
    hat, _ = norm_parts(total)
    normed_ref[...] = (hat * vec_ref[3:4] + vec_ref[4:5]).astype(bf16)


def mlp_kernel(
    chunk, live_ref, normed_ref, resid_ref, ebias_ref, vec_ref, e_ref, r_ref, given_ref,
    out_ref, act_ref, slope_ref, grad_ref,
):
    grad_ref[...] = before(given_ref, live_ref[0]).astype(bf16)
    tensor, dp, rows, width = e_ref.shape
    normed = normed_ref[...]
    total = resid_ref[...] + vec_ref[5:6]
    for t in range(tensor):
        for c in range(width // chunk):
            local = slice(c * chunk, (c + 1) * chunk)
            cols = slice(t * width + c * chunk, t * width + (c + 1) * chunk)
            e = e_ref[t, :, :, local].reshape(dp * rows, chunk)
            active, slope = gelu_and_slope(matmul(normed, e) + ebias_ref[:, cols])
            active = active.astype(bf16)
            act_ref[:, cols] = active
            slope_ref[:, cols] = slope.astype(bf16)
            r = r_ref[t, :, :, local].reshape(dp * rows, chunk)
            total = total + matmul(active, r, NT)
    out_ref[...] = total.astype(bf16)


def accumulate(first, ref, value):
    @pl.when(first)
    def _():
        ref[...] = value

    @pl.when(jnp.logical_not(first))
    def _():
        ref[...] += value


def norm_back(values, gain, grad):
    hat, inv = norm_parts(values)
    scaled = grad * gain
    back = (
        scaled
        - jnp.mean(scaled, axis=-1, keepdims=True)
        - hat * jnp.mean(scaled * hat, axis=-1, keepdims=True)
    ) * inv
    return back, jnp.sum(grad * hat, axis=0, keepdims=True), jnp.sum(grad, axis=0, keepdims=True)


def mlp_back_kernel(
    part, chunk, grad_ref, slope_ref, resid_ref, vec_ref, e_ref, r_ref, m_ref,
    pre_ref, low_ref, ctx_ref, sums_ref, esum_ref,
):
    tensor, dp, rows, width = e_ref.shape
    first = pl.program_id(0) == 0
    grad = grad_ref[...]
    total = jnp.zeros(grad.shape, f32)
    parts = []
    for t in range(tensor):
        for c in range(width // chunk):
            local = slice(c * chunk, (c + 1) * chunk)
            cols = slice(t * width + c * chunk, t * width + (c + 1) * chunk)
            r = r_ref[t, :, :, local].reshape(dp * rows, chunk)
            pre = (matmul(grad, r) * slope_ref[:, cols].astype(f32)).astype(bf16)
            pre_ref[:, cols] = pre
            parts.append(jnp.sum(pre.astype(f32), axis=0, keepdims=True))
            e = e_ref[t, :, :, local].reshape(dp * rows, chunk)
            total = total + matmul(pre, e, NT)
    sums = 0
    half = grad.shape[0] // 2
    for rows_half in (slice(0, half), slice(half, 2 * half)):
        own = grad_ref[rows_half].astype(f32)
        back, gain_sum, shift_sum = norm_back(resid_ref[rows_half], vec_ref[3:4], total[rows_half])
        resid_grad = own + back
        low_ref[rows_half] = resid_grad.astype(bf16)
        lines = [jnp.sum(own, axis=0, keepdims=True), gain_sum, shift_sum]
        sums = sums + jnp.concatenate(lines + [jnp.sum(resid_grad, axis=0, keepdims=True)], axis=0)
    low = low_ref[...]
    wide = m_ref.shape[3]
    for t in range(tensor):
        m = m_ref[t, :, :part].reshape(dp * part, wide)
        ctx_ref[:, t * wide : (t + 1) * wide] = matmul(low, m).astype(bf16)
    accumulate(first, sums_ref, sums)
    parts = jnp.concatenate(parts, axis=1)
    lines = [parts[:, k * 128 : (k + 1) * 128] for k in range(esum_ref.shape[0])]
    accumulate(first, esum_ref, jnp.concatenate(lines, axis=0))


def qkv_back_kernel(part, count, x_ref, low_ref, vec_ref, grad_ref, w_ref, out_ref, sums_ref, bsum_ref):
    tensor, dp = w_ref.shape[:2]
    width = w_ref.shape[3] // 4
    first = pl.program_id(0) == 0
    total = jnp.zeros(x_ref.shape, f32)
    for s in range(3):
        for t in range(tensor):
            w = w_ref[t, :, :part, s * width : (s + 1) * width].reshape(dp * part, width)
            total = total + matmul(grad_ref[s, :, t * width : (t + 1) * width], w, NT)
    back, gain_sum, shift_sum = norm_back(before(x_ref, count), vec_ref[0:1], total)
    out_ref[...] = (low_ref[...].astype(f32) + back).astype(bf16)
    accumulate(first, sums_ref, jnp.concatenate([gain_sum, shift_sum], axis=0))
    bias = [jnp.sum(grad_ref[s].astype(f32), axis=0, keepdims=True) for s in (0, 2)]
    accumulate(first, bsum_ref, jnp.concatenate(bias, axis=0))


def weight_grad_kernel(starts, *refs):
    count = len(starts) - 1
    lefts, rights, out_ref = refs[:count], refs[count : 2 * count], refs[-1]
    step = pl.program_id(0)
    for j in range(count):
        @pl.when((step >= starts[j]) & (step < starts[j + 1]))
        def _():
            out = matmul(lefts[j][...], rights[j][0], TN)
            out_ref[...] = out.astype(bf16).reshape(out_ref.shape)


def weight_grads(name, pairs, tensor, dp, block):
    rows, deep = pairs[0][0].shape
    locals_ = [right.shape[1] // tensor for _, right in pairs]
    block = min([block] + locals_)
    pers = [local // block for local in locals_]
    starts = [0]
    for per in pers:
        starts.append(starts[-1] + tensor * per)

    def right_map(j, i):
        i = jnp.clip(i - starts[j], 0, tensor * pers[j] - 1)
        return (0, 0, i)

    def out_map(i):
        where, column, t = 0, 0, 0
        for j, per in enumerate(pers):
            inside = (i >= starts[j]) & (i < starts[j + 1])
            t = t + jnp.where(inside, (i - starts[j]) // per, 0)
            column = column + jnp.where(inside, where + (i - starts[j]) % per, 0)
            where += per
        return (t, 0, 0, column)

    return call(
        functools.partial(weight_grad_kernel, starts),
        name,
        (starts[-1],),
        [full((rows, deep))] * len(pairs)
        + [pl.BlockSpec((1, rows, block), functools.partial(right_map, j)) for j in range(len(pairs))],
        [pl.BlockSpec((1, dp, deep // dp, block), out_map)],
        [((tensor, dp, deep // dp, sum(locals_)), bf16)],
        [left for left, _ in pairs] + [right[None] for _, right in pairs],
        flops=rows * deep * tensor * sum(locals_),
    )[0]


def flip(value, mask):
    unit = 1
    while unit <= mask:
        if mask & unit:
            value = value + unit - 2 * unit * lax.rem(lax.div(value, unit), 2)
        unit *= 2
    return value


def differ(left, right, size):
    total, unit = 0, 1
    while unit < size:
        p, q = lax.rem(lax.div(left, unit), 2), lax.rem(lax.div(right, unit), 2)
        total = total + unit * (p + q - 2 * p * q)
        unit *= 2
    return total


def slot_grad_kernel(tensor, dp, starts, *refs):
    count, steps, depth = len(starts) - 1, starts[-1], dp // 4
    lefts, rights, outs = refs[:count], refs[count : 2 * count], refs[2 * count : 2 * count + 2 * tensor]
    total, keep, send, landed, send_sem, recv_sem = refs[2 * count + 2 * tensor :]
    step, t = pl.program_id(0), pl.program_id(1)
    d, y = lax.axis_index("dp"), lax.axis_index("tensor")
    part, block = total.shape[0] // dp, total.shape[1]
    column = differ(t, y, tensor)
    slots = pl.ds(column * (2 * depth), 2 * depth)

    def copy(step):
        cols = pl.ds(pl.multiple_of(step * block, block), block)
        return pltpu.make_async_remote_copy(
            src_ref=send.at[slots, :, cols],
            dst_ref=landed.at[slots, :, cols],
            send_sem=send_sem.at[step * tensor + t],
            recv_sem=recv_sem.at[step * tensor + t],
            device_id=(flip(d, 1), y),
            device_id_type=pl.DeviceIdType.MESH,
        )

    @pl.when((step == 0) & (t == 0))
    def _():
        barrier = pltpu.get_barrier_semaphore()
        pl.semaphore_signal(
            barrier, inc=1, device_id=(flip(d, 1), y), device_id_type=pl.DeviceIdType.MESH
        )
        pl.semaphore_wait(barrier, 1)

    for j in range(count):
        @pl.when((step >= starts[j]) & (step < starts[j + 1]))
        def _():
            total[...] = matmul(lefts[j][...], rights[j][0], TN)

    @pl.when(step < steps)
    def _():
        cols = pl.ds(pl.multiple_of(step * block, block), block)
        for r in range(dp):
            owner = pl.multiple_of(flip(d, r) * part, part)
            half = send if r & 1 else keep
            slot = column * (2 * depth) + ((r >> 1) & 1) * depth + (r >> 2)
            half[slot, :, cols] = total[pl.ds(owner, part), :].astype(bf16)
        copy(step).start()

    @pl.when(step > 0)
    def _():
        copy(step - 1).wait()
        cols = pl.ds(pl.multiple_of((step - 1) * block, block), block)
        for k in range(2 * tensor):
            @pl.when(column == k // 2)
            def _():
                own = pl.ds(k * depth, depth)
                both = keep[own, :, cols].astype(f32) + landed[own, :, cols].astype(f32)
                outs[k][...] = both.astype(bf16)


def slot_grads(name, pairs, tensor, dp, block, collective_id):
    rows, deep = pairs[0][0].shape
    part, depth = deep // dp, dp // 4
    block = min([block] + [right.shape[2] // tensor for _, right in pairs])
    pers = [right.shape[2] // tensor // block for _, right in pairs]
    starts = [0]
    for (_, right), per in zip(pairs, pers):
        starts.append(starts[-1] + right.shape[0] * per)
    wide = starts[-1] * block
    half = tensor * dp // 2

    def right_map(j, i, t):
        t = jnp.where(i < starts[j], 0, jnp.where(i >= starts[j + 1], tensor - 1, t))
        i = jnp.clip(i - starts[j], 0, starts[j + 1] - starts[j] - 1)
        return (i // pers[j], 0, t * pers[j] + i % pers[j])

    spec = pl.BlockSpec((depth, part, block), lambda i, t: (0, 0, jnp.maximum(i - 1, 0)))
    return call(
        functools.partial(slot_grad_kernel, tensor, dp, starts),
        name,
        (starts[-1] + 1, tensor),
        [full((rows, deep))] * len(pairs)
        + [pl.BlockSpec((1, rows, block), functools.partial(right_map, j)) for j in range(len(pairs))],
        [spec] * (2 * tensor),
        [((depth, part, wide), bf16)] * (2 * tensor),
        [left for left, _ in pairs] + [right for _, right in pairs],
        [pltpu.VMEM((deep, block), f32)]
        + [pltpu.VMEM((half, part, wide), bf16)] * 3
        + [pltpu.SemaphoreType.DMA((starts[-1] * tensor,))] * 2,
        collective_id=collective_id,
        has_side_effects=True,
    )


def swap(values, d, t, tensor, dp):
    moves = []
    for p in range(dp):
        for q in range(tensor):
            moves.append((p * tensor + q, (p ^ d) * tensor + (q ^ t)))
    return lax.ppermute(values, ("dp", "tensor"), moves)


def send_plane(parts, tensor, dp):
    return [swap(parts[k], 2 * (k % 2), k // 2, tensor, dp) for k in range(1, 2 * tensor)]


def sum_plane(part, landed, dp):
    planes = []
    for z in range(dp // 4):
        total = part[z].astype(f32)
        for piece in landed:
            total = total + piece[z].astype(f32)
        planes.append(total.astype(bf16))
    return planes


def send_line(planes, tensor, dp):
    return [swap(planes[z], 4 * z, 0, tensor, dp) for z in range(1, dp // 4)]


def sum_line(plane, landed):
    total = plane.astype(f32)
    for piece in landed:
        total = total + piece.astype(f32)
    return total


def pack_kernel(
    heads_ref, merge_ref, expand_ref, reduce_ref, hb_ref, eb_ref, *refs
):
    small, (first_ref, later_ref) = refs[:-2], refs[-2:]
    _, part, own = heads_ref.shape
    for s in range(3):
        first_ref[:part, s * own : (s + 1) * own] = heads_ref[s]
    lines = [ref[...].astype(f32) for ref in small] + [jnp.zeros((8 - len(small), part), f32)]
    hb = hb_ref[...].astype(f32)
    hb = hb.reshape(hb.shape[0] * hb.shape[1], hb.shape[2])
    eb = eb_ref[...].astype(f32)
    pieces = []
    for piece in (jnp.concatenate(lines, axis=0), eb, hb):
        height, width = piece.shape
        if height < 8:
            piece = jnp.concatenate([piece, jnp.zeros((8 - height, width), f32)], axis=0)
        pieces.append(piece)
    used = sum(piece.shape[1] for piece in pieces)
    pieces.append(jnp.zeros((8, 128 - used), f32))
    first_ref[part:, :128] = jnp.concatenate(pieces, axis=1).astype(bf16)
    first_ref[:part, 3 * own :] = merge_ref[...]
    first_ref[part:, 128:] = jnp.zeros((8, 4 * own - 128), bf16)
    hidden = expand_ref.shape[1]
    later_ref[:, :hidden] = expand_ref[...]
    later_ref[:, hidden:] = reduce_ref[...]


def gather_kernel(in_ref, out_ref, own_sem, send_sem, recv_sem):
    d, y = lax.axis_index("dp"), lax.axis_index("tensor")
    z, x, c = lax.div(d, 4), lax.rem(lax.div(d, 2), 2), lax.rem(d, 2)
    far_x, far_y, far_c = 1 - x, 1 - y, 1 - c
    barrier = pltpu.get_barrier_semaphore()

    def index(place):
        pz, px, pc, py = place
        return (pz * 2 + px) * 2 + pc, py

    lower, upper = (z - 1, x, c, y), (z + 1, x, c, y)
    to_x, to_y, to_c = (z, far_x, c, y), (z, x, c, far_y), (z, x, far_c, y)

    def greet(peer):
        pl.semaphore_signal(barrier, inc=1, device_id=index(peer), device_id_type=pl.DeviceIdType.MESH)

    for peer in (to_x, to_y, to_c):
        greet(peer)
    pl.when(z > 0)(lambda: greet(lower))
    pl.when(z < 3)(lambda: greet(upper))
    pl.semaphore_wait(barrier, 4 + lax.rem(lax.div(z + 1, 2), 2))

    sent = []

    def copy(owner, peer, slot, source=None):
        p, q = index(owner)
        return pltpu.make_async_remote_copy(
            src_ref=out_ref.at[q, p] if source is None else source,
            dst_ref=out_ref.at[q, p],
            send_sem=send_sem.at[slot],
            recv_sem=recv_sem.at[p * 2 + q],
            device_id=index(peer),
            device_id_type=pl.DeviceIdType.MESH,
        )

    def send(owner, peer, there, source=None):
        slot = len(sent)
        sent.append((owner, peer, slot, there))

        @pl.when(there)
        def _():
            copy(owner, peer, slot, source).start()

    def arrive(owner, there):
        @pl.when(there)
        def _():
            copy(owner, to_c, 0).wait_recv()

    own = (z, x, c, y)
    keep = pltpu.make_async_copy(in_ref, out_ref.at[y, d], own_sem)
    send(own, upper, z < 3, in_ref)
    send(own, lower, z > 0, in_ref)
    for peer in (to_x, to_y, to_c):
        send(own, peer, z >= 0, in_ref)
    keep.start()
    for far in range(1, 4):
        for sign, after, onward in ((-1, upper, z < 3), (1, lower, z > 0)):
            level = z + sign * far
            there = (level >= 0) & (level <= 3)
            block = (level, x, c, y)
            arrive(block, there)
            send(block, after, there & onward)
            for peer in (to_x, to_y, to_c):
                send(block, peer, there)
    for far in range(4):
        for sign in (-1, 1) if far else (1,):
            level = z + sign * far
            there = (level >= 0) & (level <= 3)
            odd = lax.rem(level + 4, 2)
            block = (level, far_x, c, y)
            arrive(block, there)
            send(block, to_y, there & (odd == 0))
            send(block, to_c, there)
            block = (level, x, c, far_y)
            arrive(block, there)
            send(block, to_x, there & (odd == 1))
            send(block, to_c, there)
    for far in range(4):
        for sign in (-1, 1) if far else (1,):
            level = z + sign * far
            there = (level >= 0) & (level <= 3)
            block = (level, far_x, c, far_y)
            arrive(block, there)
            send(block, to_c, there)
    for level in range(4):
        for px in range(2):
            for py in range(2):
                arrive((level, px, far_c, py), z >= 0)
    for owner, peer, slot, there in sent:
        pl.when(there)(lambda: copy(owner, peer, slot).wait_send())
    keep.wait()


def gather_first(shard, tensor, dp):
    shape = (tensor, dp) + shard.shape
    if (tensor, dp) != (2, 16):
        return lax.all_gather(shard, AXES, axis=0, tiled=True).reshape(shape)
    return call(
        gather_kernel,
        "gather",
        (),
        [pl.BlockSpec(memory_space=pltpu.VMEM)],
        [pl.BlockSpec(memory_space=pl.ANY)],
        [(shape, bf16)],
        (shard,),
        [pltpu.SemaphoreType.DMA, pltpu.SemaphoreType.DMA((64,)), pltpu.SemaphoreType.DMA((32,))],
        collective_id=1,
        has_side_effects=True,
    )[0]


def tail_kernel(dp, tensor, *refs):
    count, depth = dp * tensor, dp // 4
    own_ref, refs = refs[0], refs[1:]
    others, refs = refs[: 2 * tensor - 1], refs[2 * tensor - 1 :]
    one_ref, two_ref, hb_ref, eb_ref, out_ref, sums_ref = refs[:6]
    packed, landed, line, arrived, send_sem, recv_sem, line_send, line_recv = refs[6:]
    d, y = lax.axis_index("dp"), lax.axis_index("tensor")
    me = d * tensor + y
    part = own_ref.shape[1]
    barrier = pltpu.get_barrier_semaphore()

    def place(k):
        other = lax.rem(me + k, count)
        return other, (lax.div(other, tensor), lax.rem(other, tensor))

    def greet(k, carry):
        _, where = place(k)
        pl.semaphore_signal(barrier, inc=1, device_id=where, device_id_type=pl.DeviceIdType.MESH)
        return carry

    lax.fori_loop(1, count, greet, 0)

    def plane(z):
        total = own_ref[z].astype(f32)
        for ref in others:
            total = total + ref[z].astype(f32)
        return total

    for z in range(1, depth):
        line[z - 1] = plane(z).astype(bf16)
    heads = hb_ref.shape[1] // HEAD_DIM
    own_heads, hb_wide = heads // tensor, HEAD_DIM // dp
    eb_tall, eb_wide = eb_ref.shape[0] // tensor, eb_ref.shape[1] // dp
    hb = [
        hb_ref[k : k + 1, h * HEAD_DIM : (h + 1) * HEAD_DIM] for k in range(2) for h in range(heads)
    ]
    hb = jnp.concatenate(hb, axis=0).T
    eb = eb_ref[...].T
    sums = jnp.concatenate([one_ref[...], two_ref[3:4], two_ref[1:3], two_ref[0:1]], axis=0)
    for p in range(dp):
        piece = sums[:, p * part : (p + 1) * part]
        for q in range(tensor):
            packed[p * tensor + q, 0:6, 0:part] = piece
            lane = part
            packed[p * tensor + q, 0:eb_wide, lane : lane + eb_tall] = eb[
                p * eb_wide : (p + 1) * eb_wide, q * eb_tall : (q + 1) * eb_tall
            ]
            for k in range(2):
                lane = part + eb_tall + k * own_heads
                packed[p * tensor + q, 0:hb_wide, lane : lane + own_heads] = hb[
                    p * hb_wide : (p + 1) * hb_wide,
                    k * heads + q * own_heads : k * heads + (q + 1) * own_heads,
                ]
    pl.semaphore_wait(barrier, count - 1)

    copies = []
    for z in range(1, depth):
        far = d
        for bit in range(depth.bit_length() - 1):
            if (z >> bit) & 1:
                unit = 4 << bit
                far = far + unit - 2 * unit * lax.rem(lax.div(far, unit), 2)
        copies.append(pltpu.make_async_remote_copy(
            src_ref=line.at[z - 1],
            dst_ref=arrived.at[z - 1],
            send_sem=line_send.at[z - 1],
            recv_sem=line_recv.at[z - 1],
            device_id=(far, y),
            device_id_type=pl.DeviceIdType.MESH,
        ))

    def copy(k):
        other, where = place(k)
        return pltpu.make_async_remote_copy(
            src_ref=packed.at[other],
            dst_ref=landed.at[k],
            send_sem=send_sem.at[k],
            recv_sem=recv_sem.at[k],
            device_id=where,
            device_id_type=pl.DeviceIdType.MESH,
        )

    def start(k, carry):
        copy(k).start()
        return carry

    lax.fori_loop(1, count, start, 0)
    for item in copies:
        item.start()
    total = plane(0)

    def finish(k, sums):
        copy(k).wait()
        return sums + landed[k]

    sums = lax.fori_loop(1, count, finish, packed[me])
    sums_ref[...] = sums
    for item, z in zip(copies, range(1, depth)):
        item.wait()
        total = total + arrived[z - 1].astype(f32)
    own = out_ref.shape[2]
    for s in range(3):
        out_ref[s] = total[:, s * own : (s + 1) * own]


def tail(part_own, landed, sums, hb, eb, tensor, dp):
    depth, part, lanes = part_own.shape
    count = tensor * dp
    arrays = [part_own, *landed, *sums, hb, eb]
    vmem = pl.BlockSpec(memory_space=pltpu.VMEM)
    out = [((3, part, lanes // 3), f32), ((8, 128), f32)]
    return call(
        functools.partial(tail_kernel, dp, tensor),
        "tail",
        (),
        [vmem] * len(arrays),
        [vmem] * len(out),
        out,
        arrays,
        [
            pltpu.VMEM((count, 8, 128), f32), pltpu.VMEM((count, 8, 128), f32),
            pltpu.VMEM((depth - 1, part, lanes), bf16), pltpu.VMEM((depth - 1, part, lanes), bf16),
            pltpu.SemaphoreType.DMA((count,)), pltpu.SemaphoreType.DMA((count,)),
            pltpu.SemaphoreType.DMA((depth - 1,)), pltpu.SemaphoreType.DMA((depth - 1,)),
        ],
        collective_id=0,
        has_side_effects=True,
    )


def finish_kernel(sums_ref, heads_ref, out_ref, hb_ref, eb_ref, *vectors):
    out_ref[...] = heads_ref[...]
    part = vectors[0].shape[1]
    for r, ref in enumerate(vectors):
        ref[...] = sums_ref[r : r + 1, :part]
    wide, tall = eb_ref.shape
    eb_ref[...] = sums_ref[:wide, part : part + tall]
    wide, count = hb_ref.shape[1:]
    for k in range(2):
        lane = part + tall + k * count
        hb_ref[k] = sums_ref[:wide, lane : lane + count]


def shards(
    tensor,
    dp,
    activations,
    first_gain,
    first_shift,
    heads_weight,
    heads_bias,
    merge_weight,
    merge_bias,
    second_gain,
    second_shift,
    expand_weight,
    expand_bias,
    reduce_weight,
    reduce_bias,
    output_grad,
    real_images,
):
    rows, deep = activations.shape
    images = rows // SEQ
    part = deep // dp
    own = heads_weight.shape[2]
    hidden_own = expand_weight.shape[1]
    hidden = hidden_own * tensor
    heads = deep // HEAD_DIM
    least = (images - 1) * STRIDE + WINDOW
    blocks = -(-least // 512)
    block = -(-least // blocks // 16) * 16
    total_rows = block * blocks

    def gather(shard):
        out = lax.all_gather(shard, AXES, axis=0, tiled=True)
        return out.reshape(tensor, dp, *shard.shape)

    small = [first_gain, first_shift, merge_bias, second_gain, second_shift, reduce_bias]
    arrays = [
        heads_weight, merge_weight.T, expand_weight, reduce_weight.T,
        heads_bias.transpose(0, 2, 1), expand_bias.T,
    ] + [v.reshape(1, part) for v in small]
    vmem = pl.BlockSpec(memory_space=pltpu.VMEM)
    first, later = call(
        pack_kernel, "pack", (), [vmem] * len(arrays), [vmem] * 2,
        [((part + 8, 4 * own), bf16), ((part, 2 * hidden_own), bf16)], arrays,
    )
    wide = gather(later)
    wide_heads = gather_first(first, tensor, dp)

    hbs, ebs = heads_bias.shape, expand_bias.shape
    small = wide_heads[:, :, part:, :128].astype(f32)
    vectors = small[0, :, :6, :part].transpose(1, 0, 2).reshape(6, deep)
    eb = small[:, :, : ebs[1], part : part + ebs[0]].transpose(0, 3, 1, 2).reshape(1, hidden)
    hb = small[:, :, : 2 * hbs[2], part + ebs[0] : part + ebs[0] + hbs[1]]
    hb = hb.reshape(tensor, dp, 2, hbs[2], hbs[1]).transpose(2, 0, 4, 1, 3).reshape(2, deep)
    live = jnp.clip(real_images - lax.axis_index("tensor") * images, 0, images) * SEQ

    def by_rows(width):
        return pl.BlockSpec((block, width), lambda i, *_: (i, 0))

    def columns(array, index, width):
        shape = array.shape[:3] + (width,)
        return pl.BlockSpec(shape, lambda *_: (0, 0, 0, index), pipeline_mode=pl.Buffered(1))

    vec = full((6, deep))
    expand_spec, reduce_spec = columns(wide, 0, hidden_own), columns(wide, 1, hidden_own)
    merge_spec = columns(wide_heads, 3, own)
    triple_spec = pl.BlockSpec((3, block, deep), lambda i: (0, i, 0))
    normed_one, triple = call(
        functools.partial(qkv_kernel, part, rows),
        "qkv",
        (blocks,),
        [by_rows(deep), vec, full((2, deep)), full(wide_heads.shape)],
        [by_rows(deep), triple_spec],
        [((total_rows, deep), bf16), ((3, total_rows, deep), bf16)],
        (activations, vectors, hb, wide_heads),
        flops=total_rows * deep * deep * 3,
    )

    group = 4
    groups = heads // group
    panel = group * HEAD_DIM
    head_spec = pl.BlockSpec((3, total_rows, panel), lambda g, i: (0, 0, g))
    ctx_spec = pl.BlockSpec((total_rows, panel), lambda g, i: (0, g))
    stat_spec = pl.BlockSpec((1, group, WINDOW), lambda g, i: (g * images + i, 0, 0))
    attend_flops = images * heads * WINDOW * 768 * 256 * 2
    context, stat = call(
        attend_kernel,
        "attend",
        (groups, images),
        [head_spec],
        [ctx_spec, stat_spec],
        [((total_rows, deep), bf16), ((images * groups, group, WINDOW), f32)],
        (triple,),
        flops=attend_flops,
    )

    resid, normed_two = call(
        functools.partial(merge_kernel, part, rows),
        "merge",
        (blocks,),
        [by_rows(deep), by_rows(deep), vec, merge_spec],
        [by_rows(deep), by_rows(deep)],
        [((total_rows, deep), f32), ((total_rows, deep), bf16)],
        (context, activations, vectors, wide_heads),
        flops=total_rows * deep * deep,
    )

    chunk = min(1024, hidden_own)
    output, active, slope, grad = call(
        functools.partial(mlp_kernel, chunk),
        "mlp",
        (blocks,),
        [
            by_rows(deep), by_rows(deep), full((1, hidden)), vec, expand_spec, reduce_spec, by_rows(deep),
        ],
        [by_rows(deep), by_rows(hidden), by_rows(hidden), by_rows(deep)],
        [
            ((rows, deep), bf16), ((total_rows, hidden), bf16), ((total_rows, hidden), bf16),
            ((total_rows, deep), bf16),
        ],
        (live, normed_two, resid, eb, vectors, wide, wide, output_grad),
        prefetch=1,
        flops=total_rows * deep * hidden * 2,
    )

    def scatter(grads):
        grads = grads.reshape(tensor * dp * part, grads.shape[3])
        return lax.psum_scatter(grads, AXES, scatter_dimension=0, tiled=True)

    grad_reduce = weight_grads("reduce_grad", [(grad, active)], tensor, dp, 512)
    grad, slope, grad_reduce = lax.optimization_barrier((grad, slope, grad_reduce))
    grad_reduce = scatter(grad_reduce)

    back_chunk = min(512, hidden_own)
    pre_grad, resid_low, grad_context, sums_two, esum = call(
        functools.partial(mlp_back_kernel, part, back_chunk),
        "mlp_back",
        (blocks,),
        [
            by_rows(deep), by_rows(hidden), by_rows(deep), vec,
            expand_spec, reduce_spec, merge_spec,
        ],
        [
            by_rows(hidden), by_rows(deep), by_rows(deep),
            pl.BlockSpec((4, deep), lambda i: (0, 0)), pl.BlockSpec((hidden // 128, 128), lambda i: (0, 0)),
        ],
        [
            ((total_rows, hidden), bf16), ((total_rows, deep), bf16), ((total_rows, deep), bf16),
            ((4, deep), f32), ((hidden // 128, 128), f32),
        ],
        (grad, slope, resid, vectors, wide, wide, wide_heads),
    )
    parts = slot_grads(
        "middle_grad", [(normed_two, pre_grad[None]), (resid_low, context[None])], tensor, dp, 512, 2
    )
    *parts, grad_context = lax.optimization_barrier((*parts, grad_context))
    landed = send_plane(parts, tensor, dp)
    grad_triple = call(
        attend_back_kernel,
        "attend_back",
        (groups, images),
        [head_spec, stat_spec, ctx_spec],
        [head_spec],
        [((3, total_rows, deep), bf16)],
        (triple, stat, grad_context),
    )[0]
    *landed, part_own, grad_triple = lax.optimization_barrier((*landed, parts[0], grad_triple))
    planes = sum_plane(part_own, landed, dp)
    *planes, grad_triple = lax.optimization_barrier((*planes, grad_triple))
    landed = send_line(planes, tensor, dp)
    parts = slot_grads("heads_grad", [(normed_one, grad_triple)], tensor, dp, 512, 3)
    held = (tuple(parts), tuple(landed), planes[0], resid_low)
    parts, landed, plane_own, resid_low = lax.optimization_barrier(held)
    last = send_plane(parts, tensor, dp)
    grad_middle = sum_line(plane_own, landed)
    input_grad, sums_one, bsum = call(
        functools.partial(qkv_back_kernel, part, rows),
        "qkv_back",
        (blocks,),
        [by_rows(deep), by_rows(deep), vec, triple_spec, full(wide_heads.shape)],
        [by_rows(deep), pl.BlockSpec((2, deep), lambda i: (0, 0)), pl.BlockSpec((2, deep), lambda i: (0, 0))],
        [((rows, deep), bf16), ((2, deep), f32), ((2, deep), f32)],
        (activations, resid_low, vectors, grad_triple, wide_heads),
        flops=total_rows * deep * deep * 3,
    )

    heads_sum, sums = tail(parts[0], last, (sums_one, sums_two), bsum, esum, tensor, dp)
    grad_heads, hb_grad, eb_grad, *vector = call(
        finish_kernel, "finish", (), [vmem] * 2, [vmem] * 9,
        [(heads_sum.shape, f32), ((2, hbs[2], hbs[1]), f32), (ebs[::-1], f32)] + [((1, part), f32)] * 6,
        (sums, heads_sum),
    )
    vector = [v.reshape(part) for v in vector]

    return (
        output,
        input_grad,
        vector[0],
        vector[1],
        grad_heads,
        hb_grad.transpose(0, 2, 1),
        grad_middle[:, hidden_own:].T,
        vector[2],
        vector[3],
        vector[4],
        grad_middle[:, :hidden_own],
        eb_grad.T,
        grad_reduce.astype(f32).T,
        vector[5],
    )


def solution(mesh):
    rows = P(("dp", "tensor"), None)
    specs = (
        P("dp"),
        P("dp"),
        P(None, "dp", "tensor"),
        P(None, "tensor", "dp"),
        P("tensor", "dp"),
        P("dp"),
        P("dp"),
        P("dp"),
        P("dp", "tensor"),
        P("tensor", "dp"),
        P("tensor", "dp"),
        P("dp"),
    )
    return jax.shard_map(
        functools.partial(shards, mesh.shape["tensor"], mesh.shape["dp"]),
        mesh=mesh,
        in_specs=(rows,) + specs + (rows, P("dp")),
        out_specs=(rows, rows) + specs,
        check_vma=False,
    )
```

```python
import functools
import math

import jax
import jax.numpy as jnp
from jax import lax
from jax.experimental import pallas as pl
from jax.experimental.pallas import tpu as pltpu
from jax.sharding import PartitionSpec as P

HEAD_DIM = 64
SEQ = 577
STRIDE = 576
WINDOW = 592
LANES = 640
EPSILON = 1e-06
LOG_SCALE = 0.125
bf16 = jnp.bfloat16
f32 = jnp.float32
NN = (((1,), (0,)), ((), ()))
NT = (((1,), (1,)), ((), ()))
TN = (((0,), (0,)), ((), ()))
AXES = ("tensor", "dp")


def matmul(left, right, dims=NN):
    return lax.dot_general(left, right, dims, preferred_element_type=f32)


def norm_parts(values):
    center = values - jnp.mean(values, axis=-1, keepdims=True)
    second = jnp.mean(center * center, axis=-1, keepdims=True)
    inv = lax.rsqrt(second + EPSILON)
    return center * inv, inv


def gelu_and_slope(pre):
    phi = 0.5 + 0.5 * lax.erf(pre * 0.7071067811865476)
    bell = jnp.exp(pre * pre * -0.5)
    return pre * phi, phi + pre * (bell * 0.3989422804014327)


def full(shape):
    return pl.BlockSpec(shape, lambda *_: (0,) * len(shape), pipeline_mode=pl.Buffered(1))


def call(kernel, name, grid, in_specs, out_specs, out_shape, args, scratch=(), flops=0, prefetch=0, **params):
    moved = 0
    if flops:
        moved = sum(a.size * a.dtype.itemsize for a in args)
        moved += sum(math.prod(shape) * jnp.dtype(dtype).itemsize for shape, dtype in out_shape)
    return pl.pallas_call(
        kernel,
        grid_spec=pltpu.PrefetchScalarGridSpec(
            num_scalar_prefetch=prefetch,
            grid=grid,
            in_specs=in_specs,
            out_specs=out_specs,
            scratch_shapes=list(scratch),
        ),
        out_shape=[jax.ShapeDtypeStruct(shape, dtype) for shape, dtype in out_shape],
        compiler_params=pltpu.CompilerParams(vmem_limit_bytes=60 * 2**20, **params),
        cost_estimate=pl.CostEstimate(flops=2 * flops, bytes_accessed=moved, transcendentals=0),
        name=name,
    )(*args)


def before(ref, count):
    height = ref.shape[0]
    rows = pl.program_id(0) * height + lax.broadcasted_iota(jnp.int32, (height, 1), 0)
    return jnp.where(rows < count, ref[...].astype(f32), 0.0)


def qkv_kernel(part, count, x_ref, vec_ref, bias_ref, w_ref, normed_ref, triple_ref):
    hat, _ = norm_parts(before(x_ref, count))
    normed = (hat * vec_ref[0:1] + vec_ref[1:2]).astype(bf16)
    normed_ref[...] = normed
    tensor, dp = w_ref.shape[:2]
    width = w_ref.shape[3] // 3
    for s in range(3):
        for t in range(tensor):
            cols = slice(t * width, (t + 1) * width)
            w = w_ref[t, :, :part, s * width : (s + 1) * width].reshape(dp * part, width)
            out = matmul(normed, w)
            if s != 1:
                out = out + bias_ref[s // 2 : s // 2 + 1, cols]
            triple_ref[s, :, cols] = out.astype(bf16)


def window(image):
    start = pl.multiple_of(image * STRIDE, 16)
    return pl.ds(start, WINDOW)


def keep_before(image, ref, index, value):
    edge = pl.ds(pl.multiple_of(image * STRIDE, 16), 16)
    rest = pl.ds(pl.multiple_of(image * STRIDE + 16, 16), WINDOW - 16)
    rows = lax.broadcasted_iota(jnp.int32, (16, 1), 0)
    head = jnp.where(rows < image, ref[(*index[:-1], edge, index[-1])].astype(f32), value[:16])
    ref[(*index[:-1], edge, index[-1])] = head.astype(ref.dtype)
    ref[(*index[:-1], rest, index[-1])] = value[16:].astype(ref.dtype)


def two_heads(first, second):
    blank, below = jnp.zeros_like(first), jnp.zeros((LANES - WINDOW, 2 * HEAD_DIM), first.dtype)
    return jnp.concatenate(
        [
            jnp.concatenate([first, blank], axis=1), below,
            jnp.concatenate([blank, second], axis=1), below,
        ],
        axis=0,
    )


def head_columns(h):
    return (
        slice(HEAD_DIM * h, HEAD_DIM * (h + 2)),
        (slice(HEAD_DIM * h, HEAD_DIM * (h + 1)), slice(HEAD_DIM * (h + 1), HEAD_DIM * (h + 2))),
    )


def attend_kernel(triple_ref, context_ref, stat_ref):
    image = pl.program_id(1)
    lanes = lax.broadcasted_iota(jnp.int32, (1, LANES), 1)
    mask = jnp.where((lanes >= image) & (lanes < image + SEQ), 0.0, -1e30)
    own = window(image)
    left = lax.broadcasted_iota(jnp.int32, (1, 2 * HEAD_DIM), 1) < HEAD_DIM
    stats = []
    for h in range(0, triple_ref.shape[2] // HEAD_DIM, 2):
        pair, single = head_columns(h)
        keys = two_heads(*(triple_ref[1, own, cols] for cols in single))
        both = matmul(triple_ref[0, own, pair] * bf16(LOG_SCALE), keys, NT)
        probs, scale = [], []
        for u in range(2):
            scores = both[:, u * LANES : (u + 1) * LANES] + mask
            top = jnp.max(scores, axis=1, keepdims=True)
            expo = jnp.exp(scores - top)
            total = jnp.sum(expo, axis=1, keepdims=True)
            probs.append(expo.astype(bf16))
            scale.append(1.0 / total)
            stats.append(top + jnp.log(total))
        values = two_heads(*(triple_ref[2, own, cols] for cols in single))
        context = matmul(jnp.concatenate(probs, axis=1), values)
        keep_before(image, context_ref, (pair,), context * jnp.where(left, *scale))
    stat_ref[0] = jnp.concatenate(stats, axis=1).T


def attend_back_kernel(triple_ref, stat_ref, grad_ref, out_ref):
    image = pl.program_id(1)
    rows = lax.broadcasted_iota(jnp.int32, (WINDOW, 1), 0)
    mask = jnp.where((rows >= image) & (rows < image + SEQ), 0.0, -1e30)
    lanes = lax.broadcasted_iota(jnp.int32, (1, LANES), 1)
    real = (lanes >= image) & (lanes < image + SEQ)
    own = window(image)
    for h in range(0, triple_ref.shape[2] // HEAD_DIM, 2):
        pair, single = head_columns(h)
        keys = triple_ref[1, own, pair]
        queries = [triple_ref[0, own, cols] for cols in single]
        grads = [grad_ref[own, cols] for cols in single]
        both = matmul(keys, two_heads(*queries) * bf16(LOG_SCALE), NT)
        both_grad = matmul(triple_ref[2, own, pair], two_heads(*grads), NT)
        turned = keys.T
        value_grad, key_grad, query_grad = [], [], []
        for u in range(2):
            side = slice(u * LANES, (u + 1) * LANES)
            stat = jnp.concatenate(
                [stat_ref[0, h + u : h + u + 1, :], jnp.zeros((1, LANES - WINDOW), f32)], axis=1
            )
            probs = jnp.exp(both[:, side] + mask - jnp.where(real, stat, 1e30))
            grad_probs = both_grad[:, side]
            inner = jnp.sum(probs * grad_probs, axis=0, keepdims=True)
            grad_scores = (probs * (grad_probs - inner)).astype(bf16)
            out = matmul(
                jnp.concatenate([probs.astype(bf16), grad_scores], axis=1),
                two_heads(grads[u], queries[u]),
            )
            value_grad.append(out[:, :HEAD_DIM])
            key_grad.append(out[:, HEAD_DIM:])
            query_grad.append(matmul(turned[u * HEAD_DIM : (u + 1) * HEAD_DIM], grad_scores))
        keep_before(image, out_ref, (2, pair), jnp.concatenate(value_grad, axis=1))
        keep_before(image, out_ref, (1, pair), jnp.concatenate(key_grad, axis=1) * LOG_SCALE)
        query_grad = jnp.concatenate(query_grad, axis=0).T[:WINDOW]
        keep_before(image, out_ref, (0, pair), query_grad * LOG_SCALE)


def merge_kernel(count, live_ref, ctx_ref, x_ref, vec_ref, w_ref, given_ref, resid_ref, normed_ref, grad_ref):
    grad_ref[...] = before(given_ref, live_ref[0]).astype(bf16)
    tensor, dp, part, width = w_ref.shape
    total = before(x_ref, count) + vec_ref[2:3]
    for t in range(tensor):
        w = w_ref[t].reshape(dp * part, width)
        total = total + matmul(ctx_ref[:, t * width : (t + 1) * width], w, NT)
    resid_ref[...] = total
    hat, _ = norm_parts(total)
    normed_ref[...] = (hat * vec_ref[3:4] + vec_ref[4:5]).astype(bf16)


def expand_kernel(normed_ref, grad_ref, bias_ref, w_ref, act_ref, slope_ref, out_ref):
    _, dp, part, width = w_ref.shape
    w = w_ref[0].reshape(dp * part, width)
    active, slope = gelu_and_slope(matmul(normed_ref[...], w) + bias_ref[...])
    active = active.astype(bf16)
    act_ref[...] = active
    slope_ref[...] = slope.astype(bf16)
    out_ref[...] = matmul(grad_ref[...], active, TN).astype(bf16).reshape(out_ref.shape)


def accumulate(first, ref, value):
    @pl.when(first)
    def _():
        ref[...] = value

    @pl.when(jnp.logical_not(first))
    def _():
        ref[...] += value


def norm_back(values, gain, grad):
    hat, inv = norm_parts(values)
    scaled = grad * gain
    back = (
        scaled
        - jnp.mean(scaled, axis=-1, keepdims=True)
        - hat * jnp.mean(scaled * hat, axis=-1, keepdims=True)
    ) * inv
    return back, jnp.sum(grad * hat, axis=0, keepdims=True), jnp.sum(grad, axis=0, keepdims=True)


def mlp_back_kernel(
    chunk, grad_ref, slope_ref, resid_ref, vec_ref, e_ref, r_ref, m_ref,
    pre_ref, low_ref, ctx_ref, sums_ref, esum_ref,
):
    tensor, dp, rows, width = e_ref.shape
    first = pl.program_id(0) == 0
    grad = grad_ref[...]
    total = jnp.zeros(grad.shape, f32)
    parts = []
    for t in range(tensor):
        for c in range(width // chunk):
            local = slice(c * chunk, (c + 1) * chunk)
            cols = slice(t * width + c * chunk, t * width + (c + 1) * chunk)
            r = r_ref[t, :, :, local].reshape(dp * rows, chunk)
            pre = (matmul(grad, r) * slope_ref[:, cols].astype(f32)).astype(bf16)
            pre_ref[:, cols] = pre
            parts.append(jnp.sum(pre.astype(f32), axis=0, keepdims=True))
            e = e_ref[t, :, :, local].reshape(dp * rows, chunk)
            total = total + matmul(pre, e, NT)
    sums = 0
    half = grad.shape[0] // 2
    for rows_half in (slice(0, half), slice(half, 2 * half)):
        own = grad_ref[rows_half].astype(f32)
        back, gain_sum, shift_sum = norm_back(resid_ref[rows_half], vec_ref[3:4], total[rows_half])
        resid_grad = own + back
        low_ref[rows_half] = resid_grad.astype(bf16)
        lines = [jnp.sum(own, axis=0, keepdims=True), gain_sum, shift_sum]
        sums = sums + jnp.concatenate(lines + [jnp.sum(resid_grad, axis=0, keepdims=True)], axis=0)
    low = low_ref[...]
    wide = m_ref.shape[3]
    for t in range(tensor):
        m = m_ref[t].reshape(dp * rows, wide)
        ctx_ref[:, t * wide : (t + 1) * wide] = matmul(low, m).astype(bf16)
    accumulate(first, sums_ref, sums)
    parts = jnp.concatenate(parts, axis=1)
    lines = [parts[:, k * 128 : (k + 1) * 128] for k in range(esum_ref.shape[0])]
    accumulate(first, esum_ref, jnp.concatenate(lines, axis=0))


def qkv_back_kernel(part, count, depth, x_ref, low_ref, vec_ref, grad_ref, w_ref, *refs):
    reduce_ref, planes, refs = refs[0], refs[1 : depth + 1], refs[depth + 1 :]
    out_ref, sums_ref, bsum_ref, expand_out_ref, merge_out_ref, reduce_out_ref = refs

    @pl.when(pl.program_id(0) == 0)
    def _():
        total = planes[0][...].astype(f32)
        for ref in planes[1:]:
            total = total + ref[...].astype(f32)
        hidden = expand_out_ref.shape[1]
        expand_out_ref[...] = total[:, :hidden]
        merge_out_ref[...] = total[:, hidden:]
        reduce_out_ref[...] = reduce_ref[...].astype(f32)

    tensor, dp = w_ref.shape[:2]
    width = w_ref.shape[3] // 3
    first = pl.program_id(0) == 0
    total = jnp.zeros(x_ref.shape, f32)
    for s in range(3):
        for t in range(tensor):
            w = w_ref[t, :, :part, s * width : (s + 1) * width].reshape(dp * part, width)
            total = total + matmul(grad_ref[s, :, t * width : (t + 1) * width], w, NT)
    back, gain_sum, shift_sum = norm_back(before(x_ref, count), vec_ref[0:1], total)
    out_ref[...] = (low_ref[...].astype(f32) + back).astype(bf16)
    accumulate(first, sums_ref, jnp.concatenate([gain_sum, shift_sum], axis=0))
    bias = [jnp.sum(grad_ref[s].astype(f32), axis=0, keepdims=True) for s in (0, 2)]
    accumulate(first, bsum_ref, jnp.concatenate(bias, axis=0))


def flip(value, mask):
    unit = 1
    while unit <= mask:
        if mask & unit:
            value = value + unit - 2 * unit * lax.rem(lax.div(value, unit), 2)
        unit *= 2
    return value


def differ(left, right, size):
    total, unit = 0, 1
    while unit < size:
        p, q = lax.rem(lax.div(left, unit), 2), lax.rem(lax.div(right, unit), 2)
        total = total + unit * (p + q - 2 * p * q)
        unit *= 2
    return total


def slot_grad_kernel(tensor, dp, starts, *refs):
    count, steps, depth = len(starts) - 1, starts[-1], dp // 4
    lefts, rights, outs = refs[:count], refs[count : 2 * count], refs[2 * count : 2 * count + 2 * tensor]
    total, keep, send, landed, send_sem, recv_sem = refs[2 * count + 2 * tensor :]
    step, t = pl.program_id(0), pl.program_id(1)
    d, y = lax.axis_index("dp"), lax.axis_index("tensor")
    part, block = total.shape[0] // dp, total.shape[1]
    column = differ(t, y, tensor)
    slots = pl.ds(column * (2 * depth), 2 * depth)

    def copy(step):
        cols = pl.ds(pl.multiple_of(step * block, block), block)
        return pltpu.make_async_remote_copy(
            src_ref=send.at[slots, :, cols],
            dst_ref=landed.at[slots, :, cols],
            send_sem=send_sem.at[step * tensor + t],
            recv_sem=recv_sem.at[step * tensor + t],
            device_id=(flip(d, 1), y),
            device_id_type=pl.DeviceIdType.MESH,
        )

    @pl.when((step == 0) & (t == 0))
    def _():
        barrier = pltpu.get_barrier_semaphore()
        pl.semaphore_signal(
            barrier, inc=1, device_id=(flip(d, 1), y), device_id_type=pl.DeviceIdType.MESH
        )
        pl.semaphore_wait(barrier, 1)

    for j in range(count):
        @pl.when((step >= starts[j]) & (step < starts[j + 1]))
        def _():
            total[...] = matmul(lefts[j][...], rights[j][0], TN)

    @pl.when(step < steps)
    def _():
        cols = pl.ds(pl.multiple_of(step * block, block), block)
        for r in range(dp):
            owner = pl.multiple_of(flip(d, r) * part, part)
            half = send if r & 1 else keep
            slot = column * (2 * depth) + ((r >> 1) & 1) * depth + (r >> 2)
            half[slot, :, cols] = total[pl.ds(owner, part), :].astype(bf16)
        copy(step).start()

    @pl.when(step > 0)
    def _():
        copy(step - 1).wait()
        cols = pl.ds(pl.multiple_of((step - 1) * block, block), block)
        for k in range(2 * tensor):
            @pl.when(column == k // 2)
            def _():
                own = pl.ds(k * depth, depth)
                both = keep[own, :, cols].astype(f32) + landed[own, :, cols].astype(f32)
                outs[k][...] = both.astype(bf16)


def slot_grads(name, pairs, tensor, dp, block, collective_id):
    rows, deep = pairs[0][0].shape
    part, depth = deep // dp, dp // 4
    block = min([block] + [right.shape[2] // tensor for _, right in pairs])
    pers = [right.shape[2] // tensor // block for _, right in pairs]
    starts = [0]
    for (_, right), per in zip(pairs, pers):
        starts.append(starts[-1] + right.shape[0] * per)
    wide = starts[-1] * block
    half = tensor * dp // 2

    def right_map(j, i, t):
        t = jnp.where(i < starts[j], 0, jnp.where(i >= starts[j + 1], tensor - 1, t))
        i = jnp.clip(i - starts[j], 0, starts[j + 1] - starts[j] - 1)
        return (i // pers[j], 0, t * pers[j] + i % pers[j])

    spec = pl.BlockSpec((depth, part, block), lambda i, t: (0, 0, jnp.maximum(i - 1, 0)))
    return call(
        functools.partial(slot_grad_kernel, tensor, dp, starts),
        name,
        (starts[-1] + 1, tensor),
        [full((rows, deep))] * len(pairs)
        + [pl.BlockSpec((1, rows, block), functools.partial(right_map, j)) for j in range(len(pairs))],
        [spec] * (2 * tensor),
        [((depth, part, wide), bf16)] * (2 * tensor),
        [left for left, _ in pairs] + [right for _, right in pairs],
        [pltpu.VMEM((deep, block), f32)]
        + [pltpu.VMEM((half, part, wide), bf16)] * 3
        + [pltpu.SemaphoreType.DMA((starts[-1] * tensor,))] * 2,
        collective_id=collective_id,
        has_side_effects=True,
    )


def swap(values, d, t, tensor, dp):
    moves = []
    for p in range(dp):
        for q in range(tensor):
            moves.append((p * tensor + q, (p ^ d) * tensor + (q ^ t)))
    return lax.ppermute(values, ("dp", "tensor"), moves)


def send_plane(parts, tensor, dp):
    return [swap(parts[k], 2 * (k % 2), k // 2, tensor, dp) for k in range(1, 2 * tensor)]


def sum_plane(part, landed, dp):
    planes = []
    for z in range(dp // 4):
        total = part[z].astype(f32)
        for piece in landed:
            total = total + piece[z].astype(f32)
        planes.append(total.astype(bf16))
    return planes


def send_line(planes, tensor, dp):
    return [swap(planes[z], 4 * z, 0, tensor, dp) for z in range(1, dp // 4)]


def pack_kernel(
    heads_ref, merge_ref, expand_ref, hb_ref, eb_ref, *refs
):
    small, (first_ref, later_ref) = refs[:-2], refs[-2:]
    _, part, own = heads_ref.shape
    for s in range(3):
        first_ref[:part, s * own : (s + 1) * own] = heads_ref[s]
    lines = [ref[...].astype(f32) for ref in small] + [jnp.zeros((8 - len(small), part), f32)]
    hb = hb_ref[...].astype(f32)
    hb = hb.reshape(hb.shape[0] * hb.shape[1], hb.shape[2])
    eb = eb_ref[...].astype(f32)
    pieces = []
    for piece in (jnp.concatenate(lines, axis=0), eb, hb):
        height, width = piece.shape
        if height < 8:
            piece = jnp.concatenate([piece, jnp.zeros((8 - height, width), f32)], axis=0)
        pieces.append(piece)
    used = sum(piece.shape[1] for piece in pieces)
    pieces.append(jnp.zeros((8, 128 - used), f32))
    first_ref[part:, :128] = jnp.concatenate(pieces, axis=1).astype(bf16)
    first_ref[part:, 128:] = jnp.zeros((8, 3 * own - 128), bf16)
    hidden = expand_ref.shape[1]
    later_ref[:, :hidden] = expand_ref[...]
    later_ref[:, hidden:] = merge_ref[...]


def gather_kernel(in_ref, out_ref, own_sem, send_sem, recv_sem):
    d, y = lax.axis_index("dp"), lax.axis_index("tensor")
    z, x, c = lax.div(d, 4), lax.rem(lax.div(d, 2), 2), lax.rem(d, 2)
    far_x, far_y, far_c = 1 - x, 1 - y, 1 - c
    barrier = pltpu.get_barrier_semaphore()

    def index(place):
        pz, px, pc, py = place
        return (pz * 2 + px) * 2 + pc, py

    lower, upper = (z - 1, x, c, y), (z + 1, x, c, y)
    to_x, to_y, to_c = (z, far_x, c, y), (z, x, c, far_y), (z, x, far_c, y)

    def greet(peer):
        pl.semaphore_signal(barrier, inc=1, device_id=index(peer), device_id_type=pl.DeviceIdType.MESH)

    for peer in (to_x, to_y, to_c):
        greet(peer)
    pl.when(z > 0)(lambda: greet(lower))
    pl.when(z < 3)(lambda: greet(upper))
    pl.semaphore_wait(barrier, 4 + lax.rem(lax.div(z + 1, 2), 2))

    sent = []

    def copy(owner, peer, slot, source=None):
        p, q = index(owner)
        return pltpu.make_async_remote_copy(
            src_ref=out_ref.at[q, p] if source is None else source,
            dst_ref=out_ref.at[q, p],
            send_sem=send_sem.at[slot],
            recv_sem=recv_sem.at[p * 2 + q],
            device_id=index(peer),
            device_id_type=pl.DeviceIdType.MESH,
        )

    def send(owner, peer, there, source=None):
        slot = len(sent)
        sent.append((owner, peer, slot, there))

        @pl.when(there)
        def _():
            copy(owner, peer, slot, source).start()

    def arrive(owner, there):
        @pl.when(there)
        def _():
            copy(owner, to_c, 0).wait_recv()

    own = (z, x, c, y)
    keep = pltpu.make_async_copy(in_ref, out_ref.at[y, d], own_sem)
    send(own, upper, z < 3, in_ref)
    send(own, lower, z > 0, in_ref)
    for peer in (to_x, to_y, to_c):
        send(own, peer, z >= 0, in_ref)
    keep.start()
    for far in range(1, 4):
        for sign, after, onward in ((-1, upper, z < 3), (1, lower, z > 0)):
            level = z + sign * far
            there = (level >= 0) & (level <= 3)
            block = (level, x, c, y)
            arrive(block, there)
            send(block, after, there & onward)
            for peer in (to_x, to_y, to_c):
                send(block, peer, there)
    for far in range(4):
        for sign in (-1, 1) if far else (1,):
            level = z + sign * far
            there = (level >= 0) & (level <= 3)
            odd = lax.rem(level + 4, 2)
            block = (level, far_x, c, y)
            arrive(block, there)
            send(block, to_y, there & (odd == 0))
            send(block, to_c, there)
            block = (level, x, c, far_y)
            arrive(block, there)
            send(block, to_x, there & (odd == 1))
            send(block, to_c, there)
    for far in range(4):
        for sign in (-1, 1) if far else (1,):
            level = z + sign * far
            there = (level >= 0) & (level <= 3)
            block = (level, far_x, c, far_y)
            arrive(block, there)
            send(block, to_c, there)
    for level in range(4):
        for px in range(2):
            for py in range(2):
                arrive((level, px, far_c, py), z >= 0)
    for owner, peer, slot, there in sent:
        pl.when(there)(lambda: copy(owner, peer, slot).wait_send())
    keep.wait()


def gather_first(shard, tensor, dp):
    shape = (tensor, dp) + shard.shape
    if (tensor, dp) != (2, 16):
        return lax.all_gather(shard, AXES, axis=0, tiled=True).reshape(shape)
    return call(
        gather_kernel,
        "gather",
        (),
        [pl.BlockSpec(memory_space=pltpu.VMEM)],
        [pl.BlockSpec(memory_space=pl.ANY)],
        [(shape, bf16)],
        (shard,),
        [pltpu.SemaphoreType.DMA, pltpu.SemaphoreType.DMA((64,)), pltpu.SemaphoreType.DMA((32,))],
        collective_id=1,
        has_side_effects=True,
    )[0]


def last_kernel(dp, tensor, act_ref, resid_ref, vec_ref, w_ref, *refs):
    count, depth = dp * tensor, dp // 4
    own_ref, others, refs = refs[0], refs[1 : 2 * tensor], refs[2 * tensor :]
    one_ref, two_ref, hb_ref, eb_ref, out_ref, heads_ref, sums_ref = refs[:7]
    packed, landed, line, arrived, send_sem, recv_sem, line_send, line_recv = refs[7:]
    step = pl.program_id(0)
    d, y = lax.axis_index("dp"), lax.axis_index("tensor")
    me = d * tensor + y
    part = own_ref.shape[1]
    barrier = pltpu.get_barrier_semaphore()

    def place(k):
        other = lax.rem(me + k, count)
        return other, (lax.div(other, tensor), lax.rem(other, tensor))

    def greet(k, carry):
        _, where = place(k)
        pl.semaphore_signal(barrier, inc=1, device_id=where, device_id_type=pl.DeviceIdType.MESH)
        return carry

    def plane(z):
        total = own_ref[z].astype(f32)
        for ref in others:
            total = total + ref[z].astype(f32)
        return total

    @pl.when(step == 0)
    def _():
        lax.fori_loop(1, count, greet, 0)
        for z in range(1, depth):
            line[z - 1] = plane(z).astype(bf16)
        heads = hb_ref.shape[1] // HEAD_DIM
        own_heads, hb_wide = heads // tensor, HEAD_DIM // dp
        eb_tall, eb_wide = eb_ref.shape[0] // tensor, eb_ref.shape[1] // dp
        hb = [
            hb_ref[k : k + 1, h * HEAD_DIM : (h + 1) * HEAD_DIM] for k in range(2) for h in range(heads)
        ]
        hb = jnp.concatenate(hb, axis=0).T
        eb = eb_ref[...].T
        sums = jnp.concatenate([one_ref[...], two_ref[3:4], two_ref[1:3], two_ref[0:1]], axis=0)
        for p in range(dp):
            piece = sums[:, p * part : (p + 1) * part]
            for q in range(tensor):
                packed[p * tensor + q, 0:6, 0:part] = piece
                packed[p * tensor + q, 0:eb_wide, part : part + eb_tall] = eb[
                    p * eb_wide : (p + 1) * eb_wide, q * eb_tall : (q + 1) * eb_tall
                ]
                for k in range(2):
                    lane = part + eb_tall + k * own_heads
                    packed[p * tensor + q, 0:hb_wide, lane : lane + own_heads] = hb[
                        p * hb_wide : (p + 1) * hb_wide,
                        k * heads + q * own_heads : k * heads + (q + 1) * own_heads,
                    ]

    copies = [
        pltpu.make_async_remote_copy(
            src_ref=line.at[z - 1],
            dst_ref=arrived.at[z - 1],
            send_sem=line_send.at[z - 1],
            recv_sem=line_recv.at[z - 1],
            device_id=(flip(d, 4 * z), y),
            device_id_type=pl.DeviceIdType.MESH,
        )
        for z in range(1, depth)
    ]

    def copy(k):
        other, where = place(k)
        return pltpu.make_async_remote_copy(
            src_ref=packed.at[other],
            dst_ref=landed.at[k],
            send_sem=send_sem.at[k],
            recv_sem=recv_sem.at[k],
            device_id=where,
            device_id_type=pl.DeviceIdType.MESH,
        )

    def start(k, carry):
        copy(k).start()
        return carry

    @pl.when(step == 1)
    def _():
        pl.semaphore_wait(barrier, count - 1)
        lax.fori_loop(1, count, start, 0)
        for item in copies:
            item.start()

    total = resid_ref[...] + vec_ref[5:6]
    width = w_ref.shape[3]
    for t in range(tensor):
        w = w_ref[t].reshape(dp * part, width)
        total = total + matmul(act_ref[:, t * width : (t + 1) * width], w, NT)
    out_ref[...] = total.astype(bf16)

    def finish(k, sums):
        copy(k).wait()
        return sums + landed[k]

    @pl.when(step == pl.num_programs(0) - 1)
    def _():
        sums_ref[...] = lax.fori_loop(1, count, finish, packed[me])
        total = plane(0)
        for item, z in zip(copies, range(1, depth)):
            item.wait()
            total = total + arrived[z - 1].astype(f32)
        own = heads_ref.shape[2]
        for s in range(3):
            heads_ref[s] = total[:, s * own : (s + 1) * own]


def finish_kernel(sums_ref, heads_ref, out_ref, hb_ref, eb_ref, *vectors):
    out_ref[...] = heads_ref[...]
    part = vectors[0].shape[1]
    for r, ref in enumerate(vectors):
        ref[...] = sums_ref[r : r + 1, :part]
    wide, tall = eb_ref.shape
    eb_ref[...] = sums_ref[:wide, part : part + tall]
    wide, count = hb_ref.shape[1:]
    for k in range(2):
        lane = part + tall + k * count
        hb_ref[k] = sums_ref[:wide, lane : lane + count]


def shards(
    tensor,
    dp,
    activations,
    first_gain,
    first_shift,
    heads_weight,
    heads_bias,
    merge_weight,
    merge_bias,
    second_gain,
    second_shift,
    expand_weight,
    expand_bias,
    reduce_weight,
    reduce_bias,
    output_grad,
    real_images,
):
    rows, deep = activations.shape
    images = rows // SEQ
    part = deep // dp
    own = heads_weight.shape[2]
    hidden_own = expand_weight.shape[1]
    hidden = hidden_own * tensor
    heads = deep // HEAD_DIM
    least = (images - 1) * STRIDE + WINDOW
    blocks = -(-least // 512)
    block = -(-least // blocks // 16) * 16
    total_rows = block * blocks

    def gather(shard):
        out = lax.all_gather(shard, AXES, axis=0, tiled=True)
        return out.reshape(tensor, dp, *shard.shape)

    small = [first_gain, first_shift, merge_bias, second_gain, second_shift, reduce_bias]
    arrays = [
        heads_weight, merge_weight.T, expand_weight,
        heads_bias.transpose(0, 2, 1), expand_bias.T,
    ] + [v.reshape(1, part) for v in small]
    vmem = pl.BlockSpec(memory_space=pltpu.VMEM)
    first, later = call(
        pack_kernel, "pack", (), [vmem] * len(arrays), [vmem] * 2,
        [((part + 8, 3 * own), bf16), ((part, hidden_own + own), bf16)], arrays,
    )
    wide = gather(later)
    wide_heads = gather_first(first, tensor, dp)
    wide_heads, turned = lax.optimization_barrier((wide_heads, reduce_weight.T))
    wide_reduce = gather(turned)

    hbs, ebs = heads_bias.shape, expand_bias.shape
    small = wide_heads[:, :, part:, :128].astype(f32)
    vectors = small[0, :, :6, :part].transpose(1, 0, 2).reshape(6, deep)
    eb = small[:, :, : ebs[1], part : part + ebs[0]].transpose(0, 3, 1, 2).reshape(1, hidden)
    hb = small[:, :, : 2 * hbs[2], part + ebs[0] : part + ebs[0] + hbs[1]]
    hb = hb.reshape(tensor, dp, 2, hbs[2], hbs[1]).transpose(2, 0, 4, 1, 3).reshape(2, deep)
    live = jnp.clip(real_images - lax.axis_index("tensor") * images, 0, images) * SEQ

    def by_rows(width):
        return pl.BlockSpec((block, width), lambda i, *_: (i, 0))

    def columns(array, index, width):
        shape = array.shape[:3] + (width,)
        return pl.BlockSpec(shape, lambda *_: (0, 0, 0, index), pipeline_mode=pl.Buffered(1))

    vec = full((6, deep))
    expand_spec, merge_spec = columns(wide, 0, hidden_own), columns(wide, hidden_own // own, own)
    triple_spec = pl.BlockSpec((3, block, deep), lambda i: (0, i, 0))
    normed_one, triple = call(
        functools.partial(qkv_kernel, part, rows),
        "qkv",
        (blocks,),
        [by_rows(deep), vec, full((2, deep)), full(wide_heads.shape)],
        [by_rows(deep), triple_spec],
        [((total_rows, deep), bf16), ((3, total_rows, deep), bf16)],
        (activations, vectors, hb, wide_heads),
        flops=total_rows * deep * deep * 3,
    )

    group = 4
    groups = heads // group
    panel = group * HEAD_DIM
    head_spec = pl.BlockSpec((3, total_rows, panel), lambda g, i: (0, 0, g))
    ctx_spec = pl.BlockSpec((total_rows, panel), lambda g, i: (0, g))
    stat_spec = pl.BlockSpec((1, group, WINDOW), lambda g, i: (g * images + i, 0, 0))
    attend_flops = images * heads * WINDOW * 768 * 256 * 2
    context, stat = call(
        attend_kernel,
        "attend",
        (groups, images),
        [head_spec],
        [ctx_spec, stat_spec],
        [((total_rows, deep), bf16), ((images * groups, group, WINDOW), f32)],
        (triple,),
        flops=attend_flops,
    )

    resid, normed_two, grad = call(
        functools.partial(merge_kernel, rows),
        "merge",
        (blocks,),
        [by_rows(deep), by_rows(deep), vec, merge_spec, by_rows(deep)],
        [by_rows(deep), by_rows(deep), by_rows(deep)],
        [((total_rows, deep), f32), ((total_rows, deep), bf16), ((total_rows, deep), bf16)],
        (live, context, activations, vectors, wide, output_grad),
        flops=total_rows * deep * deep,
        prefetch=1,
    )

    chunk = min(512, hidden_own)
    per = hidden_own // chunk
    chunk_spec = pl.BlockSpec((total_rows, chunk), lambda c: (0, c))
    shard_spec = pl.BlockSpec((1, dp, part, chunk), lambda c: (c // per, 0, 0, c % per))
    active, slope, grad_reduce = call(
        expand_kernel,
        "expand",
        (hidden // chunk,),
        [
            full((total_rows, deep)), full((total_rows, deep)),
            pl.BlockSpec((1, chunk), lambda c: (0, c)), shard_spec,
        ],
        [chunk_spec, chunk_spec, shard_spec],
        [
            ((total_rows, hidden), bf16), ((total_rows, hidden), bf16),
            ((tensor, dp, part, hidden_own), bf16),
        ],
        (normed_two, grad, eb, wide),
        flops=total_rows * deep * hidden * 2,
    )
    grad_reduce = grad_reduce.reshape(tensor * dp * part, hidden_own)
    grad_reduce = lax.psum_scatter(grad_reduce, AXES, scatter_dimension=0, tiled=True)

    back_chunk = min(512, hidden_own)
    pre_grad, resid_low, grad_context, sums_two, esum = call(
        functools.partial(mlp_back_kernel, back_chunk),
        "mlp_back",
        (blocks,),
        [
            by_rows(deep), by_rows(hidden), by_rows(deep), vec,
            expand_spec, full(wide_reduce.shape), merge_spec,
        ],
        [
            by_rows(hidden), by_rows(deep), by_rows(deep),
            pl.BlockSpec((4, deep), lambda i: (0, 0)), pl.BlockSpec((hidden // 128, 128), lambda i: (0, 0)),
        ],
        [
            ((total_rows, hidden), bf16), ((total_rows, deep), bf16), ((total_rows, deep), bf16),
            ((4, deep), f32), ((hidden // 128, 128), f32),
        ],
        (grad, slope, resid, vectors, wide, wide_reduce, wide),
    )
    parts = slot_grads(
        "middle_grad", [(normed_two, pre_grad[None]), (resid_low, context[None])], tensor, dp, 512, 2
    )
    *parts, grad_context = lax.optimization_barrier((*parts, grad_context))
    landed = send_plane(parts, tensor, dp)
    grad_triple = call(
        attend_back_kernel,
        "attend_back",
        (groups, images),
        [head_spec, stat_spec, ctx_spec],
        [head_spec],
        [((3, total_rows, deep), bf16)],
        (triple, stat, grad_context),
    )[0]
    *landed, part_own, grad_triple = lax.optimization_barrier((*landed, parts[0], grad_triple))
    planes = sum_plane(part_own, landed, dp)
    *planes, grad_triple = lax.optimization_barrier((*planes, grad_triple))
    landed = send_line(planes, tensor, dp)
    parts = slot_grads("heads_grad", [(normed_one, grad_triple)], tensor, dp, 512, 3)
    held = (tuple(parts), tuple(landed), planes[0], resid_low)
    parts, landed, plane_own, resid_low = lax.optimization_barrier(held)
    last = send_plane(parts, tensor, dp)
    def whole(shape):
        return pl.BlockSpec(shape, lambda *_: (0,) * len(shape))

    shapes = [(2, deep), (2, deep), (part, hidden_own), (part, own), (part, hidden_own)]
    input_grad, sums_one, bsum, grad_expand, grad_merge, grad_reduce = call(
        functools.partial(qkv_back_kernel, part, rows, dp // 4),
        "qkv_back",
        (blocks,),
        [by_rows(deep), by_rows(deep), vec, triple_spec, full(wide_heads.shape), full(grad_reduce.shape)]
        + [full(plane_own.shape)] * (dp // 4),
        [by_rows(deep)] + [whole(shape) for shape in shapes],
        [((rows, deep), bf16)] + [(shape, f32) for shape in shapes],
        (activations, resid_low, vectors, grad_triple, wide_heads, grad_reduce, plane_own, *landed),
        flops=total_rows * deep * deep * 3,
    )

    hbs, ebs = heads_bias.shape, expand_bias.shape
    depth = dp // 4
    arrays = [parts[0], *last, sums_one, sums_two, bsum, esum]
    output, heads_sum, sums = call(
        functools.partial(last_kernel, dp, tensor),
        "reduce",
        (blocks,),
        [by_rows(hidden), by_rows(deep), vec, full(wide_reduce.shape)] + [full(v.shape) for v in arrays],
        [by_rows(deep), whole((3, part, own)), whole((8, 128))],
        [((rows, deep), bf16), ((3, part, own), f32), ((8, 128), f32)],
        (active, resid, vectors, wide_reduce, *arrays),
        [
            pltpu.VMEM((tensor * dp, 8, 128), f32), pltpu.VMEM((tensor * dp, 8, 128), f32),
            pltpu.VMEM((depth - 1, part, 3 * own), bf16), pltpu.VMEM((depth - 1, part, 3 * own), bf16),
            pltpu.SemaphoreType.DMA((tensor * dp,)), pltpu.SemaphoreType.DMA((tensor * dp,)),
            pltpu.SemaphoreType.DMA((depth - 1,)), pltpu.SemaphoreType.DMA((depth - 1,)),
        ],
        flops=total_rows * deep * hidden,
        collective_id=0,
        has_side_effects=True,
    )
    grad_heads, hb_grad, eb_grad, *vector = call(
        finish_kernel, "finish", (), [vmem] * 2, [vmem] * 9,
        [(heads_sum.shape, f32), ((2, hbs[2], hbs[1]), f32), (ebs[::-1], f32)] + [((1, part), f32)] * 6,
        (sums, heads_sum),
    )
    vector = [v.reshape(part) for v in vector]

    return (
        output,
        input_grad,
        vector[0],
        vector[1],
        grad_heads,
        hb_grad.transpose(0, 2, 1),
        grad_merge.T,
        vector[2],
        vector[3],
        vector[4],
        grad_expand,
        eb_grad.T,
        grad_reduce.T,
        vector[5],
    )


def solution(mesh):
    rows = P(("dp", "tensor"), None)
    specs = (
        P("dp"),
        P("dp"),
        P(None, "dp", "tensor"),
        P(None, "tensor", "dp"),
        P("tensor", "dp"),
        P("dp"),
        P("dp"),
        P("dp"),
        P("dp", "tensor"),
        P("tensor", "dp"),
        P("tensor", "dp"),
        P("dp"),
    )
    return jax.shard_map(
        functools.partial(shards, mesh.shape["tensor"], mesh.shape["dp"]),
        mesh=mesh,
        in_specs=(rows,) + specs + (rows, P("dp")),
        out_specs=(rows, rows) + specs,
        check_vma=False,
    )
```

```python
import functools
import math

import jax
import jax.numpy as jnp
from jax import lax
from jax.experimental import pallas as pl
from jax.experimental.pallas import tpu as pltpu
from jax.sharding import PartitionSpec as P

HEAD_DIM = 64
SEQ = 577
STRIDE = 576
WINDOW = 592
LANES = 640
EPSILON = 1e-06
LOG_SCALE = 0.125
bf16 = jnp.bfloat16
f32 = jnp.float32
NN = (((1,), (0,)), ((), ()))
NT = (((1,), (1,)), ((), ()))
TN = (((0,), (0,)), ((), ()))
AXES = ("tensor", "dp")


def matmul(left, right, dims=NN):
    return lax.dot_general(left, right, dims, preferred_element_type=f32)


def norm_parts(values):
    center = values - jnp.mean(values, axis=-1, keepdims=True)
    second = jnp.mean(center * center, axis=-1, keepdims=True)
    inv = lax.rsqrt(second + EPSILON)
    return center * inv, inv


def gelu_and_slope(pre):
    phi = 0.5 + 0.5 * lax.erf(pre * 0.7071067811865476)
    bell = jnp.exp(pre * pre * -0.5)
    return pre * phi, phi + pre * (bell * 0.3989422804014327)


def full(shape):
    return pl.BlockSpec(shape, lambda *_: (0,) * len(shape), pipeline_mode=pl.Buffered(1))


def call(kernel, name, grid, in_specs, out_specs, out_shape, args, scratch=(), flops=0, prefetch=0, **params):
    moved = 0
    if flops:
        moved = sum(a.size * a.dtype.itemsize for a in args)
        moved += sum(math.prod(shape) * jnp.dtype(dtype).itemsize for shape, dtype in out_shape)
    return pl.pallas_call(
        kernel,
        grid_spec=pltpu.PrefetchScalarGridSpec(
            num_scalar_prefetch=prefetch,
            grid=grid,
            in_specs=in_specs,
            out_specs=out_specs,
            scratch_shapes=list(scratch),
        ),
        out_shape=[jax.ShapeDtypeStruct(shape, dtype) for shape, dtype in out_shape],
        compiler_params=pltpu.CompilerParams(vmem_limit_bytes=60 * 2**20, **params),
        cost_estimate=pl.CostEstimate(flops=2 * flops, bytes_accessed=moved, transcendentals=0),
        name=name,
    )(*args)


def before(ref, count):
    height = ref.shape[0]
    rows = pl.program_id(0) * height + lax.broadcasted_iota(jnp.int32, (height, 1), 0)
    return jnp.where(rows < count, ref[...].astype(f32), 0.0)


def qkv_kernel(part, count, x_ref, vec_ref, bias_ref, w_ref, normed_ref, triple_ref):
    hat, _ = norm_parts(before(x_ref, count))
    normed = (hat * vec_ref[0:1] + vec_ref[1:2]).astype(bf16)
    normed_ref[...] = normed
    tensor, dp = w_ref.shape[:2]
    width = w_ref.shape[3] // 3
    for s in range(3):
        for t in range(tensor):
            cols = slice(t * width, (t + 1) * width)
            w = w_ref[t, :, :part, s * width : (s + 1) * width].reshape(dp * part, width)
            out = matmul(normed, w)
            if s != 1:
                out = out + bias_ref[s // 2 : s // 2 + 1, cols]
            triple_ref[s, :, cols] = out.astype(bf16)


def window(image):
    start = pl.multiple_of(image * STRIDE, 16)
    return pl.ds(start, WINDOW)


def keep_before(image, ref, index, value):
    edge = pl.ds(pl.multiple_of(image * STRIDE, 16), 16)
    rest = pl.ds(pl.multiple_of(image * STRIDE + 16, 16), WINDOW - 16)
    rows = lax.broadcasted_iota(jnp.int32, (16, 1), 0)
    head = jnp.where(rows < image, ref[(*index[:-1], edge, index[-1])].astype(f32), value[:16])
    ref[(*index[:-1], edge, index[-1])] = head.astype(ref.dtype)
    ref[(*index[:-1], rest, index[-1])] = value[16:].astype(ref.dtype)


def two_heads(first, second):
    blank, below = jnp.zeros_like(first), jnp.zeros((LANES - WINDOW, 2 * HEAD_DIM), first.dtype)
    return jnp.concatenate(
        [
            jnp.concatenate([first, blank], axis=1), below,
            jnp.concatenate([blank, second], axis=1), below,
        ],
        axis=0,
    )


def head_columns(h):
    return (
        slice(HEAD_DIM * h, HEAD_DIM * (h + 2)),
        (slice(HEAD_DIM * h, HEAD_DIM * (h + 1)), slice(HEAD_DIM * (h + 1), HEAD_DIM * (h + 2))),
    )


def attend_kernel(triple_ref, context_ref, stat_ref):
    image = pl.program_id(1)
    lanes = lax.broadcasted_iota(jnp.int32, (1, LANES), 1)
    mask = jnp.where((lanes >= image) & (lanes < image + SEQ), 0.0, -1e30)
    own = window(image)
    left = lax.broadcasted_iota(jnp.int32, (1, 2 * HEAD_DIM), 1) < HEAD_DIM
    stats = []
    for h in range(0, triple_ref.shape[2] // HEAD_DIM, 2):
        pair, single = head_columns(h)
        keys = two_heads(*(triple_ref[1, own, cols] for cols in single))
        both = matmul(triple_ref[0, own, pair] * bf16(LOG_SCALE), keys, NT)
        probs, scale = [], []
        for u in range(2):
            scores = both[:, u * LANES : (u + 1) * LANES] + mask
            top = jnp.max(scores, axis=1, keepdims=True)
            expo = jnp.exp(scores - top)
            total = jnp.sum(expo, axis=1, keepdims=True)
            probs.append(expo.astype(bf16))
            scale.append(1.0 / total)
            stats.append(top + jnp.log(total))
        values = two_heads(*(triple_ref[2, own, cols] for cols in single))
        context = matmul(jnp.concatenate(probs, axis=1), values)
        keep_before(image, context_ref, (pair,), context * jnp.where(left, *scale))
    stat_ref[0] = jnp.concatenate(stats, axis=1).T


def attend_back_kernel(tensor, triple_ref, stat_ref, grad_ref, *refs):
    peers = 2 * tensor - 1
    parts, (out_ref, planes_ref, landed, send_sem, recv_sem) = refs[: peers + 1], refs[peers + 1 :]
    image = pl.program_id(1)
    step = pl.program_id(0) * pl.num_programs(1) + image
    d, y = lax.axis_index("dp"), lax.axis_index("tensor")
    barrier = pltpu.get_barrier_semaphore()
    mesh = pl.DeviceIdType.MESH
    places = [(flip(d, 2 * (k % 2)), flip(y, k // 2)) for k in range(1, peers + 1)]

    @pl.when(step == 0)
    def _():
        for where in places:
            pl.semaphore_signal(barrier, inc=1, device_id=where, device_id_type=mesh)

    copies = [
        pltpu.make_async_remote_copy(
            src_ref=parts[k + 1], dst_ref=landed.at[k], send_sem=send_sem.at[k],
            recv_sem=recv_sem.at[k], device_id=where, device_id_type=mesh,
        )
        for k, where in enumerate(places)
    ]

    @pl.when(step == 1)
    def _():
        pl.semaphore_wait(barrier, peers)
        for item in copies:
            item.start()

    rows = lax.broadcasted_iota(jnp.int32, (WINDOW, 1), 0)
    mask = jnp.where((rows >= image) & (rows < image + SEQ), 0.0, -1e30)
    lanes = lax.broadcasted_iota(jnp.int32, (1, LANES), 1)
    real = (lanes >= image) & (lanes < image + SEQ)
    own = window(image)
    for h in range(0, triple_ref.shape[2] // HEAD_DIM, 2):
        pair, single = head_columns(h)
        keys = triple_ref[1, own, pair]
        queries = [triple_ref[0, own, cols] for cols in single]
        grads = [grad_ref[own, cols] for cols in single]
        both = matmul(keys, two_heads(*queries) * bf16(LOG_SCALE), NT)
        both_grad = matmul(triple_ref[2, own, pair], two_heads(*grads), NT)
        turned = keys.T
        value_grad, key_grad, query_grad = [], [], []
        for u in range(2):
            side = slice(u * LANES, (u + 1) * LANES)
            stat = jnp.concatenate(
                [stat_ref[0, h + u : h + u + 1, :], jnp.zeros((1, LANES - WINDOW), f32)], axis=1
            )
            probs = jnp.exp(both[:, side] + mask - jnp.where(real, stat, 1e30))
            grad_probs = both_grad[:, side]
            inner = jnp.sum(probs * grad_probs, axis=0, keepdims=True)
            grad_scores = (probs * (grad_probs - inner)).astype(bf16)
            out = matmul(
                jnp.concatenate([probs.astype(bf16), grad_scores], axis=1),
                two_heads(grads[u], queries[u]),
            )
            value_grad.append(out[:, :HEAD_DIM])
            key_grad.append(out[:, HEAD_DIM:])
            query_grad.append(matmul(turned[u * HEAD_DIM : (u + 1) * HEAD_DIM], grad_scores))
        keep_before(image, out_ref, (2, pair), jnp.concatenate(value_grad, axis=1))
        keep_before(image, out_ref, (1, pair), jnp.concatenate(key_grad, axis=1) * LOG_SCALE)
        query_grad = jnp.concatenate(query_grad, axis=0).T[:WINDOW]
        keep_before(image, out_ref, (0, pair), query_grad * LOG_SCALE)

    @pl.when(step == pl.num_programs(0) * pl.num_programs(1) - 1)
    def _():
        for item in copies:
            item.wait()
        for z in range(planes_ref.shape[0]):
            total = parts[0][z].astype(f32)
            for k in range(peers):
                total = total + landed[k, z].astype(f32)
            planes_ref[z] = total.astype(bf16)


def merge_kernel(count, ctx_ref, x_ref, vec_ref, w_ref, resid_ref, normed_ref):
    tensor, dp, part, width = w_ref.shape
    total = before(x_ref, count) + vec_ref[2:3]
    for t in range(tensor):
        w = w_ref[t].reshape(dp * part, width)
        total = total + matmul(ctx_ref[:, t * width : (t + 1) * width], w, NT)
    resid_ref[...] = total
    hat, _ = norm_parts(total)
    normed_ref[...] = (hat * vec_ref[3:4] + vec_ref[4:5]).astype(bf16)


def expand_kernel(live_ref, normed_ref, given_ref, bias_ref, w_ref, act_ref, slope_ref, out_ref, grad_ref):
    @pl.when(pl.program_id(0) == 0)
    def _():
        count = given_ref.shape[0]
        even = count // 16 * 16
        rows = lax.broadcasted_iota(jnp.int32, (count, 1), 0)
        grad_ref[:even] = jnp.where(rows[:even] < live_ref[0], given_ref[:even], bf16(0))
        grad_ref[even:] = jnp.zeros((grad_ref.shape[0] - even, grad_ref.shape[1]), bf16)
        rest = jnp.where(rows[even:] < live_ref[0], given_ref[even:].astype(f32), 0.0)
        grad_ref[even:count] = rest.astype(bf16)

    _, dp, part, width = w_ref.shape
    w = w_ref[0].reshape(dp * part, width)
    active, slope = gelu_and_slope(matmul(normed_ref[...], w) + bias_ref[...])
    active = active.astype(bf16)
    act_ref[...] = active
    slope_ref[...] = slope.astype(bf16)
    out_ref[...] = matmul(grad_ref[...], active, TN).astype(bf16).reshape(out_ref.shape)


def accumulate(first, ref, value):
    @pl.when(first)
    def _():
        ref[...] = value

    @pl.when(jnp.logical_not(first))
    def _():
        ref[...] += value


def norm_back(values, gain, grad):
    hat, inv = norm_parts(values)
    scaled = grad * gain
    back = (
        scaled
        - jnp.mean(scaled, axis=-1, keepdims=True)
        - hat * jnp.mean(scaled * hat, axis=-1, keepdims=True)
    ) * inv
    return back, jnp.sum(grad * hat, axis=0, keepdims=True), jnp.sum(grad, axis=0, keepdims=True)


def mlp_back_kernel(
    chunk, live_ref, given_ref, slope_ref, resid_ref, vec_ref, e_ref, r_ref, m_ref,
    pre_ref, low_ref, ctx_ref, sums_ref, esum_ref,
):
    tensor, dp, rows, width = e_ref.shape
    first = pl.program_id(0) == 0
    given = before(given_ref, live_ref[0])
    grad = given.astype(bf16)
    total = jnp.zeros(grad.shape, f32)
    parts = []
    for t in range(tensor):
        for c in range(width // chunk):
            local = slice(c * chunk, (c + 1) * chunk)
            cols = slice(t * width + c * chunk, t * width + (c + 1) * chunk)
            r = r_ref[t, :, :, local].reshape(dp * rows, chunk)
            pre = (matmul(grad, r) * slope_ref[:, cols].astype(f32)).astype(bf16)
            pre_ref[:, cols] = pre
            parts.append(jnp.sum(pre.astype(f32), axis=0, keepdims=True))
            e = e_ref[t, :, :, local].reshape(dp * rows, chunk)
            total = total + matmul(pre, e, NT)
    sums = 0
    half = grad.shape[0] // 2
    for rows_half in (slice(0, half), slice(half, 2 * half)):
        own = given[rows_half]
        back, gain_sum, shift_sum = norm_back(resid_ref[rows_half], vec_ref[3:4], total[rows_half])
        resid_grad = own + back
        low_ref[rows_half] = resid_grad.astype(bf16)
        lines = [jnp.sum(own, axis=0, keepdims=True), gain_sum, shift_sum]
        sums = sums + jnp.concatenate(lines + [jnp.sum(resid_grad, axis=0, keepdims=True)], axis=0)
    low = low_ref[...]
    wide = m_ref.shape[3]
    for t in range(tensor):
        m = m_ref[t].reshape(dp * rows, wide)
        ctx_ref[:, t * wide : (t + 1) * wide] = matmul(low, m).astype(bf16)
    accumulate(first, sums_ref, sums)
    parts = jnp.concatenate(parts, axis=1)
    lines = [parts[:, k * 128 : (k + 1) * 128] for k in range(esum_ref.shape[0])]
    accumulate(first, esum_ref, jnp.concatenate(lines, axis=0))


def qkv_back_kernel(part, count, x_ref, low_ref, vec_ref, grad_ref, w_ref, *refs):
    reduce_ref, middle_ref, out_ref, sums_ref, bsum_ref, expand_out_ref, merge_out_ref, reduce_out_ref = refs

    @pl.when(pl.program_id(0) == 0)
    def _():
        hidden = expand_out_ref.shape[1]
        expand_out_ref[...] = middle_ref[:, :hidden]
        merge_out_ref[...] = middle_ref[:, hidden:]
        reduce_out_ref[...] = reduce_ref[...].astype(f32)

    tensor, dp = w_ref.shape[:2]
    width = w_ref.shape[3] // 3
    first = pl.program_id(0) == 0
    total = jnp.zeros(x_ref.shape, f32)
    for s in range(3):
        for t in range(tensor):
            w = w_ref[t, :, :part, s * width : (s + 1) * width].reshape(dp * part, width)
            total = total + matmul(grad_ref[s, :, t * width : (t + 1) * width], w, NT)
    back, gain_sum, shift_sum = norm_back(before(x_ref, count), vec_ref[0:1], total)
    out_ref[...] = (low_ref[...].astype(f32) + back).astype(bf16)
    accumulate(first, sums_ref, jnp.concatenate([gain_sum, shift_sum], axis=0))
    bias = [jnp.sum(grad_ref[s].astype(f32), axis=0, keepdims=True) for s in (0, 2)]
    accumulate(first, bsum_ref, jnp.concatenate(bias, axis=0))


def flip(value, mask):
    unit = 1
    while unit <= mask:
        if mask & unit:
            value = value + unit - 2 * unit * lax.rem(lax.div(value, unit), 2)
        unit *= 2
    return value


def differ(left, right, size):
    total, unit = 0, 1
    while unit < size:
        p, q = lax.rem(lax.div(left, unit), 2), lax.rem(lax.div(right, unit), 2)
        total = total + unit * (p + q - 2 * p * q)
        unit *= 2
    return total


def slot_grad_kernel(tensor, dp, starts, carried, *refs):
    count, steps, depth = len(starts) - 1, starts[-1], dp // 4
    lefts, rights, refs = refs[:count], refs[count : 2 * count], refs[2 * count :]
    if carried:
        line_ref, *refs, arrived, line_send, line_recv = refs
        sum_ref, refs = refs[0], refs[1:]
    outs = refs[: 2 * tensor]
    total, keep, send, landed, send_sem, recv_sem = refs[2 * tensor :]
    step, t = pl.program_id(0), pl.program_id(1)
    d, y = lax.axis_index("dp"), lax.axis_index("tensor")
    part, block = total.shape[0] // dp, total.shape[1]
    column = differ(t, y, tensor)
    slots = pl.ds(column * (2 * depth), 2 * depth)

    def copy(step):
        cols = pl.ds(pl.multiple_of(step * block, block), block)
        return pltpu.make_async_remote_copy(
            src_ref=send.at[slots, :, cols],
            dst_ref=landed.at[slots, :, cols],
            send_sem=send_sem.at[step * tensor + t],
            recv_sem=recv_sem.at[step * tensor + t],
            device_id=(flip(d, 1), y),
            device_id_type=pl.DeviceIdType.MESH,
        )

    def line(z):
        return pltpu.make_async_remote_copy(
            src_ref=line_ref.at[z],
            dst_ref=arrived.at[z - 1],
            send_sem=line_send.at[z - 1],
            recv_sem=line_recv.at[z - 1],
            device_id=(flip(d, 4 * z), y),
            device_id_type=pl.DeviceIdType.MESH,
        )

    @pl.when((step == 0) & (t == 0))
    def _():
        barrier = pltpu.get_barrier_semaphore()
        masks = [1] + ([4 * z for z in range(1, depth)] if carried else [])
        for mask in masks:
            pl.semaphore_signal(
                barrier, inc=1, device_id=(flip(d, mask), y), device_id_type=pl.DeviceIdType.MESH
            )
        pl.semaphore_wait(barrier, len(masks))
        for z in range(1, depth) if carried else ():
            line(z).start()

    for j in range(count):
        @pl.when((step >= starts[j]) & (step < starts[j + 1]))
        def _():
            total[...] = matmul(lefts[j][...], rights[j][0], TN)

    @pl.when(step < steps)
    def _():
        cols = pl.ds(pl.multiple_of(step * block, block), block)
        for r in range(dp):
            owner = pl.multiple_of(flip(d, r) * part, part)
            half = send if r & 1 else keep
            slot = column * (2 * depth) + ((r >> 1) & 1) * depth + (r >> 2)
            half[slot, :, cols] = total[pl.ds(owner, part), :].astype(bf16)
        copy(step).start()

    @pl.when(step > 0)
    def _():
        copy(step - 1).wait()
        cols = pl.ds(pl.multiple_of((step - 1) * block, block), block)
        for k in range(2 * tensor):
            @pl.when(column == k // 2)
            def _():
                own = pl.ds(k * depth, depth)
                both = keep[own, :, cols].astype(f32) + landed[own, :, cols].astype(f32)
                outs[k][...] = both.astype(bf16)

    if carried:
        @pl.when((step == steps) & (t == tensor - 1))
        def _():
            whole = line_ref[0].astype(f32)
            for z in range(1, depth):
                line(z).wait()
                whole = whole + arrived[z - 1].astype(f32)
            sum_ref[...] = whole


def slot_grads(name, pairs, tensor, dp, block, collective_id, carried=()):
    rows, deep = pairs[0][0].shape
    part, depth = deep // dp, dp // 4
    block = min([block] + [right.shape[2] // tensor for _, right in pairs])
    pers = [right.shape[2] // tensor // block for _, right in pairs]
    starts = [0]
    for (_, right), per in zip(pairs, pers):
        starts.append(starts[-1] + right.shape[0] * per)
    wide = starts[-1] * block
    half = tensor * dp // 2

    def right_map(j, i, t):
        t = jnp.where(i < starts[j], 0, jnp.where(i >= starts[j + 1], tensor - 1, t))
        i = jnp.clip(i - starts[j], 0, starts[j + 1] - starts[j] - 1)
        return (i // pers[j], 0, t * pers[j] + i % pers[j])

    spec = pl.BlockSpec((depth, part, block), lambda i, t: (0, 0, jnp.maximum(i - 1, 0)))
    return call(
        functools.partial(slot_grad_kernel, tensor, dp, starts, bool(carried)),
        name,
        (starts[-1] + 1, tensor),
        [full((rows, deep))] * len(pairs)
        + [pl.BlockSpec((1, rows, block), functools.partial(right_map, j)) for j in range(len(pairs))]
        + [full(v.shape) for v in carried],
        [pl.BlockSpec(v.shape[1:], lambda i, t: (0, 0)) for v in carried] + [spec] * (2 * tensor),
        [(v.shape[1:], f32) for v in carried] + [((depth, part, wide), bf16)] * (2 * tensor),
        [left for left, _ in pairs] + [right for _, right in pairs] + list(carried),
        [pltpu.VMEM((deep, block), f32)]
        + [pltpu.VMEM((half, part, wide), bf16)] * 3
        + [pltpu.SemaphoreType.DMA((starts[-1] * tensor,))] * 2
        + [pltpu.VMEM((depth - 1,) + v.shape[1:], bf16) for v in carried]
        + [pltpu.SemaphoreType.DMA((depth - 1,))] * (2 * len(carried)),
        collective_id=collective_id,
        has_side_effects=True,
    )


def swap(values, d, t, tensor, dp):
    moves = []
    for p in range(dp):
        for q in range(tensor):
            moves.append((p * tensor + q, (p ^ d) * tensor + (q ^ t)))
    return lax.ppermute(values, ("dp", "tensor"), moves)


def send_plane(parts, tensor, dp):
    return [swap(parts[k], 2 * (k % 2), k // 2, tensor, dp) for k in range(1, 2 * tensor)]


def pack_kernel(
    heads_ref, merge_ref, expand_ref, hb_ref, eb_ref, *refs
):
    small, (first_ref, later_ref) = refs[:-2], refs[-2:]
    _, part, own = heads_ref.shape
    for s in range(3):
        first_ref[:part, s * own : (s + 1) * own] = heads_ref[s]
    lines = [ref[...].astype(f32) for ref in small] + [jnp.zeros((8 - len(small), part), f32)]
    hb = hb_ref[...].astype(f32)
    hb = hb.reshape(hb.shape[0] * hb.shape[1], hb.shape[2])
    eb = eb_ref[...].astype(f32)
    pieces = []
    for piece in (jnp.concatenate(lines, axis=0), eb, hb):
        height, width = piece.shape
        if height < 8:
            piece = jnp.concatenate([piece, jnp.zeros((8 - height, width), f32)], axis=0)
        pieces.append(piece)
    used = sum(piece.shape[1] for piece in pieces)
    pieces.append(jnp.zeros((8, 128 - used), f32))
    first_ref[part:, :128] = jnp.concatenate(pieces, axis=1).astype(bf16)
    first_ref[part:, 128:] = jnp.zeros((8, 3 * own - 128), bf16)
    hidden = expand_ref.shape[1]
    later_ref[:, :hidden] = expand_ref[...]
    later_ref[:, hidden:] = merge_ref[...]


def gather_kernel(in_ref, out_ref, own_sem, send_sem, recv_sem):
    d, y = lax.axis_index("dp"), lax.axis_index("tensor")
    z, x, c = lax.div(d, 4), lax.rem(lax.div(d, 2), 2), lax.rem(d, 2)
    far_x, far_y, far_c = 1 - x, 1 - y, 1 - c
    barrier = pltpu.get_barrier_semaphore()

    def index(place):
        pz, px, pc, py = place
        return (pz * 2 + px) * 2 + pc, py

    lower, upper = (z - 1, x, c, y), (z + 1, x, c, y)
    to_x, to_y, to_c = (z, far_x, c, y), (z, x, c, far_y), (z, x, far_c, y)

    def greet(peer):
        pl.semaphore_signal(barrier, inc=1, device_id=index(peer), device_id_type=pl.DeviceIdType.MESH)

    for peer in (to_x, to_y, to_c):
        greet(peer)
    pl.when(z > 0)(lambda: greet(lower))
    pl.when(z < 3)(lambda: greet(upper))
    pl.semaphore_wait(barrier, 4 + lax.rem(lax.div(z + 1, 2), 2))

    sent = []

    def copy(owner, peer, slot, source=None):
        p, q = index(owner)
        return pltpu.make_async_remote_copy(
            src_ref=out_ref.at[q, p] if source is None else source,
            dst_ref=out_ref.at[q, p],
            send_sem=send_sem.at[slot],
            recv_sem=recv_sem.at[p * 2 + q],
            device_id=index(peer),
            device_id_type=pl.DeviceIdType.MESH,
        )

    def send(owner, peer, there, source=None):
        slot = len(sent)
        sent.append((owner, peer, slot, there))

        @pl.when(there)
        def _():
            copy(owner, peer, slot, source).start()

    def arrive(owner, there):
        @pl.when(there)
        def _():
            copy(owner, to_c, 0).wait_recv()

    own = (z, x, c, y)
    keep = pltpu.make_async_copy(in_ref, out_ref.at[y, d], own_sem)
    send(own, upper, z < 3, in_ref)
    send(own, lower, z > 0, in_ref)
    for peer in (to_x, to_y, to_c):
        send(own, peer, z >= 0, in_ref)
    keep.start()
    for far in range(1, 4):
        for sign, after, onward in ((-1, upper, z < 3), (1, lower, z > 0)):
            level = z + sign * far
            there = (level >= 0) & (level <= 3)
            block = (level, x, c, y)
            arrive(block, there)
            send(block, after, there & onward)
            for peer in (to_x, to_y, to_c):
                send(block, peer, there)
    for far in range(4):
        for sign in (-1, 1) if far else (1,):
            level = z + sign * far
            there = (level >= 0) & (level <= 3)
            odd = lax.rem(level + 4, 2)
            block = (level, far_x, c, y)
            arrive(block, there)
            send(block, to_y, there & (odd == 0))
            send(block, to_c, there)
            block = (level, x, c, far_y)
            arrive(block, there)
            send(block, to_x, there & (odd == 1))
            send(block, to_c, there)
    for far in range(4):
        for sign in (-1, 1) if far else (1,):
            level = z + sign * far
            there = (level >= 0) & (level <= 3)
            block = (level, far_x, c, far_y)
            arrive(block, there)
            send(block, to_c, there)
    for level in range(4):
        for px in range(2):
            for py in range(2):
                arrive((level, px, far_c, py), z >= 0)
    for owner, peer, slot, there in sent:
        pl.when(there)(lambda: copy(owner, peer, slot).wait_send())
    keep.wait()


def gather_first(shard, tensor, dp):
    shape = (tensor, dp) + shard.shape
    if (tensor, dp) != (2, 16):
        return lax.all_gather(shard, AXES, axis=0, tiled=True).reshape(shape)
    return call(
        gather_kernel,
        "gather",
        (),
        [pl.BlockSpec(memory_space=pltpu.VMEM)],
        [pl.BlockSpec(memory_space=pl.ANY)],
        [(shape, bf16)],
        (shard,),
        [pltpu.SemaphoreType.DMA, pltpu.SemaphoreType.DMA((64,)), pltpu.SemaphoreType.DMA((32,))],
        collective_id=1,
        has_side_effects=True,
    )[0]


def last_kernel(dp, tensor, act_ref, resid_ref, vec_ref, w_ref, *refs):
    count, depth = dp * tensor, dp // 4
    own_ref, others, refs = refs[0], refs[1 : 2 * tensor], refs[2 * tensor :]
    one_ref, two_ref, hb_ref, eb_ref, out_ref, heads_ref, sums_ref = refs[:7]
    packed, landed, line, arrived, send_sem, recv_sem, line_send, line_recv = refs[7:]
    step = pl.program_id(0)
    d, y = lax.axis_index("dp"), lax.axis_index("tensor")
    me = d * tensor + y
    part = own_ref.shape[1]
    barrier = pltpu.get_barrier_semaphore()

    def place(k):
        other = lax.rem(me + k, count)
        return other, (lax.div(other, tensor), lax.rem(other, tensor))

    def greet(k, carry):
        _, where = place(k)
        pl.semaphore_signal(barrier, inc=1, device_id=where, device_id_type=pl.DeviceIdType.MESH)
        return carry

    def plane(z):
        total = own_ref[z].astype(f32)
        for ref in others:
            total = total + ref[z].astype(f32)
        return total

    @pl.when(step == 0)
    def _():
        lax.fori_loop(1, count, greet, 0)
        for z in range(1, depth):
            line[z - 1] = plane(z).astype(bf16)
        heads = hb_ref.shape[1] // HEAD_DIM
        own_heads, hb_wide = heads // tensor, HEAD_DIM // dp
        eb_tall, eb_wide = eb_ref.shape[0] // tensor, eb_ref.shape[1] // dp
        hb = [
            hb_ref[k : k + 1, h * HEAD_DIM : (h + 1) * HEAD_DIM] for k in range(2) for h in range(heads)
        ]
        hb = jnp.concatenate(hb, axis=0).T
        eb = eb_ref[...].T
        sums = jnp.concatenate([one_ref[...], two_ref[3:4], two_ref[1:3], two_ref[0:1]], axis=0)
        for p in range(dp):
            piece = sums[:, p * part : (p + 1) * part]
            for q in range(tensor):
                packed[p * tensor + q, 0:6, 0:part] = piece
                packed[p * tensor + q, 0:eb_wide, part : part + eb_tall] = eb[
                    p * eb_wide : (p + 1) * eb_wide, q * eb_tall : (q + 1) * eb_tall
                ]
                for k in range(2):
                    lane = part + eb_tall + k * own_heads
                    packed[p * tensor + q, 0:hb_wide, lane : lane + own_heads] = hb[
                        p * hb_wide : (p + 1) * hb_wide,
                        k * heads + q * own_heads : k * heads + (q + 1) * own_heads,
                    ]

    copies = [
        pltpu.make_async_remote_copy(
            src_ref=line.at[z - 1],
            dst_ref=arrived.at[z - 1],
            send_sem=line_send.at[z - 1],
            recv_sem=line_recv.at[z - 1],
            device_id=(flip(d, 4 * z), y),
            device_id_type=pl.DeviceIdType.MESH,
        )
        for z in range(1, depth)
    ]

    def copy(k):
        other, where = place(k)
        return pltpu.make_async_remote_copy(
            src_ref=packed.at[other],
            dst_ref=landed.at[k],
            send_sem=send_sem.at[k],
            recv_sem=recv_sem.at[k],
            device_id=where,
            device_id_type=pl.DeviceIdType.MESH,
        )

    def start(k, carry):
        copy(k).start()
        return carry

    @pl.when(step == 1)
    def _():
        pl.semaphore_wait(barrier, count - 1)
        lax.fori_loop(1, count, start, 0)
        for item in copies:
            item.start()

    total = resid_ref[...] + vec_ref[5:6]
    width = w_ref.shape[3]
    for t in range(tensor):
        w = w_ref[t].reshape(dp * part, width)
        total = total + matmul(act_ref[:, t * width : (t + 1) * width], w, NT)
    out_ref[...] = total.astype(bf16)

    def finish(k, sums):
        copy(k).wait()
        return sums + landed[k]

    @pl.when(step == pl.num_programs(0) - 1)
    def _():
        sums_ref[...] = lax.fori_loop(1, count, finish, packed[me])
        total = plane(0)
        for item, z in zip(copies, range(1, depth)):
            item.wait()
            total = total + arrived[z - 1].astype(f32)
        own = heads_ref.shape[2]
        for s in range(3):
            heads_ref[s] = total[:, s * own : (s + 1) * own]


def finish_kernel(sums_ref, heads_ref, given_ref, copy_ref, out_ref, hb_ref, eb_ref, *vectors):
    copy_ref[...] = given_ref[...]
    out_ref[...] = heads_ref[...]
    part = vectors[0].shape[1]
    for r, ref in enumerate(vectors):
        ref[...] = sums_ref[r : r + 1, :part]
    wide, tall = eb_ref.shape
    eb_ref[...] = sums_ref[:wide, part : part + tall]
    wide, count = hb_ref.shape[1:]
    for k in range(2):
        lane = part + tall + k * count
        hb_ref[k] = sums_ref[:wide, lane : lane + count]


def shards(
    tensor,
    dp,
    activations,
    first_gain,
    first_shift,
    heads_weight,
    heads_bias,
    merge_weight,
    merge_bias,
    second_gain,
    second_shift,
    expand_weight,
    expand_bias,
    reduce_weight,
    reduce_bias,
    output_grad,
    real_images,
):
    rows, deep = activations.shape
    images = rows // SEQ
    part = deep // dp
    own = heads_weight.shape[2]
    hidden_own = expand_weight.shape[1]
    hidden = hidden_own * tensor
    heads = deep // HEAD_DIM
    least = (images - 1) * STRIDE + WINDOW
    blocks = -(-least // 512)
    block = -(-least // blocks // 16) * 16
    total_rows = block * blocks

    def gather(shard):
        out = lax.all_gather(shard, AXES, axis=0, tiled=True)
        return out.reshape(tensor, dp, *shard.shape)

    small = [first_gain, first_shift, merge_bias, second_gain, second_shift, reduce_bias]
    arrays = [
        heads_weight, merge_weight.T, expand_weight,
        heads_bias.transpose(0, 2, 1), expand_bias.T,
    ] + [v.reshape(1, part) for v in small]
    vmem = pl.BlockSpec(memory_space=pltpu.VMEM)
    first, later = call(
        pack_kernel, "pack", (), [vmem] * len(arrays), [vmem] * 2,
        [((part + 8, 3 * own), bf16), ((part, hidden_own + own), bf16)], arrays,
    )
    wide = gather(later)
    wide_heads = gather_first(first, tensor, dp)
    wide_heads, turned = lax.optimization_barrier((wide_heads, reduce_weight.T))
    wide_reduce = gather(turned)

    hbs, ebs = heads_bias.shape, expand_bias.shape
    small = wide_heads[:, :, part:, :128].astype(f32)
    vectors = small[0, :, :6, :part].transpose(1, 0, 2).reshape(6, deep)
    eb = small[:, :, : ebs[1], part : part + ebs[0]].transpose(0, 3, 1, 2).reshape(1, hidden)
    hb = small[:, :, : 2 * hbs[2], part + ebs[0] : part + ebs[0] + hbs[1]]
    hb = hb.reshape(tensor, dp, 2, hbs[2], hbs[1]).transpose(2, 0, 4, 1, 3).reshape(2, deep)
    live = jnp.clip(real_images - lax.axis_index("tensor") * images, 0, images) * SEQ

    def by_rows(width):
        return pl.BlockSpec((block, width), lambda i, *_: (i, 0))

    def columns(array, index, width):
        shape = array.shape[:3] + (width,)
        return pl.BlockSpec(shape, lambda *_: (0, 0, 0, index), pipeline_mode=pl.Buffered(1))

    vec = full((6, deep))
    expand_spec, merge_spec = columns(wide, 0, hidden_own), columns(wide, hidden_own // own, own)
    triple_spec = pl.BlockSpec((3, block, deep), lambda i: (0, i, 0))
    normed_one, triple = call(
        functools.partial(qkv_kernel, part, rows),
        "qkv",
        (blocks,),
        [by_rows(deep), vec, full((2, deep)), full(wide_heads.shape)],
        [by_rows(deep), triple_spec],
        [((total_rows, deep), bf16), ((3, total_rows, deep), bf16)],
        (activations, vectors, hb, wide_heads),
        flops=total_rows * deep * deep * 3,
    )

    group = 4
    groups = heads // group
    panel = group * HEAD_DIM
    head_spec = pl.BlockSpec((3, total_rows, panel), lambda g, i: (0, 0, g))
    ctx_spec = pl.BlockSpec((total_rows, panel), lambda g, i: (0, g))
    stat_spec = pl.BlockSpec((1, group, WINDOW), lambda g, i: (g * images + i, 0, 0))
    attend_flops = images * heads * WINDOW * 768 * 256 * 2
    context, stat = call(
        attend_kernel,
        "attend",
        (groups, images),
        [head_spec],
        [ctx_spec, stat_spec],
        [((total_rows, deep), bf16), ((images * groups, group, WINDOW), f32)],
        (triple,),
        flops=attend_flops,
    )

    resid, normed_two = call(
        functools.partial(merge_kernel, rows),
        "merge",
        (blocks,),
        [by_rows(deep), by_rows(deep), vec, merge_spec],
        [by_rows(deep), by_rows(deep)],
        [((total_rows, deep), f32), ((total_rows, deep), bf16)],
        (context, activations, vectors, wide),
        flops=total_rows * deep * deep,
    )

    chunk = min(512, hidden_own)
    per = hidden_own // chunk
    chunk_spec = pl.BlockSpec((total_rows, chunk), lambda c, *_: (0, c))
    shard_spec = pl.BlockSpec((1, dp, part, chunk), lambda c, *_: (c // per, 0, 0, c % per))
    active, slope, grad_reduce = call(
        expand_kernel,
        "expand",
        (hidden // chunk,),
        [
            full((total_rows, deep)), full((rows, deep)),
            pl.BlockSpec((1, chunk), lambda c, *_: (0, c)), shard_spec,
        ],
        [chunk_spec, chunk_spec, shard_spec],
        [
            ((total_rows, hidden), bf16), ((total_rows, hidden), bf16),
            ((tensor, dp, part, hidden_own), bf16),
        ],
        (live, normed_two, output_grad, eb, wide),
        [pltpu.VMEM((total_rows, deep), bf16)],
        flops=total_rows * deep * hidden * 2,
        prefetch=1,
    )
    grad_reduce = grad_reduce.reshape(tensor * dp * part, hidden_own)
    grad_reduce = lax.psum_scatter(grad_reduce, AXES, scatter_dimension=0, tiled=True)

    back_chunk = min(512, hidden_own)
    pre_grad, resid_low, grad_context, sums_two, esum = call(
        functools.partial(mlp_back_kernel, back_chunk),
        "mlp_back",
        (blocks,),
        [
            by_rows(deep), by_rows(hidden), by_rows(deep), vec,
            expand_spec, full(wide_reduce.shape), merge_spec,
        ],
        [
            by_rows(hidden), by_rows(deep), by_rows(deep),
            pl.BlockSpec((4, deep), lambda *_: (0, 0)), pl.BlockSpec((hidden // 128, 128), lambda *_: (0, 0)),
        ],
        [
            ((total_rows, hidden), bf16), ((total_rows, deep), bf16), ((total_rows, deep), bf16),
            ((4, deep), f32), ((hidden // 128, 128), f32),
        ],
        (live, output_grad, slope, resid, vectors, wide, wide_reduce, wide),
        prefetch=1,
    )
    parts = slot_grads(
        "middle_grad", [(normed_two, pre_grad[None]), (resid_low, context[None])], tensor, dp, 512, 2
    )
    peers = 2 * tensor - 1
    shape = parts[0].shape
    grad_triple, planes = call(
        functools.partial(attend_back_kernel, tensor),
        "attend_back",
        (groups, images),
        [head_spec, stat_spec, ctx_spec] + [full(shape)] * (peers + 1),
        [head_spec, pl.BlockSpec(shape, lambda g, i: (0, 0, 0))],
        [((3, total_rows, deep), bf16), (shape, bf16)],
        (triple, stat, grad_context, *parts),
        [
            pltpu.VMEM((peers,) + shape, bf16),
            pltpu.SemaphoreType.DMA((peers,)), pltpu.SemaphoreType.DMA((peers,)),
        ],
        collective_id=4,
        has_side_effects=True,
    )
    middle, *parts = slot_grads(
        "heads_grad", [(normed_one, grad_triple)], tensor, dp, 512, 3, (planes,)
    )
    *parts, resid_low = lax.optimization_barrier((*parts, resid_low))
    last = send_plane(parts, tensor, dp)
    def whole(shape):
        return pl.BlockSpec(shape, lambda *_: (0,) * len(shape))

    shapes = [(2, deep), (2, deep), (part, hidden_own), (part, own), (part, hidden_own)]
    input_grad, sums_one, bsum, grad_expand, grad_merge, grad_reduce = call(
        functools.partial(qkv_back_kernel, part, rows),
        "qkv_back",
        (blocks,),
        [by_rows(deep), by_rows(deep), vec, triple_spec, full(wide_heads.shape), full(grad_reduce.shape)]
        + [full(middle.shape)],
        [by_rows(deep)] + [whole(shape) for shape in shapes],
        [((rows, deep), bf16)] + [(shape, f32) for shape in shapes],
        (activations, resid_low, vectors, grad_triple, wide_heads, grad_reduce, middle),
        flops=total_rows * deep * deep * 3,
    )

    hbs, ebs = heads_bias.shape, expand_bias.shape
    depth = dp // 4
    arrays = [parts[0], *last, sums_one, sums_two, bsum, esum]
    output, heads_sum, sums = call(
        functools.partial(last_kernel, dp, tensor),
        "reduce",
        (blocks,),
        [by_rows(hidden), by_rows(deep), vec, full(wide_reduce.shape)] + [full(v.shape) for v in arrays],
        [by_rows(deep), whole((3, part, own)), whole((8, 128))],
        [((rows, deep), bf16), ((3, part, own), f32), ((8, 128), f32)],
        (active, resid, vectors, wide_reduce, *arrays),
        [
            pltpu.VMEM((tensor * dp, 8, 128), f32), pltpu.VMEM((tensor * dp, 8, 128), f32),
            pltpu.VMEM((depth - 1, part, 3 * own), bf16), pltpu.VMEM((depth - 1, part, 3 * own), bf16),
            pltpu.SemaphoreType.DMA((tensor * dp,)), pltpu.SemaphoreType.DMA((tensor * dp,)),
            pltpu.SemaphoreType.DMA((depth - 1,)), pltpu.SemaphoreType.DMA((depth - 1,)),
        ],
        flops=total_rows * deep * hidden,
        collective_id=0,
        has_side_effects=True,
    )
    shapes = [heads_sum.shape, (2, hbs[2], hbs[1]), ebs[::-1]] + [(1, part)] * 6
    output, grad_heads, hb_grad, eb_grad, *vector = call(
        finish_kernel,
        "finish",
        (blocks,),
        [full(sums.shape), full(heads_sum.shape), by_rows(deep)],
        [by_rows(deep)] + [whole(shape) for shape in shapes],
        [((rows, deep), bf16)] + [(shape, f32) for shape in shapes],
        (sums, heads_sum, output),
    )
    vector = [v.reshape(part) for v in vector]

    return (
        output,
        input_grad,
        vector[0],
        vector[1],
        grad_heads,
        hb_grad.transpose(0, 2, 1),
        grad_merge.T,
        vector[2],
        vector[3],
        vector[4],
        grad_expand,
        eb_grad.T,
        grad_reduce.T,
        vector[5],
    )


def solution(mesh):
    rows = P(("dp", "tensor"), None)
    specs = (
        P("dp"),
        P("dp"),
        P(None, "dp", "tensor"),
        P(None, "tensor", "dp"),
        P("tensor", "dp"),
        P("dp"),
        P("dp"),
        P("dp"),
        P("dp", "tensor"),
        P("tensor", "dp"),
        P("tensor", "dp"),
        P("dp"),
    )
    return jax.shard_map(
        functools.partial(shards, mesh.shape["tensor"], mesh.shape["dp"]),
        mesh=mesh,
        in_specs=(rows,) + specs + (rows, P("dp")),
        out_specs=(rows, rows) + specs,
        check_vma=False,
    )
```

```python
import functools
import math

import jax
import jax.numpy as jnp
from jax import lax
from jax.experimental import pallas as pl
from jax.experimental.pallas import tpu as pltpu
from jax.sharding import PartitionSpec as P

HEAD_DIM = 64
SEQ = 577
STRIDE = 576
WINDOW = 592
LANES = 640
EPSILON = 1e-06
LOG_SCALE = 0.125
bf16 = jnp.bfloat16
f32 = jnp.float32
NN = (((1,), (0,)), ((), ()))
NT = (((1,), (1,)), ((), ()))
TN = (((0,), (0,)), ((), ()))
AXES = ("tensor", "dp")


def matmul(left, right, dims=NN):
    return lax.dot_general(left, right, dims, preferred_element_type=f32)


def norm_parts(values):
    center = values - jnp.mean(values, axis=-1, keepdims=True)
    second = jnp.mean(center * center, axis=-1, keepdims=True)
    inv = lax.rsqrt(second + EPSILON)
    return center * inv, inv


def gelu_and_slope(pre):
    phi = 0.5 + 0.5 * lax.erf(pre * 0.7071067811865476)
    bell = jnp.exp(pre * pre * -0.5)
    return pre * phi, phi + pre * (bell * 0.3989422804014327)


def full(shape):
    return pl.BlockSpec(shape, lambda *_: (0,) * len(shape), pipeline_mode=pl.Buffered(1))


def call(kernel, name, grid, in_specs, out_specs, out_shape, args, scratch=(), flops=0, prefetch=0, **params):
    moved = 0
    if flops:
        moved = sum(a.size * a.dtype.itemsize for a in args)
        moved += sum(math.prod(shape) * jnp.dtype(dtype).itemsize for shape, dtype in out_shape)
    return pl.pallas_call(
        kernel,
        grid_spec=pltpu.PrefetchScalarGridSpec(
            num_scalar_prefetch=prefetch,
            grid=grid,
            in_specs=in_specs,
            out_specs=out_specs,
            scratch_shapes=list(scratch),
        ),
        out_shape=[jax.ShapeDtypeStruct(shape, dtype) for shape, dtype in out_shape],
        compiler_params=pltpu.CompilerParams(vmem_limit_bytes=60 * 2**20, **params),
        cost_estimate=pl.CostEstimate(flops=2 * flops, bytes_accessed=moved, transcendentals=0),
        name=name,
    )(*args)


def before(ref, count):
    height = ref.shape[0]
    rows = pl.program_id(0) * height + lax.broadcasted_iota(jnp.int32, (height, 1), 0)
    return jnp.where(rows < count, ref[...].astype(f32), 0.0)


def qkv_kernel(part, count, x_ref, vec_ref, bias_ref, w_ref, normed_ref, triple_ref):
    hat, _ = norm_parts(before(x_ref, count))
    normed = (hat * vec_ref[0:1] + vec_ref[1:2]).astype(bf16)
    normed_ref[...] = normed
    tensor, dp = w_ref.shape[:2]
    width = w_ref.shape[3] // 3
    for s in range(3):
        for t in range(tensor):
            cols = slice(t * width, (t + 1) * width)
            w = w_ref[t, :, :part, s * width : (s + 1) * width].reshape(dp * part, width)
            out = matmul(normed, w)
            if s != 1:
                out = out + bias_ref[s // 2 : s // 2 + 1, cols]
            triple_ref[s, :, cols] = out.astype(bf16)


def window(image):
    start = pl.multiple_of(image * STRIDE, 16)
    return pl.ds(start, WINDOW)


def keep_before(image, ref, index, value):
    edge = pl.ds(pl.multiple_of(image * STRIDE, 16), 16)
    rest = pl.ds(pl.multiple_of(image * STRIDE + 16, 16), WINDOW - 16)
    rows = lax.broadcasted_iota(jnp.int32, (16, 1), 0)
    head = jnp.where(rows < image, ref[(*index[:-1], edge, index[-1])].astype(f32), value[:16])
    ref[(*index[:-1], edge, index[-1])] = head.astype(ref.dtype)
    ref[(*index[:-1], rest, index[-1])] = value[16:].astype(ref.dtype)


def two_heads(first, second):
    blank, below = jnp.zeros_like(first), jnp.zeros((LANES - WINDOW, 2 * HEAD_DIM), first.dtype)
    return jnp.concatenate(
        [
            jnp.concatenate([first, blank], axis=1), below,
            jnp.concatenate([blank, second], axis=1), below,
        ],
        axis=0,
    )


def head_columns(h):
    return (
        slice(HEAD_DIM * h, HEAD_DIM * (h + 2)),
        (slice(HEAD_DIM * h, HEAD_DIM * (h + 1)), slice(HEAD_DIM * (h + 1), HEAD_DIM * (h + 2))),
    )


def attend_kernel(triple_ref, context_ref, stat_ref):
    image = pl.program_id(1)
    lanes = lax.broadcasted_iota(jnp.int32, (1, LANES), 1)
    mask = jnp.where((lanes >= image) & (lanes < image + SEQ), 0.0, -1e30)
    own = window(image)
    left = lax.broadcasted_iota(jnp.int32, (1, 2 * HEAD_DIM), 1) < HEAD_DIM
    stats = []
    for h in range(0, triple_ref.shape[2] // HEAD_DIM, 2):
        pair, single = head_columns(h)
        keys = two_heads(*(triple_ref[1, own, cols] for cols in single))
        both = matmul(triple_ref[0, own, pair] * bf16(LOG_SCALE), keys, NT)
        probs, scale = [], []
        for u in range(2):
            scores = both[:, u * LANES : (u + 1) * LANES] + mask
            top = jnp.max(scores, axis=1, keepdims=True)
            expo = jnp.exp(scores - top)
            total = jnp.sum(expo, axis=1, keepdims=True)
            probs.append(expo.astype(bf16))
            scale.append(1.0 / total)
            stats.append(top + jnp.log(total))
        values = two_heads(*(triple_ref[2, own, cols] for cols in single))
        context = matmul(jnp.concatenate(probs, axis=1), values)
        keep_before(image, context_ref, (pair,), context * jnp.where(left, *scale))
    stat_ref[0] = jnp.concatenate(stats, axis=1).T


def attend_back_kernel(triple_ref, stat_ref, grad_ref, out_ref):
    image = pl.program_id(1)
    rows = lax.broadcasted_iota(jnp.int32, (WINDOW, 1), 0)
    mask = jnp.where((rows >= image) & (rows < image + SEQ), 0.0, -1e30)
    lanes = lax.broadcasted_iota(jnp.int32, (1, LANES), 1)
    real = (lanes >= image) & (lanes < image + SEQ)
    own = window(image)
    for h in range(0, triple_ref.shape[2] // HEAD_DIM, 2):
        pair, single = head_columns(h)
        keys = triple_ref[1, own, pair]
        queries = [triple_ref[0, own, cols] for cols in single]
        grads = [grad_ref[own, cols] for cols in single]
        both = matmul(keys, two_heads(*queries) * bf16(LOG_SCALE), NT)
        both_grad = matmul(triple_ref[2, own, pair], two_heads(*grads), NT)
        turned = keys.T
        value_grad, key_grad, query_grad = [], [], []
        for u in range(2):
            side = slice(u * LANES, (u + 1) * LANES)
            stat = jnp.concatenate(
                [stat_ref[0, h + u : h + u + 1, :], jnp.zeros((1, LANES - WINDOW), f32)], axis=1
            )
            probs = jnp.exp(both[:, side] + mask - jnp.where(real, stat, 1e30))
            grad_probs = both_grad[:, side]
            inner = jnp.sum(probs * grad_probs, axis=0, keepdims=True)
            grad_scores = (probs * (grad_probs - inner)).astype(bf16)
            out = matmul(
                jnp.concatenate([probs.astype(bf16), grad_scores], axis=1),
                two_heads(grads[u], queries[u]),
            )
            value_grad.append(out[:, :HEAD_DIM])
            key_grad.append(out[:, HEAD_DIM:])
            query_grad.append(matmul(turned[u * HEAD_DIM : (u + 1) * HEAD_DIM], grad_scores))
        keep_before(image, out_ref, (2, pair), jnp.concatenate(value_grad, axis=1))
        keep_before(image, out_ref, (1, pair), jnp.concatenate(key_grad, axis=1) * LOG_SCALE)
        query_grad = jnp.concatenate(query_grad, axis=0).T[:WINDOW]
        keep_before(image, out_ref, (0, pair), query_grad * LOG_SCALE)


def merge_kernel(count, ctx_ref, x_ref, vec_ref, w_ref, resid_ref, normed_ref):
    tensor, dp, part, width = w_ref.shape
    total = before(x_ref, count) + vec_ref[2:3]
    for t in range(tensor):
        w = w_ref[t].reshape(dp * part, width)
        total = total + matmul(ctx_ref[:, t * width : (t + 1) * width], w, NT)
    resid_ref[...] = total
    hat, _ = norm_parts(total)
    normed_ref[...] = (hat * vec_ref[3:4] + vec_ref[4:5]).astype(bf16)


def expand_kernel(live_ref, normed_ref, given_ref, bias_ref, w_ref, act_ref, slope_ref, out_ref, grad_ref):
    @pl.when(pl.program_id(0) == 0)
    def _():
        count = given_ref.shape[0]
        even = count // 16 * 16
        rows = lax.broadcasted_iota(jnp.int32, (count, 1), 0)
        grad_ref[:even] = jnp.where(rows[:even] < live_ref[0], given_ref[:even], bf16(0))
        grad_ref[even:] = jnp.zeros((grad_ref.shape[0] - even, grad_ref.shape[1]), bf16)
        rest = jnp.where(rows[even:] < live_ref[0], given_ref[even:].astype(f32), 0.0)
        grad_ref[even:count] = rest.astype(bf16)

    _, dp, part, width = w_ref.shape
    w = w_ref[0].reshape(dp * part, width)
    active, slope = gelu_and_slope(matmul(normed_ref[...], w) + bias_ref[...])
    active = active.astype(bf16)
    act_ref[...] = active
    slope_ref[...] = slope.astype(bf16)
    out_ref[...] = matmul(grad_ref[...], active, TN).astype(bf16).reshape(out_ref.shape)


def accumulate(first, ref, value):
    @pl.when(first)
    def _():
        ref[...] = value

    @pl.when(jnp.logical_not(first))
    def _():
        ref[...] += value


def norm_back(values, gain, grad):
    hat, inv = norm_parts(values)
    scaled = grad * gain
    back = (
        scaled
        - jnp.mean(scaled, axis=-1, keepdims=True)
        - hat * jnp.mean(scaled * hat, axis=-1, keepdims=True)
    ) * inv
    return back, jnp.sum(grad * hat, axis=0, keepdims=True), jnp.sum(grad, axis=0, keepdims=True)


def mlp_back_kernel(
    chunk, live_ref, given_ref, slope_ref, resid_ref, vec_ref, e_ref, r_ref, m_ref,
    pre_ref, low_ref, ctx_ref, sums_ref, esum_ref,
):
    tensor, dp, rows, width = e_ref.shape
    first = pl.program_id(0) == 0
    given = before(given_ref, live_ref[0])
    grad = given.astype(bf16)
    total = jnp.zeros(grad.shape, f32)
    parts = []
    for t in range(tensor):
        for c in range(width // chunk):
            local = slice(c * chunk, (c + 1) * chunk)
            cols = slice(t * width + c * chunk, t * width + (c + 1) * chunk)
            r = r_ref[t, :, :, local].reshape(dp * rows, chunk)
            pre = (matmul(grad, r) * slope_ref[:, cols].astype(f32)).astype(bf16)
            pre_ref[:, cols] = pre
            parts.append(jnp.sum(pre.astype(f32), axis=0, keepdims=True))
            e = e_ref[t, :, :, local].reshape(dp * rows, chunk)
            total = total + matmul(pre, e, NT)
    sums = 0
    half = grad.shape[0] // 2
    for rows_half in (slice(0, half), slice(half, 2 * half)):
        own = given[rows_half]
        back, gain_sum, shift_sum = norm_back(resid_ref[rows_half], vec_ref[3:4], total[rows_half])
        resid_grad = own + back
        low_ref[rows_half] = resid_grad.astype(bf16)
        lines = [jnp.sum(own, axis=0, keepdims=True), gain_sum, shift_sum]
        sums = sums + jnp.concatenate(lines + [jnp.sum(resid_grad, axis=0, keepdims=True)], axis=0)
    low = low_ref[...]
    wide = m_ref.shape[3]
    for t in range(tensor):
        m = m_ref[t].reshape(dp * rows, wide)
        ctx_ref[:, t * wide : (t + 1) * wide] = matmul(low, m).astype(bf16)
    accumulate(first, sums_ref, sums)
    parts = jnp.concatenate(parts, axis=1)
    lines = [parts[:, k * 128 : (k + 1) * 128] for k in range(esum_ref.shape[0])]
    accumulate(first, esum_ref, jnp.concatenate(lines, axis=0))


def qkv_back_kernel(part, count, x_ref, low_ref, vec_ref, grad_ref, w_ref, *refs):
    out_ref, sums_ref, bsum_ref = refs
    tensor, dp = w_ref.shape[:2]
    width = w_ref.shape[3] // 3
    first = pl.program_id(0) == 0
    total = jnp.zeros(x_ref.shape, f32)
    for s in range(3):
        for t in range(tensor):
            w = w_ref[t, :, :part, s * width : (s + 1) * width].reshape(dp * part, width)
            total = total + matmul(grad_ref[s, :, t * width : (t + 1) * width], w, NT)
    back, gain_sum, shift_sum = norm_back(before(x_ref, count), vec_ref[0:1], total)
    out_ref[...] = (low_ref[...].astype(f32) + back).astype(bf16)
    accumulate(first, sums_ref, jnp.concatenate([gain_sum, shift_sum], axis=0))
    bias = [jnp.sum(grad_ref[s].astype(f32), axis=0, keepdims=True) for s in (0, 2)]
    accumulate(first, bsum_ref, jnp.concatenate(bias, axis=0))


def flip(value, mask):
    unit = 1
    while unit <= mask:
        if mask & unit:
            value = value + unit - 2 * unit * lax.rem(lax.div(value, unit), 2)
        unit *= 2
    return value


def differ(left, right, size):
    total, unit = 0, 1
    while unit < size:
        p, q = lax.rem(lax.div(left, unit), 2), lax.rem(lax.div(right, unit), 2)
        total = total + unit * (p + q - 2 * p * q)
        unit *= 2
    return total


def slot_grad_kernel(tensor, dp, starts, *refs):
    count, steps, depth = len(starts) - 1, starts[-1], dp // 4
    lefts, rights, outs = refs[:count], refs[count : 2 * count], refs[2 * count : 2 * count + 2 * tensor]
    total, keep, send, landed, send_sem, recv_sem = refs[2 * count + 2 * tensor :]
    step, t = pl.program_id(0), pl.program_id(1)
    d, y = lax.axis_index("dp"), lax.axis_index("tensor")
    part, block = total.shape[0] // dp, total.shape[1]
    column = differ(t, y, tensor)
    slots = pl.ds(column * (2 * depth), 2 * depth)

    def copy(step):
        cols = pl.ds(pl.multiple_of(step * block, block), block)
        return pltpu.make_async_remote_copy(
            src_ref=send.at[slots, :, cols],
            dst_ref=landed.at[slots, :, cols],
            send_sem=send_sem.at[step * tensor + t],
            recv_sem=recv_sem.at[step * tensor + t],
            device_id=(flip(d, 1), y),
            device_id_type=pl.DeviceIdType.MESH,
        )

    @pl.when((step == 0) & (t == 0))
    def _():
        barrier = pltpu.get_barrier_semaphore()
        pl.semaphore_signal(
            barrier, inc=1, device_id=(flip(d, 1), y), device_id_type=pl.DeviceIdType.MESH
        )
        pl.semaphore_wait(barrier, 1)

    for j in range(count):
        @pl.when((step >= starts[j]) & (step < starts[j + 1]))
        def _():
            total[...] = matmul(lefts[j][...], rights[j][0], TN)

    @pl.when(step < steps)
    def _():
        cols = pl.ds(pl.multiple_of(step * block, block), block)
        for r in range(dp):
            owner = pl.multiple_of(flip(d, r) * part, part)
            half = send if r & 1 else keep
            slot = column * (2 * depth) + ((r >> 1) & 1) * depth + (r >> 2)
            half[slot, :, cols] = total[pl.ds(owner, part), :].astype(bf16)
        copy(step).start()

    @pl.when(step > 0)
    def _():
        copy(step - 1).wait()
        cols = pl.ds(pl.multiple_of((step - 1) * block, block), block)
        for k in range(2 * tensor):
            @pl.when(column == k // 2)
            def _():
                own = pl.ds(k * depth, depth)
                both = keep[own, :, cols].astype(f32) + landed[own, :, cols].astype(f32)
                outs[k][...] = both.astype(bf16)


def slot_grads(name, pairs, tensor, dp, block, collective_id):
    rows, deep = pairs[0][0].shape
    part, depth = deep // dp, dp // 4
    block = min([block] + [right.shape[2] // tensor for _, right in pairs])
    pers = [right.shape[2] // tensor // block for _, right in pairs]
    starts = [0]
    for (_, right), per in zip(pairs, pers):
        starts.append(starts[-1] + right.shape[0] * per)
    wide = starts[-1] * block
    half = tensor * dp // 2

    def right_map(j, i, t):
        t = jnp.where(i < starts[j], 0, jnp.where(i >= starts[j + 1], tensor - 1, t))
        i = jnp.clip(i - starts[j], 0, starts[j + 1] - starts[j] - 1)
        return (i // pers[j], 0, t * pers[j] + i % pers[j])

    spec = pl.BlockSpec((depth, part, block), lambda i, t: (0, 0, jnp.maximum(i - 1, 0)))
    return call(
        functools.partial(slot_grad_kernel, tensor, dp, starts),
        name,
        (starts[-1] + 1, tensor),
        [full((rows, deep))] * len(pairs)
        + [pl.BlockSpec((1, rows, block), functools.partial(right_map, j)) for j in range(len(pairs))],
        [spec] * (2 * tensor),
        [((depth, part, wide), bf16)] * (2 * tensor),
        [left for left, _ in pairs] + [right for _, right in pairs],
        [pltpu.VMEM((deep, block), f32)]
        + [pltpu.VMEM((half, part, wide), bf16)] * 3
        + [pltpu.SemaphoreType.DMA((starts[-1] * tensor,))] * 2,
        collective_id=collective_id,
        has_side_effects=True,
    )


def swap(values, d, t, tensor, dp):
    moves = []
    for p in range(dp):
        for q in range(tensor):
            moves.append((p * tensor + q, (p ^ d) * tensor + (q ^ t)))
    return lax.ppermute(values, ("dp", "tensor"), moves)


def send_plane(parts, tensor, dp):
    return [swap(parts[k], 2 * (k % 2), k // 2, tensor, dp) for k in range(1, 2 * tensor)]


def sum_plane(part, landed, dp):
    planes = []
    for z in range(dp // 4):
        total = part[z].astype(f32)
        for piece in landed:
            total = total + piece[z].astype(f32)
        planes.append(total.astype(bf16))
    return planes


def send_line(planes, tensor, dp):
    return [swap(planes[z], 4 * z, 0, tensor, dp) for z in range(1, dp // 4)]


def pack_kernel(
    heads_ref, merge_ref, expand_ref, hb_ref, eb_ref, *refs
):
    small, (first_ref, later_ref) = refs[:-2], refs[-2:]
    _, part, own = heads_ref.shape
    for s in range(3):
        first_ref[:part, s * own : (s + 1) * own] = heads_ref[s]
    lines = [ref[...].astype(f32) for ref in small] + [jnp.zeros((8 - len(small), part), f32)]
    hb = hb_ref[...].astype(f32)
    hb = hb.reshape(hb.shape[0] * hb.shape[1], hb.shape[2])
    eb = eb_ref[...].astype(f32)
    pieces = []
    for piece in (jnp.concatenate(lines, axis=0), eb, hb):
        height, width = piece.shape
        if height < 8:
            piece = jnp.concatenate([piece, jnp.zeros((8 - height, width), f32)], axis=0)
        pieces.append(piece)
    used = sum(piece.shape[1] for piece in pieces)
    pieces.append(jnp.zeros((8, 128 - used), f32))
    first_ref[part:, :128] = jnp.concatenate(pieces, axis=1).astype(bf16)
    first_ref[part:, 128:] = jnp.zeros((8, 3 * own - 128), bf16)
    hidden = expand_ref.shape[1]
    later_ref[:, :hidden] = expand_ref[...]
    later_ref[:, hidden:] = merge_ref[...]


def gather_kernel(in_ref, out_ref, own_sem, send_sem, recv_sem):
    d, y = lax.axis_index("dp"), lax.axis_index("tensor")
    z, x, c = lax.div(d, 4), lax.rem(lax.div(d, 2), 2), lax.rem(d, 2)
    far_x, far_y, far_c = 1 - x, 1 - y, 1 - c
    barrier = pltpu.get_barrier_semaphore()

    def index(place):
        pz, px, pc, py = place
        return (pz * 2 + px) * 2 + pc, py

    lower, upper = (z - 1, x, c, y), (z + 1, x, c, y)
    to_x, to_y, to_c = (z, far_x, c, y), (z, x, c, far_y), (z, x, far_c, y)

    def greet(peer):
        pl.semaphore_signal(barrier, inc=1, device_id=index(peer), device_id_type=pl.DeviceIdType.MESH)

    for peer in (to_x, to_y, to_c):
        greet(peer)
    pl.when(z > 0)(lambda: greet(lower))
    pl.when(z < 3)(lambda: greet(upper))
    pl.semaphore_wait(barrier, 4 + lax.rem(lax.div(z + 1, 2), 2))

    sent = []

    def copy(owner, peer, slot, source=None):
        p, q = index(owner)
        return pltpu.make_async_remote_copy(
            src_ref=out_ref.at[q, p] if source is None else source,
            dst_ref=out_ref.at[q, p],
            send_sem=send_sem.at[slot],
            recv_sem=recv_sem.at[p * 2 + q],
            device_id=index(peer),
            device_id_type=pl.DeviceIdType.MESH,
        )

    def send(owner, peer, there, source=None):
        slot = len(sent)
        sent.append((owner, peer, slot, there))

        @pl.when(there)
        def _():
            copy(owner, peer, slot, source).start()

    def arrive(owner, there):
        @pl.when(there)
        def _():
            copy(owner, to_c, 0).wait_recv()

    own = (z, x, c, y)
    keep = pltpu.make_async_copy(in_ref, out_ref.at[y, d], own_sem)
    send(own, upper, z < 3, in_ref)
    send(own, lower, z > 0, in_ref)
    for peer in (to_x, to_y, to_c):
        send(own, peer, z >= 0, in_ref)
    keep.start()
    for far in range(1, 4):
        for sign, after, onward in ((-1, upper, z < 3), (1, lower, z > 0)):
            level = z + sign * far
            there = (level >= 0) & (level <= 3)
            block = (level, x, c, y)
            arrive(block, there)
            send(block, after, there & onward)
            for peer in (to_x, to_y, to_c):
                send(block, peer, there)
    for far in range(4):
        for sign in (-1, 1) if far else (1,):
            level = z + sign * far
            there = (level >= 0) & (level <= 3)
            odd = lax.rem(level + 4, 2)
            block = (level, far_x, c, y)
            arrive(block, there)
            send(block, to_y, there & (odd == 0))
            send(block, to_c, there)
            block = (level, x, c, far_y)
            arrive(block, there)
            send(block, to_x, there & (odd == 1))
            send(block, to_c, there)
    for far in range(4):
        for sign in (-1, 1) if far else (1,):
            level = z + sign * far
            there = (level >= 0) & (level <= 3)
            block = (level, far_x, c, far_y)
            arrive(block, there)
            send(block, to_c, there)
    for level in range(4):
        for px in range(2):
            for py in range(2):
                arrive((level, px, far_c, py), z >= 0)
    for owner, peer, slot, there in sent:
        pl.when(there)(lambda: copy(owner, peer, slot).wait_send())
    keep.wait()


def gather_first(shard, tensor, dp):
    shape = (tensor, dp) + shard.shape
    if (tensor, dp) != (2, 16):
        return lax.all_gather(shard, AXES, axis=0, tiled=True).reshape(shape)
    return call(
        gather_kernel,
        "gather",
        (),
        [pl.BlockSpec(memory_space=pltpu.VMEM)],
        [pl.BlockSpec(memory_space=pl.ANY)],
        [(shape, bf16)],
        (shard,),
        [pltpu.SemaphoreType.DMA, pltpu.SemaphoreType.DMA((64,)), pltpu.SemaphoreType.DMA((32,))],
        collective_id=1,
        has_side_effects=True,
    )[0]


def last_kernel(dp, tensor, act_ref, resid_ref, vec_ref, w_ref, *refs):
    count, depth = dp * tensor, dp // 4
    own_ref, others, refs = refs[0], refs[1 : 2 * tensor], refs[2 * tensor :]
    one_ref, two_ref, hb_ref, eb_ref, out_ref, heads_ref, sums_ref = refs[:7]
    packed, landed, line, arrived, send_sem, recv_sem, line_send, line_recv = refs[7:]
    step = pl.program_id(0)
    d, y = lax.axis_index("dp"), lax.axis_index("tensor")
    me = d * tensor + y
    part = own_ref.shape[1]
    barrier = pltpu.get_barrier_semaphore()

    def place(k):
        other = lax.rem(me + k, count)
        return other, (lax.div(other, tensor), lax.rem(other, tensor))

    def greet(k, carry):
        _, where = place(k)
        pl.semaphore_signal(barrier, inc=1, device_id=where, device_id_type=pl.DeviceIdType.MESH)
        return carry

    def plane(z):
        total = own_ref[z].astype(f32)
        for ref in others:
            total = total + ref[z].astype(f32)
        return total

    @pl.when(step == 0)
    def _():
        lax.fori_loop(1, count, greet, 0)
        for z in range(1, depth):
            line[z - 1] = plane(z).astype(bf16)
        heads = hb_ref.shape[1] // HEAD_DIM
        own_heads, hb_wide = heads // tensor, HEAD_DIM // dp
        eb_tall, eb_wide = eb_ref.shape[0] // tensor, eb_ref.shape[1] // dp
        hb = [
            hb_ref[k : k + 1, h * HEAD_DIM : (h + 1) * HEAD_DIM] for k in range(2) for h in range(heads)
        ]
        hb = jnp.concatenate(hb, axis=0).T
        eb = eb_ref[...].T
        sums = jnp.concatenate([one_ref[...], two_ref[3:4], two_ref[1:3], two_ref[0:1]], axis=0)
        for p in range(dp):
            piece = sums[:, p * part : (p + 1) * part]
            for q in range(tensor):
                packed[p * tensor + q, 0:6, 0:part] = piece
                packed[p * tensor + q, 0:eb_wide, part : part + eb_tall] = eb[
                    p * eb_wide : (p + 1) * eb_wide, q * eb_tall : (q + 1) * eb_tall
                ]
                for k in range(2):
                    lane = part + eb_tall + k * own_heads
                    packed[p * tensor + q, 0:hb_wide, lane : lane + own_heads] = hb[
                        p * hb_wide : (p + 1) * hb_wide,
                        k * heads + q * own_heads : k * heads + (q + 1) * own_heads,
                    ]

    copies = [
        pltpu.make_async_remote_copy(
            src_ref=line.at[z - 1],
            dst_ref=arrived.at[z - 1],
            send_sem=line_send.at[z - 1],
            recv_sem=line_recv.at[z - 1],
            device_id=(flip(d, 4 * z), y),
            device_id_type=pl.DeviceIdType.MESH,
        )
        for z in range(1, depth)
    ]

    def copy(k):
        other, where = place(k)
        return pltpu.make_async_remote_copy(
            src_ref=packed.at[other],
            dst_ref=landed.at[k],
            send_sem=send_sem.at[k],
            recv_sem=recv_sem.at[k],
            device_id=where,
            device_id_type=pl.DeviceIdType.MESH,
        )

    def start(k, carry):
        copy(k).start()
        return carry

    @pl.when(step == 1)
    def _():
        pl.semaphore_wait(barrier, count - 1)
        lax.fori_loop(1, count, start, 0)
        for item in copies:
            item.start()

    total = resid_ref[...] + vec_ref[5:6]
    width = w_ref.shape[3]
    for t in range(tensor):
        w = w_ref[t].reshape(dp * part, width)
        total = total + matmul(act_ref[:, t * width : (t + 1) * width], w, NT)
    out_ref[...] = total.astype(bf16)

    def finish(k, sums):
        copy(k).wait()
        return sums + landed[k]

    @pl.when(step == pl.num_programs(0) - 1)
    def _():
        sums_ref[...] = lax.fori_loop(1, count, finish, packed[me])
        total = plane(0)
        for item, z in zip(copies, range(1, depth)):
            item.wait()
            total = total + arrived[z - 1].astype(f32)
        own = heads_ref.shape[2]
        for s in range(3):
            heads_ref[s] = total[:, s * own : (s + 1) * own]


def finish_kernel(depth, given_ref, sums_ref, heads_ref, reduced_ref, *refs):
    planes, (copy_ref, reduce_ref, expand_ref, merge_ref, out_ref, hb_ref, eb_ref) = refs[:depth], refs[depth : depth + 7]
    vectors, sem = refs[depth + 7 : -1], refs[-1]
    copies = []
    for k in range(sem.shape[0]):
        width = given_ref.shape[1] // sem.shape[0]
        cols = pl.ds(k * width, width)
        copies.append(pltpu.make_async_copy(given_ref.at[:, cols], copy_ref.at[:, cols], sem.at[k]))
    for item in copies:
        item.start()
    total = planes[0][...].astype(f32)
    for ref in planes[1:]:
        total = total + ref[...].astype(f32)
    hidden = expand_ref.shape[1]
    expand_ref[...] = total[:, :hidden]
    merge_ref[...] = total[:, hidden:]
    reduce_ref[...] = reduced_ref[...].astype(f32)
    out_ref[...] = heads_ref[...]
    part = vectors[0].shape[1]
    for r, ref in enumerate(vectors):
        ref[...] = sums_ref[r : r + 1, :part]
    wide, tall = eb_ref.shape
    eb_ref[...] = sums_ref[:wide, part : part + tall]
    wide, count = hb_ref.shape[1:]
    for k in range(2):
        lane = part + tall + k * count
        hb_ref[k] = sums_ref[:wide, lane : lane + count]
    for item in copies:
        item.wait()


def shards(
    tensor,
    dp,
    activations,
    first_gain,
    first_shift,
    heads_weight,
    heads_bias,
    merge_weight,
    merge_bias,
    second_gain,
    second_shift,
    expand_weight,
    expand_bias,
    reduce_weight,
    reduce_bias,
    output_grad,
    real_images,
):
    rows, deep = activations.shape
    images = rows // SEQ
    part = deep // dp
    own = heads_weight.shape[2]
    hidden_own = expand_weight.shape[1]
    hidden = hidden_own * tensor
    heads = deep // HEAD_DIM
    least = (images - 1) * STRIDE + WINDOW
    blocks = -(-least // 512)
    block = -(-least // blocks // 16) * 16
    total_rows = block * blocks

    def gather(shard):
        out = lax.all_gather(shard, AXES, axis=0, tiled=True)
        return out.reshape(tensor, dp, *shard.shape)

    small = [first_gain, first_shift, merge_bias, second_gain, second_shift, reduce_bias]
    arrays = [
        heads_weight, merge_weight.T, expand_weight,
        heads_bias.transpose(0, 2, 1), expand_bias.T,
    ] + [v.reshape(1, part) for v in small]
    vmem = pl.BlockSpec(memory_space=pltpu.VMEM)
    first, later = call(
        pack_kernel, "pack", (), [vmem] * len(arrays), [vmem] * 2,
        [((part + 8, 3 * own), bf16), ((part, hidden_own + own), bf16)], arrays,
    )
    wide = gather(later)
    wide_heads = gather_first(first, tensor, dp)
    wide_heads, turned = lax.optimization_barrier((wide_heads, reduce_weight.T))
    wide_reduce = gather(turned)

    hbs, ebs = heads_bias.shape, expand_bias.shape
    small = wide_heads[:, :, part:, :128].astype(f32)
    vectors = small[0, :, :6, :part].transpose(1, 0, 2).reshape(6, deep)
    eb = small[:, :, : ebs[1], part : part + ebs[0]].transpose(0, 3, 1, 2).reshape(1, hidden)
    hb = small[:, :, : 2 * hbs[2], part + ebs[0] : part + ebs[0] + hbs[1]]
    hb = hb.reshape(tensor, dp, 2, hbs[2], hbs[1]).transpose(2, 0, 4, 1, 3).reshape(2, deep)
    live = jnp.clip(real_images - lax.axis_index("tensor") * images, 0, images) * SEQ

    def by_rows(width):
        return pl.BlockSpec((block, width), lambda i, *_: (i, 0))

    def columns(array, index, width):
        shape = array.shape[:3] + (width,)
        return pl.BlockSpec(shape, lambda *_: (0, 0, 0, index), pipeline_mode=pl.Buffered(1))

    vec = full((6, deep))
    expand_spec, merge_spec = columns(wide, 0, hidden_own), columns(wide, hidden_own // own, own)
    triple_spec = pl.BlockSpec((3, block, deep), lambda i: (0, i, 0))
    normed_one, triple = call(
        functools.partial(qkv_kernel, part, rows),
        "qkv",
        (blocks,),
        [by_rows(deep), vec, full((2, deep)), full(wide_heads.shape)],
        [by_rows(deep), triple_spec],
        [((total_rows, deep), bf16), ((3, total_rows, deep), bf16)],
        (activations, vectors, hb, wide_heads),
        flops=total_rows * deep * deep * 3,
    )

    group = 4
    groups = heads // group
    panel = group * HEAD_DIM
    head_spec = pl.BlockSpec((3, total_rows, panel), lambda g, i: (0, 0, g))
    ctx_spec = pl.BlockSpec((total_rows, panel), lambda g, i: (0, g))
    stat_spec = pl.BlockSpec((1, group, WINDOW), lambda g, i: (g * images + i, 0, 0))
    attend_flops = images * heads * WINDOW * 768 * 256 * 2
    context, stat = call(
        attend_kernel,
        "attend",
        (groups, images),
        [head_spec],
        [ctx_spec, stat_spec],
        [((total_rows, deep), bf16), ((images * groups, group, WINDOW), f32)],
        (triple,),
        flops=attend_flops,
    )

    resid, normed_two = call(
        functools.partial(merge_kernel, rows),
        "merge",
        (blocks,),
        [by_rows(deep), by_rows(deep), vec, merge_spec],
        [by_rows(deep), by_rows(deep)],
        [((total_rows, deep), f32), ((total_rows, deep), bf16)],
        (context, activations, vectors, wide),
        flops=total_rows * deep * deep,
    )

    chunk = min(512, hidden_own)
    per = hidden_own // chunk
    chunk_spec = pl.BlockSpec((total_rows, chunk), lambda c, *_: (0, c))
    shard_spec = pl.BlockSpec((1, dp, part, chunk), lambda c, *_: (c // per, 0, 0, c % per))
    active, slope, grad_reduce = call(
        expand_kernel,
        "expand",
        (hidden // chunk,),
        [
            full((total_rows, deep)), full((rows, deep)),
            pl.BlockSpec((1, chunk), lambda c, *_: (0, c)), shard_spec,
        ],
        [chunk_spec, chunk_spec, shard_spec],
        [
            ((total_rows, hidden), bf16), ((total_rows, hidden), bf16),
            ((tensor, dp, part, hidden_own), bf16),
        ],
        (live, normed_two, output_grad, eb, wide),
        [pltpu.VMEM((total_rows, deep), bf16)],
        flops=total_rows * deep * hidden * 2,
        prefetch=1,
    )
    grad_reduce = grad_reduce.reshape(tensor * dp * part, hidden_own)
    grad_reduce = lax.psum_scatter(grad_reduce, AXES, scatter_dimension=0, tiled=True)

    back_chunk = min(512, hidden_own)
    pre_grad, resid_low, grad_context, sums_two, esum = call(
        functools.partial(mlp_back_kernel, back_chunk),
        "mlp_back",
        (blocks,),
        [
            by_rows(deep), by_rows(hidden), by_rows(deep), vec,
            expand_spec, full(wide_reduce.shape), merge_spec,
        ],
        [
            by_rows(hidden), by_rows(deep), by_rows(deep),
            pl.BlockSpec((4, deep), lambda *_: (0, 0)), pl.BlockSpec((hidden // 128, 128), lambda *_: (0, 0)),
        ],
        [
            ((total_rows, hidden), bf16), ((total_rows, deep), bf16), ((total_rows, deep), bf16),
            ((4, deep), f32), ((hidden // 128, 128), f32),
        ],
        (live, output_grad, slope, resid, vectors, wide, wide_reduce, wide),
        prefetch=1,
    )
    parts = slot_grads(
        "middle_grad", [(normed_two, pre_grad[None]), (resid_low, context[None])], tensor, dp, 512, 2
    )
    *parts, grad_context = lax.optimization_barrier((*parts, grad_context))
    landed = send_plane(parts, tensor, dp)
    grad_triple = call(
        attend_back_kernel,
        "attend_back",
        (groups, images),
        [head_spec, stat_spec, ctx_spec],
        [head_spec],
        [((3, total_rows, deep), bf16)],
        (triple, stat, grad_context),
    )[0]
    heads = slot_grads("heads_grad", [(normed_one, grad_triple)], tensor, dp, 512, 3)
    held = (tuple(heads), tuple(landed), parts[0], resid_low)
    heads, landed, part_own, resid_low = lax.optimization_barrier(held)
    last = send_plane(heads, tensor, dp)
    planes = sum_plane(part_own, landed, dp)
    planes, resid_low = lax.optimization_barrier((tuple(planes), resid_low))
    line = send_line(planes, tensor, dp)

    def whole(shape):
        return pl.BlockSpec(shape, lambda *_: (0,) * len(shape))

    shapes = [(2, deep), (2, deep)]
    input_grad, sums_one, bsum = call(
        functools.partial(qkv_back_kernel, part, rows),
        "qkv_back",
        (blocks,),
        [by_rows(deep), by_rows(deep), vec, triple_spec, full(wide_heads.shape)],
        [by_rows(deep)] + [whole(shape) for shape in shapes],
        [((rows, deep), bf16)] + [(shape, f32) for shape in shapes],
        (activations, resid_low, vectors, grad_triple, wide_heads),
        flops=total_rows * deep * deep * 3,
    )

    hbs, ebs = heads_bias.shape, expand_bias.shape
    depth = dp // 4
    arrays = [heads[0], *last, sums_one, sums_two, bsum, esum]
    output, heads_sum, sums = call(
        functools.partial(last_kernel, dp, tensor),
        "reduce",
        (blocks,),
        [by_rows(hidden), by_rows(deep), vec, full(wide_reduce.shape)] + [full(v.shape) for v in arrays],
        [by_rows(deep), whole((3, part, own)), whole((8, 128))],
        [((rows, deep), bf16), ((3, part, own), f32), ((8, 128), f32)],
        (active, resid, vectors, wide_reduce, *arrays),
        [
            pltpu.VMEM((tensor * dp, 8, 128), f32), pltpu.VMEM((tensor * dp, 8, 128), f32),
            pltpu.VMEM((depth - 1, part, 3 * own), bf16), pltpu.VMEM((depth - 1, part, 3 * own), bf16),
            pltpu.SemaphoreType.DMA((tensor * dp,)), pltpu.SemaphoreType.DMA((tensor * dp,)),
            pltpu.SemaphoreType.DMA((depth - 1,)), pltpu.SemaphoreType.DMA((depth - 1,)),
        ],
        flops=total_rows * deep * hidden,
        collective_id=0,
        has_side_effects=True,
    )
    shapes = [(part, hidden_own), (part, hidden_own), (part, own)]
    shapes += [heads_sum.shape, (2, hbs[2], hbs[1]), ebs[::-1]] + [(1, part)] * 6
    hbm = pl.BlockSpec(memory_space=pl.ANY)
    arrays = [output, sums, heads_sum, grad_reduce, planes[0], *line]
    output, grad_reduce, grad_expand, grad_merge, grad_heads, hb_grad, eb_grad, *vector = call(
        functools.partial(finish_kernel, depth),
        "finish",
        (),
        [hbm] + [vmem] * (len(arrays) - 1),
        [hbm] + [vmem] * len(shapes),
        [((rows, deep), bf16)] + [(shape, f32) for shape in shapes],
        arrays,
        [pltpu.SemaphoreType.DMA((4,))],
    )
    vector = [v.reshape(part) for v in vector]

    return (
        output,
        input_grad,
        vector[0],
        vector[1],
        grad_heads,
        hb_grad.transpose(0, 2, 1),
        grad_merge.T,
        vector[2],
        vector[3],
        vector[4],
        grad_expand,
        eb_grad.T,
        grad_reduce.T,
        vector[5],
    )


def solution(mesh):
    rows = P(("dp", "tensor"), None)
    specs = (
        P("dp"),
        P("dp"),
        P(None, "dp", "tensor"),
        P(None, "tensor", "dp"),
        P("tensor", "dp"),
        P("dp"),
        P("dp"),
        P("dp"),
        P("dp", "tensor"),
        P("tensor", "dp"),
        P("tensor", "dp"),
        P("dp"),
    )
    return jax.shard_map(
        functools.partial(shards, mesh.shape["tensor"], mesh.shape["dp"]),
        mesh=mesh,
        in_specs=(rows,) + specs + (rows, P("dp")),
        out_specs=(rows, rows) + specs,
        check_vma=False,
    )
```

```python
import functools
import math

import jax
import jax.numpy as jnp
from jax import lax
from jax.experimental import pallas as pl
from jax.experimental.pallas import tpu as pltpu
from jax.sharding import PartitionSpec as P

HEAD_DIM = 64
SEQ = 577
STRIDE = 576
WINDOW = 592
LANES = 640
EPSILON = 1e-06
LOG_SCALE = 0.125
bf16 = jnp.bfloat16
f32 = jnp.float32
NN = (((1,), (0,)), ((), ()))
NT = (((1,), (1,)), ((), ()))
TN = (((0,), (0,)), ((), ()))
AXES = ("tensor", "dp")


def matmul(left, right, dims=NN):
    return lax.dot_general(left, right, dims, preferred_element_type=f32)


def norm_parts(values):
    center = values - jnp.mean(values, axis=-1, keepdims=True)
    second = jnp.mean(center * center, axis=-1, keepdims=True)
    inv = lax.rsqrt(second + EPSILON)
    return center * inv, inv


def gelu_and_slope(pre):
    phi = 0.5 + 0.5 * lax.erf(pre * 0.7071067811865476)
    bell = jnp.exp(pre * pre * -0.5)
    return pre * phi, phi + pre * (bell * 0.3989422804014327)


def full(shape):
    return pl.BlockSpec(shape, lambda *_: (0,) * len(shape), pipeline_mode=pl.Buffered(1))


def call(kernel, name, grid, in_specs, out_specs, out_shape, args, scratch=(), flops=0, prefetch=0, **params):
    moved = 0
    if flops:
        moved = sum(a.size * a.dtype.itemsize for a in args)
        moved += sum(math.prod(shape) * jnp.dtype(dtype).itemsize for shape, dtype in out_shape)
    return pl.pallas_call(
        kernel,
        grid_spec=pltpu.PrefetchScalarGridSpec(
            num_scalar_prefetch=prefetch,
            grid=grid,
            in_specs=in_specs,
            out_specs=out_specs,
            scratch_shapes=list(scratch),
        ),
        out_shape=[jax.ShapeDtypeStruct(shape, dtype) for shape, dtype in out_shape],
        compiler_params=pltpu.CompilerParams(vmem_limit_bytes=60 * 2**20, **params),
        cost_estimate=pl.CostEstimate(flops=2 * flops, bytes_accessed=moved, transcendentals=0),
        name=name,
    )(*args)


def before(ref, count):
    height = ref.shape[0]
    rows = pl.program_id(0) * height + lax.broadcasted_iota(jnp.int32, (height, 1), 0)
    return jnp.where(rows < count, ref[...].astype(f32), 0.0)


def qkv_kernel(part, count, x_ref, vec_ref, bias_ref, w_ref, normed_ref, triple_ref):
    hat, _ = norm_parts(before(x_ref, count))
    normed = (hat * vec_ref[0:1] + vec_ref[1:2]).astype(bf16)
    normed_ref[...] = normed
    tensor, dp = w_ref.shape[:2]
    width = w_ref.shape[3] // 3
    for s in range(3):
        for t in range(tensor):
            cols = slice(t * width, (t + 1) * width)
            w = w_ref[t, :, :part, s * width : (s + 1) * width].reshape(dp * part, width)
            out = matmul(normed, w)
            if s != 1:
                out = out + bias_ref[s // 2 : s // 2 + 1, cols]
            triple_ref[s, :, cols] = out.astype(bf16)


def window(image):
    start = pl.multiple_of(image * STRIDE, 16)
    return pl.ds(start, WINDOW)


def keep_before(image, ref, index, value):
    edge = pl.ds(pl.multiple_of(image * STRIDE, 16), 16)
    rest = pl.ds(pl.multiple_of(image * STRIDE + 16, 16), WINDOW - 16)
    rows = lax.broadcasted_iota(jnp.int32, (16, 1), 0)
    head = jnp.where(rows < image, ref[(*index[:-1], edge, index[-1])].astype(f32), value[:16])
    ref[(*index[:-1], edge, index[-1])] = head.astype(ref.dtype)
    ref[(*index[:-1], rest, index[-1])] = value[16:].astype(ref.dtype)


def two_heads(first, second):
    blank, below = jnp.zeros_like(first), jnp.zeros((LANES - WINDOW, 2 * HEAD_DIM), first.dtype)
    return jnp.concatenate(
        [
            jnp.concatenate([first, blank], axis=1), below,
            jnp.concatenate([blank, second], axis=1), below,
        ],
        axis=0,
    )


def head_columns(h):
    return (
        slice(HEAD_DIM * h, HEAD_DIM * (h + 2)),
        (slice(HEAD_DIM * h, HEAD_DIM * (h + 1)), slice(HEAD_DIM * (h + 1), HEAD_DIM * (h + 2))),
    )


def attend_kernel(triple_ref, context_ref, stat_ref):
    image = pl.program_id(1)
    lanes = lax.broadcasted_iota(jnp.int32, (1, LANES), 1)
    mask = jnp.where((lanes >= image) & (lanes < image + SEQ), 0.0, -1e30)
    own = window(image)
    left = lax.broadcasted_iota(jnp.int32, (1, 2 * HEAD_DIM), 1) < HEAD_DIM
    stats = []
    for h in range(0, triple_ref.shape[2] // HEAD_DIM, 2):
        pair, single = head_columns(h)
        keys = two_heads(*(triple_ref[1, own, cols] for cols in single))
        both = matmul(triple_ref[0, own, pair] * bf16(LOG_SCALE), keys, NT)
        probs, scale = [], []
        for u in range(2):
            scores = both[:, u * LANES : (u + 1) * LANES] + mask
            top = jnp.max(scores, axis=1, keepdims=True)
            expo = jnp.exp(scores - top)
            total = jnp.sum(expo, axis=1, keepdims=True)
            probs.append(expo.astype(bf16))
            scale.append(1.0 / total)
            stats.append(top + jnp.log(total))
        values = two_heads(*(triple_ref[2, own, cols] for cols in single))
        context = matmul(jnp.concatenate(probs, axis=1), values)
        keep_before(image, context_ref, (pair,), context * jnp.where(left, *scale))
    stat_ref[0] = jnp.concatenate(stats, axis=1).T


def attend_back_kernel(triple_ref, stat_ref, grad_ref, out_ref):
    image = pl.program_id(1)
    rows = lax.broadcasted_iota(jnp.int32, (WINDOW, 1), 0)
    mask = jnp.where((rows >= image) & (rows < image + SEQ), 0.0, -1e30)
    lanes = lax.broadcasted_iota(jnp.int32, (1, LANES), 1)
    real = (lanes >= image) & (lanes < image + SEQ)
    own = window(image)
    for h in range(0, triple_ref.shape[2] // HEAD_DIM, 2):
        pair, single = head_columns(h)
        keys = triple_ref[1, own, pair]
        queries = [triple_ref[0, own, cols] for cols in single]
        grads = [grad_ref[own, cols] for cols in single]
        both = matmul(keys, two_heads(*queries) * bf16(LOG_SCALE), NT)
        both_grad = matmul(triple_ref[2, own, pair], two_heads(*grads), NT)
        turned = keys.T
        value_grad, key_grad, query_grad = [], [], []
        for u in range(2):
            side = slice(u * LANES, (u + 1) * LANES)
            stat = jnp.concatenate(
                [stat_ref[0, h + u : h + u + 1, :], jnp.zeros((1, LANES - WINDOW), f32)], axis=1
            )
            probs = jnp.exp(both[:, side] + mask - jnp.where(real, stat, 1e30))
            grad_probs = both_grad[:, side]
            inner = jnp.sum(probs * grad_probs, axis=0, keepdims=True)
            grad_scores = (probs * (grad_probs - inner)).astype(bf16)
            out = matmul(
                jnp.concatenate([probs.astype(bf16), grad_scores], axis=1),
                two_heads(grads[u], queries[u]),
            )
            value_grad.append(out[:, :HEAD_DIM])
            key_grad.append(out[:, HEAD_DIM:])
            query_grad.append(matmul(turned[u * HEAD_DIM : (u + 1) * HEAD_DIM], grad_scores))
        keep_before(image, out_ref, (2, pair), jnp.concatenate(value_grad, axis=1))
        keep_before(image, out_ref, (1, pair), jnp.concatenate(key_grad, axis=1) * LOG_SCALE)
        query_grad = jnp.concatenate(query_grad, axis=0).T[:WINDOW]
        keep_before(image, out_ref, (0, pair), query_grad * LOG_SCALE)


def merge_kernel(count, ctx_ref, x_ref, vec_ref, w_ref, resid_ref, normed_ref):
    tensor, dp, part, width = w_ref.shape
    total = before(x_ref, count) + vec_ref[2:3]
    for t in range(tensor):
        w = w_ref[t].reshape(dp * part, width)
        total = total + matmul(ctx_ref[:, t * width : (t + 1) * width], w, NT)
    resid_ref[...] = total
    hat, _ = norm_parts(total)
    normed_ref[...] = (hat * vec_ref[3:4] + vec_ref[4:5]).astype(bf16)


def expand_kernel(live_ref, normed_ref, given_ref, bias_ref, w_ref, act_ref, slope_ref, out_ref, grad_ref):
    @pl.when(pl.program_id(0) == 0)
    def _():
        count = given_ref.shape[0]
        even = count // 16 * 16
        rows = lax.broadcasted_iota(jnp.int32, (count, 1), 0)
        grad_ref[:even] = jnp.where(rows[:even] < live_ref[0], given_ref[:even], bf16(0))
        grad_ref[even:] = jnp.zeros((grad_ref.shape[0] - even, grad_ref.shape[1]), bf16)
        rest = jnp.where(rows[even:] < live_ref[0], given_ref[even:].astype(f32), 0.0)
        grad_ref[even:count] = rest.astype(bf16)

    _, dp, part, width = w_ref.shape
    w = w_ref[0].reshape(dp * part, width)
    active, slope = gelu_and_slope(matmul(normed_ref[...], w) + bias_ref[...])
    active = active.astype(bf16)
    act_ref[...] = active
    slope_ref[...] = slope.astype(bf16)
    out_ref[...] = matmul(grad_ref[...], active, TN).astype(bf16).reshape(out_ref.shape)


def accumulate(first, ref, value):
    @pl.when(first)
    def _():
        ref[...] = value

    @pl.when(jnp.logical_not(first))
    def _():
        ref[...] += value


def norm_back(values, gain, grad):
    hat, inv = norm_parts(values)
    scaled = grad * gain
    back = (
        scaled
        - jnp.mean(scaled, axis=-1, keepdims=True)
        - hat * jnp.mean(scaled * hat, axis=-1, keepdims=True)
    ) * inv
    return back, jnp.sum(grad * hat, axis=0, keepdims=True), jnp.sum(grad, axis=0, keepdims=True)


def mlp_back_kernel(
    chunk, live_ref, given_ref, slope_ref, resid_ref, vec_ref, e_ref, r_ref, m_ref,
    pre_ref, low_ref, ctx_ref, sums_ref, esum_ref,
):
    tensor, dp, rows, width = e_ref.shape
    first = pl.program_id(0) == 0
    given = before(given_ref, live_ref[0])
    grad = given.astype(bf16)
    total = jnp.zeros(grad.shape, f32)
    parts = []
    for t in range(tensor):
        for c in range(width // chunk):
            local = slice(c * chunk, (c + 1) * chunk)
            cols = slice(t * width + c * chunk, t * width + (c + 1) * chunk)
            r = r_ref[t, :, :, local].reshape(dp * rows, chunk)
            pre = (matmul(grad, r) * slope_ref[:, cols].astype(f32)).astype(bf16)
            pre_ref[:, cols] = pre
            parts.append(jnp.sum(pre.astype(f32), axis=0, keepdims=True))
            e = e_ref[t, :, :, local].reshape(dp * rows, chunk)
            total = total + matmul(pre, e, NT)
    sums = 0
    half = grad.shape[0] // 2
    for rows_half in (slice(0, half), slice(half, 2 * half)):
        own = given[rows_half]
        back, gain_sum, shift_sum = norm_back(resid_ref[rows_half], vec_ref[3:4], total[rows_half])
        resid_grad = own + back
        low_ref[rows_half] = resid_grad.astype(bf16)
        lines = [jnp.sum(own, axis=0, keepdims=True), gain_sum, shift_sum]
        sums = sums + jnp.concatenate(lines + [jnp.sum(resid_grad, axis=0, keepdims=True)], axis=0)
    low = low_ref[...]
    wide = m_ref.shape[3]
    for t in range(tensor):
        m = m_ref[t].reshape(dp * rows, wide)
        ctx_ref[:, t * wide : (t + 1) * wide] = matmul(low, m).astype(bf16)
    accumulate(first, sums_ref, sums)
    parts = jnp.concatenate(parts, axis=1)
    lines = [parts[:, k * 128 : (k + 1) * 128] for k in range(esum_ref.shape[0])]
    accumulate(first, esum_ref, jnp.concatenate(lines, axis=0))


def qkv_back_kernel(part, count, x_ref, low_ref, vec_ref, grad_ref, w_ref, *refs):
    out_ref, sums_ref, bsum_ref = refs
    tensor, dp = w_ref.shape[:2]
    width = w_ref.shape[3] // 3
    first = pl.program_id(0) == 0
    total = jnp.zeros(x_ref.shape, f32)
    for s in range(3):
        for t in range(tensor):
            w = w_ref[t, :, :part, s * width : (s + 1) * width].reshape(dp * part, width)
            total = total + matmul(grad_ref[s, :, t * width : (t + 1) * width], w, NT)
    back, gain_sum, shift_sum = norm_back(before(x_ref, count), vec_ref[0:1], total)
    out_ref[...] = (low_ref[...].astype(f32) + back).astype(bf16)
    accumulate(first, sums_ref, jnp.concatenate([gain_sum, shift_sum], axis=0))
    bias = [jnp.sum(grad_ref[s].astype(f32), axis=0, keepdims=True) for s in (0, 2)]
    accumulate(first, bsum_ref, jnp.concatenate(bias, axis=0))


def flip(value, mask):
    unit = 1
    while unit <= mask:
        if mask & unit:
            value = value + unit - 2 * unit * lax.rem(lax.div(value, unit), 2)
        unit *= 2
    return value


def differ(left, right, size):
    total, unit = 0, 1
    while unit < size:
        p, q = lax.rem(lax.div(left, unit), 2), lax.rem(lax.div(right, unit), 2)
        total = total + unit * (p + q - 2 * p * q)
        unit *= 2
    return total


def slot_grad_kernel(tensor, dp, starts, *refs):
    count, steps, depth = len(starts) - 1, starts[-1], dp // 4
    lefts, rights, outs = refs[:count], refs[count : 2 * count], refs[2 * count : 2 * count + 2 * tensor]
    total, keep, send, landed, send_sem, recv_sem = refs[2 * count + 2 * tensor :]
    step, t = pl.program_id(0), pl.program_id(1)
    d, y = lax.axis_index("dp"), lax.axis_index("tensor")
    part, block = total.shape[0] // dp, total.shape[1]
    column = differ(t, y, tensor)
    slots = pl.ds(column * (2 * depth), 2 * depth)

    def copy(step):
        cols = pl.ds(pl.multiple_of(step * block, block), block)
        return pltpu.make_async_remote_copy(
            src_ref=send.at[slots, :, cols],
            dst_ref=landed.at[slots, :, cols],
            send_sem=send_sem.at[step * tensor + t],
            recv_sem=recv_sem.at[step * tensor + t],
            device_id=(flip(d, 1), y),
            device_id_type=pl.DeviceIdType.MESH,
        )

    @pl.when((step == 0) & (t == 0))
    def _():
        barrier = pltpu.get_barrier_semaphore()
        pl.semaphore_signal(
            barrier, inc=1, device_id=(flip(d, 1), y), device_id_type=pl.DeviceIdType.MESH
        )
        pl.semaphore_wait(barrier, 1)

    for j in range(count):
        @pl.when((step >= starts[j]) & (step < starts[j + 1]))
        def _():
            total[...] = matmul(lefts[j][...], rights[j][0], TN)

    @pl.when(step < steps)
    def _():
        cols = pl.ds(pl.multiple_of(step * block, block), block)
        for r in range(dp):
            owner = pl.multiple_of(flip(d, r) * part, part)
            half = send if r & 1 else keep
            slot = column * (2 * depth) + ((r >> 1) & 1) * depth + (r >> 2)
            half[slot, :, cols] = total[pl.ds(owner, part), :].astype(bf16)
        copy(step).start()

    @pl.when(step > 0)
    def _():
        copy(step - 1).wait()
        cols = pl.ds(pl.multiple_of((step - 1) * block, block), block)
        for k in range(2 * tensor):
            @pl.when(column == k // 2)
            def _():
                own = pl.ds(k * depth, depth)
                both = keep[own, :, cols].astype(f32) + landed[own, :, cols].astype(f32)
                outs[k][...] = both.astype(bf16)


def slot_grads(name, pairs, tensor, dp, block, collective_id):
    rows, deep = pairs[0][0].shape
    part, depth = deep // dp, dp // 4
    block = min([block] + [right.shape[2] // tensor for _, right in pairs])
    pers = [right.shape[2] // tensor // block for _, right in pairs]
    starts = [0]
    for (_, right), per in zip(pairs, pers):
        starts.append(starts[-1] + right.shape[0] * per)
    wide = starts[-1] * block
    half = tensor * dp // 2

    def right_map(j, i, t):
        t = jnp.where(i < starts[j], 0, jnp.where(i >= starts[j + 1], tensor - 1, t))
        i = jnp.clip(i - starts[j], 0, starts[j + 1] - starts[j] - 1)
        return (i // pers[j], 0, t * pers[j] + i % pers[j])

    spec = pl.BlockSpec((depth, part, block), lambda i, t: (0, 0, jnp.maximum(i - 1, 0)))
    return call(
        functools.partial(slot_grad_kernel, tensor, dp, starts),
        name,
        (starts[-1] + 1, tensor),
        [full((rows, deep))] * len(pairs)
        + [pl.BlockSpec((1, rows, block), functools.partial(right_map, j)) for j in range(len(pairs))],
        [spec] * (2 * tensor),
        [((depth, part, wide), bf16)] * (2 * tensor),
        [left for left, _ in pairs] + [right for _, right in pairs],
        [pltpu.VMEM((deep, block), f32)]
        + [pltpu.VMEM((half, part, wide), bf16)] * 3
        + [pltpu.SemaphoreType.DMA((starts[-1] * tensor,))] * 2,
        collective_id=collective_id,
        has_side_effects=True,
    )


def swap(values, d, t, tensor, dp):
    moves = []
    for p in range(dp):
        for q in range(tensor):
            moves.append((p * tensor + q, (p ^ d) * tensor + (q ^ t)))
    return lax.ppermute(values, ("dp", "tensor"), moves)


def send_plane(parts, tensor, dp):
    return [swap(parts[k], 2 * (k % 2), k // 2, tensor, dp) for k in range(1, 2 * tensor)]


def sum_plane(part, landed, dp):
    planes = []
    for z in range(dp // 4):
        total = part[z].astype(f32)
        for piece in landed:
            total = total + piece[z].astype(f32)
        planes.append(total.astype(bf16))
    return planes


def send_line(planes, tensor, dp):
    return [swap(planes[z], 4 * z, 0, tensor, dp) for z in range(1, dp // 4)]


def pack_kernel(
    heads_ref, merge_ref, expand_ref, hb_ref, eb_ref, *refs
):
    small, (first_ref, later_ref) = refs[:-2], refs[-2:]
    _, part, own = heads_ref.shape
    for s in range(3):
        first_ref[:part, s * own : (s + 1) * own] = heads_ref[s]
    lines = [ref[...].astype(f32) for ref in small] + [jnp.zeros((8 - len(small), part), f32)]
    hb = hb_ref[...].astype(f32)
    hb = hb.reshape(hb.shape[0] * hb.shape[1], hb.shape[2])
    eb = eb_ref[...].astype(f32)
    pieces = []
    for piece in (jnp.concatenate(lines, axis=0), eb, hb):
        height, width = piece.shape
        if height < 8:
            piece = jnp.concatenate([piece, jnp.zeros((8 - height, width), f32)], axis=0)
        pieces.append(piece)
    used = sum(piece.shape[1] for piece in pieces)
    pieces.append(jnp.zeros((8, 128 - used), f32))
    first_ref[part:, :128] = jnp.concatenate(pieces, axis=1).astype(bf16)
    first_ref[part:, 128:] = jnp.zeros((8, 3 * own - 128), bf16)
    hidden = expand_ref.shape[1]
    later_ref[:, :hidden] = expand_ref[...]
    later_ref[:, hidden:] = merge_ref[...]


def gather_kernel(in_ref, out_ref, own_sem, send_sem, recv_sem):
    d, y = lax.axis_index("dp"), lax.axis_index("tensor")
    z, x, c = lax.div(d, 4), lax.rem(lax.div(d, 2), 2), lax.rem(d, 2)
    far_x, far_y, far_c = 1 - x, 1 - y, 1 - c
    barrier = pltpu.get_barrier_semaphore()

    def index(place):
        pz, px, pc, py = place
        return (pz * 2 + px) * 2 + pc, py

    lower, upper = (z - 1, x, c, y), (z + 1, x, c, y)
    to_x, to_y, to_c = (z, far_x, c, y), (z, x, c, far_y), (z, x, far_c, y)

    def greet(peer):
        pl.semaphore_signal(barrier, inc=1, device_id=index(peer), device_id_type=pl.DeviceIdType.MESH)

    for peer in (to_x, to_y, to_c):
        greet(peer)
    pl.when(z > 0)(lambda: greet(lower))
    pl.when(z < 3)(lambda: greet(upper))
    pl.semaphore_wait(barrier, 4 + lax.rem(lax.div(z + 1, 2), 2))

    sent = []

    def copy(owner, peer, slot, source=None):
        p, q = index(owner)
        return pltpu.make_async_remote_copy(
            src_ref=out_ref.at[q, p] if source is None else source,
            dst_ref=out_ref.at[q, p],
            send_sem=send_sem.at[slot],
            recv_sem=recv_sem.at[p * 2 + q],
            device_id=index(peer),
            device_id_type=pl.DeviceIdType.MESH,
        )

    def send(owner, peer, there, source=None):
        slot = len(sent)
        sent.append((owner, peer, slot, there))

        @pl.when(there)
        def _():
            copy(owner, peer, slot, source).start()

    def arrive(owner, there):
        @pl.when(there)
        def _():
            copy(owner, to_c, 0).wait_recv()

    own = (z, x, c, y)
    keep = pltpu.make_async_copy(in_ref, out_ref.at[y, d], own_sem)
    send(own, upper, z < 3, in_ref)
    send(own, lower, z > 0, in_ref)
    for peer in (to_x, to_y, to_c):
        send(own, peer, z >= 0, in_ref)
    keep.start()
    for far in range(1, 4):
        for sign, after, onward in ((-1, upper, z < 3), (1, lower, z > 0)):
            level = z + sign * far
            there = (level >= 0) & (level <= 3)
            block = (level, x, c, y)
            arrive(block, there)
            send(block, after, there & onward)
            for peer in (to_x, to_y, to_c):
                send(block, peer, there)
    for far in range(4):
        for sign in (-1, 1) if far else (1,):
            level = z + sign * far
            there = (level >= 0) & (level <= 3)
            odd = lax.rem(level + 4, 2)
            block = (level, far_x, c, y)
            arrive(block, there)
            send(block, to_y, there & (odd == 0))
            send(block, to_c, there)
            block = (level, x, c, far_y)
            arrive(block, there)
            send(block, to_x, there & (odd == 1))
            send(block, to_c, there)
    for far in range(4):
        for sign in (-1, 1) if far else (1,):
            level = z + sign * far
            there = (level >= 0) & (level <= 3)
            block = (level, far_x, c, far_y)
            arrive(block, there)
            send(block, to_c, there)
    for level in range(4):
        for px in range(2):
            for py in range(2):
                arrive((level, px, far_c, py), z >= 0)
    for owner, peer, slot, there in sent:
        pl.when(there)(lambda: copy(owner, peer, slot).wait_send())
    keep.wait()


def gather_first(shard, tensor, dp):
    shape = (tensor, dp) + shard.shape
    if (tensor, dp) != (2, 16):
        return lax.all_gather(shard, AXES, axis=0, tiled=True).reshape(shape)
    return call(
        gather_kernel,
        "gather",
        (),
        [pl.BlockSpec(memory_space=pltpu.VMEM)],
        [pl.BlockSpec(memory_space=pl.ANY)],
        [(shape, bf16)],
        (shard,),
        [pltpu.SemaphoreType.DMA, pltpu.SemaphoreType.DMA((64,)), pltpu.SemaphoreType.DMA((32,))],
        collective_id=1,
        has_side_effects=True,
    )[0]


def last_kernel(dp, tensor, act_ref, resid_ref, vec_ref, w_ref, *refs):
    count, depth = dp * tensor, dp // 4
    own_ref, others, refs = refs[0], refs[1 : 2 * tensor], refs[2 * tensor :]
    one_ref, two_ref, hb_ref, eb_ref, out_ref, heads_ref, sums_ref = refs[:7]
    packed, landed, line, arrived, send_sem, recv_sem, line_send, line_recv = refs[7:]
    step = pl.program_id(0)
    d, y = lax.axis_index("dp"), lax.axis_index("tensor")
    me = d * tensor + y
    part = own_ref.shape[1]
    barrier = pltpu.get_barrier_semaphore()

    def place(k):
        other = lax.rem(me + k, count)
        return other, (lax.div(other, tensor), lax.rem(other, tensor))

    def greet(k, carry):
        _, where = place(k)
        pl.semaphore_signal(barrier, inc=1, device_id=where, device_id_type=pl.DeviceIdType.MESH)
        return carry

    def plane(z):
        total = own_ref[z].astype(f32)
        for ref in others:
            total = total + ref[z].astype(f32)
        return total

    @pl.when(step == 0)
    def _():
        lax.fori_loop(1, count, greet, 0)
        for z in range(1, depth):
            line[z - 1] = plane(z).astype(bf16)
        heads = hb_ref.shape[1] // HEAD_DIM
        own_heads, hb_wide = heads // tensor, HEAD_DIM // dp
        eb_tall, eb_wide = eb_ref.shape[0] // tensor, eb_ref.shape[1] // dp
        hb = [
            hb_ref[k : k + 1, h * HEAD_DIM : (h + 1) * HEAD_DIM] for k in range(2) for h in range(heads)
        ]
        hb = jnp.concatenate(hb, axis=0).T
        eb = eb_ref[...].T
        sums = jnp.concatenate([one_ref[...], two_ref[3:4], two_ref[1:3], two_ref[0:1]], axis=0)
        for p in range(dp):
            piece = sums[:, p * part : (p + 1) * part]
            for q in range(tensor):
                packed[p * tensor + q, 0:6, 0:part] = piece
                packed[p * tensor + q, 0:eb_wide, part : part + eb_tall] = eb[
                    p * eb_wide : (p + 1) * eb_wide, q * eb_tall : (q + 1) * eb_tall
                ]
                for k in range(2):
                    lane = part + eb_tall + k * own_heads
                    packed[p * tensor + q, 0:hb_wide, lane : lane + own_heads] = hb[
                        p * hb_wide : (p + 1) * hb_wide,
                        k * heads + q * own_heads : k * heads + (q + 1) * own_heads,
                    ]

    copies = [
        pltpu.make_async_remote_copy(
            src_ref=line.at[z - 1],
            dst_ref=arrived.at[z - 1],
            send_sem=line_send.at[z - 1],
            recv_sem=line_recv.at[z - 1],
            device_id=(flip(d, 4 * z), y),
            device_id_type=pl.DeviceIdType.MESH,
        )
        for z in range(1, depth)
    ]

    def copy(k):
        other, where = place(k)
        return pltpu.make_async_remote_copy(
            src_ref=packed.at[other],
            dst_ref=landed.at[k],
            send_sem=send_sem.at[k],
            recv_sem=recv_sem.at[k],
            device_id=where,
            device_id_type=pl.DeviceIdType.MESH,
        )

    def start(k, carry):
        copy(k).start()
        return carry

    @pl.when(step == 1)
    def _():
        pl.semaphore_wait(barrier, count - 1)
        lax.fori_loop(1, count, start, 0)
        for item in copies:
            item.start()

    total = resid_ref[...] + vec_ref[5:6]
    width = w_ref.shape[3]
    for t in range(tensor):
        w = w_ref[t].reshape(dp * part, width)
        total = total + matmul(act_ref[:, t * width : (t + 1) * width], w, NT)
    out_ref[...] = total.astype(bf16)

    def finish(k, sums):
        copy(k).wait()
        return sums + landed[k]

    @pl.when(step == pl.num_programs(0) - 1)
    def _():
        sums_ref[...] = lax.fori_loop(1, count, finish, packed[me])
        total = plane(0)
        for item, z in zip(copies, range(1, depth)):
            item.wait()
            total = total + arrived[z - 1].astype(f32)
        own = heads_ref.shape[2]
        for s in range(3):
            heads_ref[s] = total[:, s * own : (s + 1) * own]


def finish_kernel(depth, *refs):
    given_ref, *refs = refs
    sums_ref, heads_ref, reduced_ref, *refs = refs
    planes, refs = refs[:depth], refs[depth:]
    copy_ref, *refs = refs
    copy_ref[...] = given_ref[...]
    reduce_ref, expand_ref, merge_ref, out_ref, hb_ref, eb_ref, *vectors = refs
    total = planes[0][...].astype(f32)
    for ref in planes[1:]:
        total = total + ref[...].astype(f32)
    hidden = expand_ref.shape[1]
    expand_ref[...] = total[:, :hidden]
    merge_ref[...] = total[:, hidden:]
    reduce_ref[...] = reduced_ref[...].astype(f32)
    out_ref[...] = heads_ref[...]
    part = vectors[0].shape[1]
    for r, ref in enumerate(vectors):
        ref[...] = sums_ref[r : r + 1, :part]
    wide, tall = eb_ref.shape
    eb_ref[...] = sums_ref[:wide, part : part + tall]
    wide, count = hb_ref.shape[1:]
    for k in range(2):
        lane = part + tall + k * count
        hb_ref[k] = sums_ref[:wide, lane : lane + count]


def shards(
    tensor,
    dp,
    activations,
    first_gain,
    first_shift,
    heads_weight,
    heads_bias,
    merge_weight,
    merge_bias,
    second_gain,
    second_shift,
    expand_weight,
    expand_bias,
    reduce_weight,
    reduce_bias,
    output_grad,
    real_images,
):
    rows, deep = activations.shape
    images = rows // SEQ
    part = deep // dp
    own = heads_weight.shape[2]
    hidden_own = expand_weight.shape[1]
    hidden = hidden_own * tensor
    heads = deep // HEAD_DIM
    least = (images - 1) * STRIDE + WINDOW
    blocks = -(-least // 512)
    block = -(-least // blocks // 16) * 16
    total_rows = block * blocks

    def gather(shard):
        out = lax.all_gather(shard, AXES, axis=0, tiled=True)
        return out.reshape(tensor, dp, *shard.shape)

    small = [first_gain, first_shift, merge_bias, second_gain, second_shift, reduce_bias]
    arrays = [
        heads_weight, merge_weight.T, expand_weight,
        heads_bias.transpose(0, 2, 1), expand_bias.T,
    ] + [v.reshape(1, part) for v in small]
    vmem = pl.BlockSpec(memory_space=pltpu.VMEM)
    first, later = call(
        pack_kernel, "pack", (), [vmem] * len(arrays), [vmem] * 2,
        [((part + 8, 3 * own), bf16), ((part, hidden_own + own), bf16)], arrays,
    )
    wide = gather(later)
    wide_heads = gather_first(first, tensor, dp)
    wide_heads, turned = lax.optimization_barrier((wide_heads, reduce_weight.T))
    wide_reduce = gather(turned)

    hbs, ebs = heads_bias.shape, expand_bias.shape
    small = wide_heads[:, :, part:, :128].astype(f32)
    vectors = small[0, :, :6, :part].transpose(1, 0, 2).reshape(6, deep)
    eb = small[:, :, : ebs[1], part : part + ebs[0]].transpose(0, 3, 1, 2).reshape(1, hidden)
    hb = small[:, :, : 2 * hbs[2], part + ebs[0] : part + ebs[0] + hbs[1]]
    hb = hb.reshape(tensor, dp, 2, hbs[2], hbs[1]).transpose(2, 0, 4, 1, 3).reshape(2, deep)
    live = jnp.clip(real_images - lax.axis_index("tensor") * images, 0, images) * SEQ

    def by_rows(width):
        return pl.BlockSpec((block, width), lambda i, *_: (i, 0))

    def columns(array, index, width):
        shape = array.shape[:3] + (width,)
        return pl.BlockSpec(shape, lambda *_: (0, 0, 0, index), pipeline_mode=pl.Buffered(1))

    vec = full((6, deep))
    expand_spec, merge_spec = columns(wide, 0, hidden_own), columns(wide, hidden_own // own, own)
    triple_spec = pl.BlockSpec((3, block, deep), lambda i: (0, i, 0))
    normed_one, triple = call(
        functools.partial(qkv_kernel, part, rows),
        "qkv",
        (blocks,),
        [by_rows(deep), vec, full((2, deep)), full(wide_heads.shape)],
        [by_rows(deep), triple_spec],
        [((total_rows, deep), bf16), ((3, total_rows, deep), bf16)],
        (activations, vectors, hb, wide_heads),
        flops=total_rows * deep * deep * 3,
    )

    group = 4
    groups = heads // group
    panel = group * HEAD_DIM
    head_spec = pl.BlockSpec((3, total_rows, panel), lambda g, i: (0, 0, g))
    ctx_spec = pl.BlockSpec((total_rows, panel), lambda g, i: (0, g))
    stat_spec = pl.BlockSpec((1, group, WINDOW), lambda g, i: (g * images + i, 0, 0))
    attend_flops = images * heads * WINDOW * 768 * 256 * 2
    context, stat = call(
        attend_kernel,
        "attend",
        (groups, images),
        [head_spec],
        [ctx_spec, stat_spec],
        [((total_rows, deep), bf16), ((images * groups, group, WINDOW), f32)],
        (triple,),
        flops=attend_flops,
    )

    resid, normed_two = call(
        functools.partial(merge_kernel, rows),
        "merge",
        (blocks,),
        [by_rows(deep), by_rows(deep), vec, merge_spec],
        [by_rows(deep), by_rows(deep)],
        [((total_rows, deep), f32), ((total_rows, deep), bf16)],
        (context, activations, vectors, wide),
        flops=total_rows * deep * deep,
    )

    chunk = min(512, hidden_own)
    per = hidden_own // chunk
    chunk_spec = pl.BlockSpec((total_rows, chunk), lambda c, *_: (0, c))
    shard_spec = pl.BlockSpec((1, dp, part, chunk), lambda c, *_: (c // per, 0, 0, c % per))
    active, slope, grad_reduce = call(
        expand_kernel,
        "expand",
        (hidden // chunk,),
        [
            full((total_rows, deep)), full((rows, deep)),
            pl.BlockSpec((1, chunk), lambda c, *_: (0, c)), shard_spec,
        ],
        [chunk_spec, chunk_spec, shard_spec],
        [
            ((total_rows, hidden), bf16), ((total_rows, hidden), bf16),
            ((tensor, dp, part, hidden_own), bf16),
        ],
        (live, normed_two, output_grad, eb, wide),
        [pltpu.VMEM((total_rows, deep), bf16)],
        flops=total_rows * deep * hidden * 2,
        prefetch=1,
    )
    grad_reduce = grad_reduce.reshape(tensor * dp * part, hidden_own)
    grad_reduce = lax.psum_scatter(grad_reduce, AXES, scatter_dimension=0, tiled=True)

    back_chunk = min(512, hidden_own)
    pre_grad, resid_low, grad_context, sums_two, esum = call(
        functools.partial(mlp_back_kernel, back_chunk),
        "mlp_back",
        (blocks,),
        [
            by_rows(deep), by_rows(hidden), by_rows(deep), vec,
            expand_spec, full(wide_reduce.shape), merge_spec,
        ],
        [
            by_rows(hidden), by_rows(deep), by_rows(deep),
            pl.BlockSpec((4, deep), lambda *_: (0, 0)), pl.BlockSpec((hidden // 128, 128), lambda *_: (0, 0)),
        ],
        [
            ((total_rows, hidden), bf16), ((total_rows, deep), bf16), ((total_rows, deep), bf16),
            ((4, deep), f32), ((hidden // 128, 128), f32),
        ],
        (live, output_grad, slope, resid, vectors, wide, wide_reduce, wide),
        prefetch=1,
    )
    parts = slot_grads(
        "middle_grad", [(normed_two, pre_grad[None]), (resid_low, context[None])], tensor, dp, 512, 2
    )
    *parts, grad_context = lax.optimization_barrier((*parts, grad_context))
    landed = send_plane(parts, tensor, dp)
    grad_triple = call(
        attend_back_kernel,
        "attend_back",
        (groups, images),
        [head_spec, stat_spec, ctx_spec],
        [head_spec],
        [((3, total_rows, deep), bf16)],
        (triple, stat, grad_context),
    )[0]
    heads = slot_grads("heads_grad", [(normed_one, grad_triple)], tensor, dp, 512, 3)
    held = (tuple(heads), tuple(landed), parts[0], resid_low)
    heads, landed, part_own, resid_low = lax.optimization_barrier(held)
    last = send_plane(heads, tensor, dp)
    planes = sum_plane(part_own, landed, dp)
    planes, resid_low = lax.optimization_barrier((tuple(planes), resid_low))
    line = send_line(planes, tensor, dp)

    def whole(shape):
        return pl.BlockSpec(shape, lambda *_: (0,) * len(shape))

    shapes = [(2, deep), (2, deep)]
    input_grad, sums_one, bsum = call(
        functools.partial(qkv_back_kernel, part, rows),
        "qkv_back",
        (blocks,),
        [by_rows(deep), by_rows(deep), vec, triple_spec, full(wide_heads.shape)],
        [by_rows(deep)] + [whole(shape) for shape in shapes],
        [((rows, deep), bf16)] + [(shape, f32) for shape in shapes],
        (activations, resid_low, vectors, grad_triple, wide_heads),
        flops=total_rows * deep * deep * 3,
    )

    hbs, ebs = heads_bias.shape, expand_bias.shape
    depth = dp // 4
    arrays = [heads[0], *last, sums_one, sums_two, bsum, esum]
    output, heads_sum, sums = call(
        functools.partial(last_kernel, dp, tensor),
        "reduce",
        (blocks,),
        [by_rows(hidden), by_rows(deep), vec, full(wide_reduce.shape)] + [full(v.shape) for v in arrays],
        [by_rows(deep), whole((3, part, own)), whole((8, 128))],
        [((rows, deep), bf16), ((3, part, own), f32), ((8, 128), f32)],
        (active, resid, vectors, wide_reduce, *arrays),
        [
            pltpu.VMEM((tensor * dp, 8, 128), f32), pltpu.VMEM((tensor * dp, 8, 128), f32),
            pltpu.VMEM((depth - 1, part, 3 * own), bf16), pltpu.VMEM((depth - 1, part, 3 * own), bf16),
            pltpu.SemaphoreType.DMA((tensor * dp,)), pltpu.SemaphoreType.DMA((tensor * dp,)),
            pltpu.SemaphoreType.DMA((depth - 1,)), pltpu.SemaphoreType.DMA((depth - 1,)),
        ],
        flops=total_rows * deep * hidden,
        collective_id=0,
        has_side_effects=True,
    )
    shapes = [(part, hidden_own), (part, hidden_own), (part, own)]
    shapes += [heads_sum.shape, (2, hbs[2], hbs[1]), ebs[::-1]] + [(1, part)] * 6
    arrays = [sums, heads_sum, grad_reduce, planes[0], *line]
    piece = pl.BlockSpec((total_rows // 2, deep), lambda i: (i, 0))
    output, grad_reduce, grad_expand, grad_merge, grad_heads, hb_grad, eb_grad, *vector = call(
        functools.partial(finish_kernel, depth),
        "finish",
        (2,),
        [piece] + [full(v.shape) for v in arrays],
        [piece] + [whole(shape) for shape in shapes],
        [((rows, deep), bf16)] + [(shape, f32) for shape in shapes],
        [output] + arrays,
    )
    vector = [v.reshape(part) for v in vector]

    return (
        output,
        input_grad,
        vector[0],
        vector[1],
        grad_heads,
        hb_grad.transpose(0, 2, 1),
        grad_merge.T,
        vector[2],
        vector[3],
        vector[4],
        grad_expand,
        eb_grad.T,
        grad_reduce.T,
        vector[5],
    )


def solution(mesh):
    rows = P(("dp", "tensor"), None)
    specs = (
        P("dp"),
        P("dp"),
        P(None, "dp", "tensor"),
        P(None, "tensor", "dp"),
        P("tensor", "dp"),
        P("dp"),
        P("dp"),
        P("dp"),
        P("dp", "tensor"),
        P("tensor", "dp"),
        P("tensor", "dp"),
        P("dp"),
    )
    return jax.shard_map(
        functools.partial(shards, mesh.shape["tensor"], mesh.shape["dp"]),
        mesh=mesh,
        in_specs=(rows,) + specs + (rows, P("dp")),
        out_specs=(rows, rows) + specs,
        check_vma=False,
    )
```

```python
import functools
import math

import jax
import jax.numpy as jnp
from jax import lax
from jax.experimental import pallas as pl
from jax.experimental.pallas import tpu as pltpu
from jax.sharding import PartitionSpec as P

HEAD_DIM = 64
SEQ = 577
STRIDE = 576
WINDOW = 592
LANES = 640
EPSILON = 1e-06
LOG_SCALE = 0.125
bf16 = jnp.bfloat16
f32 = jnp.float32
NN = (((1,), (0,)), ((), ()))
NT = (((1,), (1,)), ((), ()))
TN = (((0,), (0,)), ((), ()))
AXES = ("tensor", "dp")


def matmul(left, right, dims=NN):
    return lax.dot_general(left, right, dims, preferred_element_type=f32)


def norm_parts(values):
    center = values - jnp.mean(values, axis=-1, keepdims=True)
    second = jnp.mean(center * center, axis=-1, keepdims=True)
    inv = lax.rsqrt(second + EPSILON)
    return center * inv, inv


def gelu_and_slope(pre):
    phi = 0.5 + 0.5 * lax.erf(pre * 0.7071067811865476)
    bell = jnp.exp(pre * pre * -0.5)
    return pre * phi, phi + pre * (bell * 0.3989422804014327)


def full(shape):
    return pl.BlockSpec(shape, lambda *_: (0,) * len(shape), pipeline_mode=pl.Buffered(1))


def call(kernel, name, grid, in_specs, out_specs, out_shape, args, scratch=(), flops=0, prefetch=0, **params):
    moved = 0
    if flops:
        moved = sum(a.size * a.dtype.itemsize for a in args)
        moved += sum(math.prod(shape) * jnp.dtype(dtype).itemsize for shape, dtype in out_shape)
    return pl.pallas_call(
        kernel,
        grid_spec=pltpu.PrefetchScalarGridSpec(
            num_scalar_prefetch=prefetch,
            grid=grid,
            in_specs=in_specs,
            out_specs=out_specs,
            scratch_shapes=list(scratch),
        ),
        out_shape=[jax.ShapeDtypeStruct(shape, dtype) for shape, dtype in out_shape],
        compiler_params=pltpu.CompilerParams(vmem_limit_bytes=60 * 2**20, **params),
        cost_estimate=pl.CostEstimate(flops=2 * flops, bytes_accessed=moved, transcendentals=0),
        name=name,
    )(*args)


def before(ref, count):
    height = ref.shape[0]
    rows = pl.program_id(0) * height + lax.broadcasted_iota(jnp.int32, (height, 1), 0)
    return jnp.where(rows < count, ref[...].astype(f32), 0.0)


def qkv_kernel(part, count, x_ref, vec_ref, bias_ref, w_ref, normed_ref, triple_ref):
    hat, _ = norm_parts(before(x_ref, count))
    normed = (hat * vec_ref[0:1] + vec_ref[1:2]).astype(bf16)
    normed_ref[...] = normed
    tensor, dp = w_ref.shape[:2]
    width = w_ref.shape[3] // 3
    for s in range(3):
        for t in range(tensor):
            cols = slice(t * width, (t + 1) * width)
            w = w_ref[t, :, :part, s * width : (s + 1) * width].reshape(dp * part, width)
            out = matmul(normed, w)
            if s != 1:
                out = out + bias_ref[s // 2 : s // 2 + 1, cols]
            triple_ref[s, :, cols] = out.astype(bf16)


def window(image):
    start = pl.multiple_of(image * STRIDE, 16)
    return pl.ds(start, WINDOW)


def keep_before(image, ref, index, value):
    edge = pl.ds(pl.multiple_of(image * STRIDE, 16), 16)
    rest = pl.ds(pl.multiple_of(image * STRIDE + 16, 16), WINDOW - 16)
    rows = lax.broadcasted_iota(jnp.int32, (16, 1), 0)
    head = jnp.where(rows < image, ref[(*index[:-1], edge, index[-1])].astype(f32), value[:16])
    ref[(*index[:-1], edge, index[-1])] = head.astype(ref.dtype)
    ref[(*index[:-1], rest, index[-1])] = value[16:].astype(ref.dtype)


def two_heads(first, second):
    blank, below = jnp.zeros_like(first), jnp.zeros((LANES - WINDOW, 2 * HEAD_DIM), first.dtype)
    return jnp.concatenate(
        [
            jnp.concatenate([first, blank], axis=1), below,
            jnp.concatenate([blank, second], axis=1), below,
        ],
        axis=0,
    )


def head_columns(h):
    return (
        slice(HEAD_DIM * h, HEAD_DIM * (h + 2)),
        (slice(HEAD_DIM * h, HEAD_DIM * (h + 1)), slice(HEAD_DIM * (h + 1), HEAD_DIM * (h + 2))),
    )


def attend_kernel(triple_ref, context_ref, stat_ref):
    image = pl.program_id(1)
    lanes = lax.broadcasted_iota(jnp.int32, (1, LANES), 1)
    mask = jnp.where((lanes >= image) & (lanes < image + SEQ), 0.0, -1e30)
    own = window(image)
    left = lax.broadcasted_iota(jnp.int32, (1, 2 * HEAD_DIM), 1) < HEAD_DIM
    stats = []
    for h in range(0, triple_ref.shape[2] // HEAD_DIM, 2):
        pair, single = head_columns(h)
        keys = two_heads(*(triple_ref[1, own, cols] for cols in single))
        both = matmul(triple_ref[0, own, pair] * bf16(LOG_SCALE), keys, NT)
        probs, scale = [], []
        for u in range(2):
            scores = both[:, u * LANES : (u + 1) * LANES] + mask
            top = jnp.max(scores, axis=1, keepdims=True)
            expo = jnp.exp(scores - top)
            total = jnp.sum(expo, axis=1, keepdims=True)
            probs.append(expo.astype(bf16))
            scale.append(1.0 / total)
            stats.append(top + jnp.log(total))
        values = two_heads(*(triple_ref[2, own, cols] for cols in single))
        context = matmul(jnp.concatenate(probs, axis=1), values)
        keep_before(image, context_ref, (pair,), context * jnp.where(left, *scale))
    stat_ref[0] = jnp.concatenate(stats, axis=1).T


def attend_back_kernel(triple_ref, stat_ref, grad_ref, out_ref):
    image = pl.program_id(1)
    rows = lax.broadcasted_iota(jnp.int32, (WINDOW, 1), 0)
    mask = jnp.where((rows >= image) & (rows < image + SEQ), 0.0, -1e30)
    lanes = lax.broadcasted_iota(jnp.int32, (1, LANES), 1)
    real = (lanes >= image) & (lanes < image + SEQ)
    own = window(image)
    for h in range(0, triple_ref.shape[2] // HEAD_DIM, 2):
        pair, single = head_columns(h)
        keys = triple_ref[1, own, pair]
        queries = [triple_ref[0, own, cols] for cols in single]
        grads = [grad_ref[own, cols] for cols in single]
        both = matmul(keys, two_heads(*queries) * bf16(LOG_SCALE), NT)
        both_grad = matmul(triple_ref[2, own, pair], two_heads(*grads), NT)
        turned = keys.T
        value_grad, key_grad, query_grad = [], [], []
        for u in range(2):
            side = slice(u * LANES, (u + 1) * LANES)
            stat = jnp.concatenate(
                [stat_ref[0, h + u : h + u + 1, :], jnp.zeros((1, LANES - WINDOW), f32)], axis=1
            )
            probs = jnp.exp(both[:, side] + mask - jnp.where(real, stat, 1e30))
            grad_probs = both_grad[:, side]
            inner = jnp.sum(probs * grad_probs, axis=0, keepdims=True)
            grad_scores = (probs * (grad_probs - inner)).astype(bf16)
            out = matmul(
                jnp.concatenate([probs.astype(bf16), grad_scores], axis=1),
                two_heads(grads[u], queries[u]),
            )
            value_grad.append(out[:, :HEAD_DIM])
            key_grad.append(out[:, HEAD_DIM:])
            query_grad.append(matmul(turned[u * HEAD_DIM : (u + 1) * HEAD_DIM], grad_scores))
        keep_before(image, out_ref, (2, pair), jnp.concatenate(value_grad, axis=1))
        keep_before(image, out_ref, (1, pair), jnp.concatenate(key_grad, axis=1) * LOG_SCALE)
        query_grad = jnp.concatenate(query_grad, axis=0).T[:WINDOW]
        keep_before(image, out_ref, (0, pair), query_grad * LOG_SCALE)


def merge_kernel(count, ctx_ref, x_ref, vec_ref, w_ref, resid_ref, normed_ref):
    tensor, dp, part, width = w_ref.shape
    total = before(x_ref, count) + vec_ref[2:3]
    for t in range(tensor):
        w = w_ref[t].reshape(dp * part, width)
        total = total + matmul(ctx_ref[:, t * width : (t + 1) * width], w, NT)
    resid_ref[...] = total
    hat, _ = norm_parts(total)
    normed_ref[...] = (hat * vec_ref[3:4] + vec_ref[4:5]).astype(bf16)


def expand_kernel(live_ref, normed_ref, given_ref, bias_ref, w_ref, act_ref, slope_ref, out_ref, grad_ref):
    @pl.when(pl.program_id(0) == 0)
    def _():
        count = given_ref.shape[0]
        even = count // 16 * 16
        rows = lax.broadcasted_iota(jnp.int32, (count, 1), 0)
        grad_ref[:even] = jnp.where(rows[:even] < live_ref[0], given_ref[:even], bf16(0))
        grad_ref[even:] = jnp.zeros((grad_ref.shape[0] - even, grad_ref.shape[1]), bf16)
        rest = jnp.where(rows[even:] < live_ref[0], given_ref[even:].astype(f32), 0.0)
        grad_ref[even:count] = rest.astype(bf16)

    _, dp, part, width = w_ref.shape
    w = w_ref[0].reshape(dp * part, width)
    active, slope = gelu_and_slope(matmul(normed_ref[...], w) + bias_ref[...])
    active = active.astype(bf16)
    act_ref[...] = active
    slope_ref[...] = slope.astype(bf16)
    out_ref[...] = matmul(grad_ref[...], active, TN).astype(bf16).reshape(out_ref.shape)


def accumulate(first, ref, value):
    @pl.when(first)
    def _():
        ref[...] = value

    @pl.when(jnp.logical_not(first))
    def _():
        ref[...] += value


def norm_back(values, gain, grad):
    hat, inv = norm_parts(values)
    scaled = grad * gain
    back = (
        scaled
        - jnp.mean(scaled, axis=-1, keepdims=True)
        - hat * jnp.mean(scaled * hat, axis=-1, keepdims=True)
    ) * inv
    return back, jnp.sum(grad * hat, axis=0, keepdims=True), jnp.sum(grad, axis=0, keepdims=True)


def mlp_back_kernel(
    chunk, live_ref, given_ref, slope_ref, resid_ref, vec_ref, e_ref, r_ref, m_ref,
    pre_ref, low_ref, ctx_ref, sums_ref, esum_ref,
):
    tensor, dp, rows, width = e_ref.shape
    first = pl.program_id(0) == 0
    given = before(given_ref, live_ref[0])
    grad = given.astype(bf16)
    total = jnp.zeros(grad.shape, f32)
    parts = []
    for t in range(tensor):
        for c in range(width // chunk):
            local = slice(c * chunk, (c + 1) * chunk)
            cols = slice(t * width + c * chunk, t * width + (c + 1) * chunk)
            r = r_ref[t, :, :, local].reshape(dp * rows, chunk)
            pre = (matmul(grad, r) * slope_ref[:, cols].astype(f32)).astype(bf16)
            pre_ref[:, cols] = pre
            parts.append(jnp.sum(pre.astype(f32), axis=0, keepdims=True))
            e = e_ref[t, :, :, local].reshape(dp * rows, chunk)
            total = total + matmul(pre, e, NT)
    sums = 0
    half = grad.shape[0] // 2
    for rows_half in (slice(0, half), slice(half, 2 * half)):
        own = given[rows_half]
        back, gain_sum, shift_sum = norm_back(resid_ref[rows_half], vec_ref[3:4], total[rows_half])
        resid_grad = own + back
        low_ref[rows_half] = resid_grad.astype(bf16)
        lines = [jnp.sum(own, axis=0, keepdims=True), gain_sum, shift_sum]
        sums = sums + jnp.concatenate(lines + [jnp.sum(resid_grad, axis=0, keepdims=True)], axis=0)
    low = low_ref[...]
    wide = m_ref.shape[3]
    for t in range(tensor):
        m = m_ref[t].reshape(dp * rows, wide)
        ctx_ref[:, t * wide : (t + 1) * wide] = matmul(low, m).astype(bf16)
    accumulate(first, sums_ref, sums)
    parts = jnp.concatenate(parts, axis=1)
    lines = [parts[:, k * 128 : (k + 1) * 128] for k in range(esum_ref.shape[0])]
    accumulate(first, esum_ref, jnp.concatenate(lines, axis=0))


def qkv_back_kernel(part, count, x_ref, low_ref, vec_ref, grad_ref, w_ref, *refs):
    out_ref, sums_ref, bsum_ref = refs
    tensor, dp = w_ref.shape[:2]
    width = w_ref.shape[3] // 3
    first = pl.program_id(0) == 0
    total = jnp.zeros(x_ref.shape, f32)
    for s in range(3):
        for t in range(tensor):
            w = w_ref[t, :, :part, s * width : (s + 1) * width].reshape(dp * part, width)
            total = total + matmul(grad_ref[s, :, t * width : (t + 1) * width], w, NT)
    back, gain_sum, shift_sum = norm_back(before(x_ref, count), vec_ref[0:1], total)
    out_ref[...] = (low_ref[...].astype(f32) + back).astype(bf16)
    accumulate(first, sums_ref, jnp.concatenate([gain_sum, shift_sum], axis=0))
    bias = [jnp.sum(grad_ref[s].astype(f32), axis=0, keepdims=True) for s in (0, 2)]
    accumulate(first, bsum_ref, jnp.concatenate(bias, axis=0))


def flip(value, mask):
    unit = 1
    while unit <= mask:
        if mask & unit:
            value = value + unit - 2 * unit * lax.rem(lax.div(value, unit), 2)
        unit *= 2
    return value


def differ(left, right, size):
    total, unit = 0, 1
    while unit < size:
        p, q = lax.rem(lax.div(left, unit), 2), lax.rem(lax.div(right, unit), 2)
        total = total + unit * (p + q - 2 * p * q)
        unit *= 2
    return total


def slot_grad_kernel(tensor, dp, starts, *refs):
    count, steps, depth = len(starts) - 1, starts[-1], dp // 4
    lefts, rights, outs = refs[:count], refs[count : 2 * count], refs[2 * count : 2 * count + 2 * tensor]
    total, keep, send, landed, send_sem, recv_sem = refs[2 * count + 2 * tensor :]
    step, t = pl.program_id(0), pl.program_id(1)
    d, y = lax.axis_index("dp"), lax.axis_index("tensor")
    part, block = total.shape[0] // dp, total.shape[1]
    column = differ(t, y, tensor)
    slots = pl.ds(column * (2 * depth), 2 * depth)

    def copy(step):
        cols = pl.ds(pl.multiple_of(step * block, block), block)
        return pltpu.make_async_remote_copy(
            src_ref=send.at[slots, :, cols],
            dst_ref=landed.at[slots, :, cols],
            send_sem=send_sem.at[step * tensor + t],
            recv_sem=recv_sem.at[step * tensor + t],
            device_id=(flip(d, 1), y),
            device_id_type=pl.DeviceIdType.MESH,
        )

    @pl.when((step == 0) & (t == 0))
    def _():
        barrier = pltpu.get_barrier_semaphore()
        pl.semaphore_signal(
            barrier, inc=1, device_id=(flip(d, 1), y), device_id_type=pl.DeviceIdType.MESH
        )
        pl.semaphore_wait(barrier, 1)

    for j in range(count):
        @pl.when((step >= starts[j]) & (step < starts[j + 1]))
        def _():
            total[...] = matmul(lefts[j][...], rights[j][0], TN)

    @pl.when(step < steps)
    def _():
        cols = pl.ds(pl.multiple_of(step * block, block), block)
        for r in range(dp):
            owner = pl.multiple_of(flip(d, r) * part, part)
            half = send if r & 1 else keep
            slot = column * (2 * depth) + ((r >> 1) & 1) * depth + (r >> 2)
            half[slot, :, cols] = total[pl.ds(owner, part), :].astype(bf16)
        copy(step).start()

    @pl.when(step > 0)
    def _():
        copy(step - 1).wait()
        cols = pl.ds(pl.multiple_of((step - 1) * block, block), block)
        for k in range(2 * tensor):
            @pl.when(column == k // 2)
            def _():
                own = pl.ds(k * depth, depth)
                both = keep[own, :, cols].astype(f32) + landed[own, :, cols].astype(f32)
                outs[k][...] = both.astype(bf16)


def slot_grads(name, pairs, tensor, dp, block, collective_id):
    rows, deep = pairs[0][0].shape
    part, depth = deep // dp, dp // 4
    block = min([block] + [right.shape[2] // tensor for _, right in pairs])
    pers = [right.shape[2] // tensor // block for _, right in pairs]
    starts = [0]
    for (_, right), per in zip(pairs, pers):
        starts.append(starts[-1] + right.shape[0] * per)
    wide = starts[-1] * block
    half = tensor * dp // 2

    def right_map(j, i, t):
        t = jnp.where(i < starts[j], 0, jnp.where(i >= starts[j + 1], tensor - 1, t))
        i = jnp.clip(i - starts[j], 0, starts[j + 1] - starts[j] - 1)
        return (i // pers[j], 0, t * pers[j] + i % pers[j])

    spec = pl.BlockSpec((depth, part, block), lambda i, t: (0, 0, jnp.maximum(i - 1, 0)))
    return call(
        functools.partial(slot_grad_kernel, tensor, dp, starts),
        name,
        (starts[-1] + 1, tensor),
        [full((rows, deep))] * len(pairs)
        + [pl.BlockSpec((1, rows, block), functools.partial(right_map, j)) for j in range(len(pairs))],
        [spec] * (2 * tensor),
        [((depth, part, wide), bf16)] * (2 * tensor),
        [left for left, _ in pairs] + [right for _, right in pairs],
        [pltpu.VMEM((deep, block), f32)]
        + [pltpu.VMEM((half, part, wide), bf16)] * 3
        + [pltpu.SemaphoreType.DMA((starts[-1] * tensor,))] * 2,
        collective_id=collective_id,
        has_side_effects=True,
    )


def swap(values, d, t, tensor, dp):
    moves = []
    for p in range(dp):
        for q in range(tensor):
            moves.append((p * tensor + q, (p ^ d) * tensor + (q ^ t)))
    return lax.ppermute(values, ("dp", "tensor"), moves)


def send_plane(parts, tensor, dp):
    return [swap(parts[k], 2 * (k % 2), k // 2, tensor, dp) for k in range(1, 2 * tensor)]


def sum_plane(part, landed, dp):
    planes = []
    for z in range(dp // 4):
        total = part[z].astype(f32)
        for piece in landed:
            total = total + piece[z].astype(f32)
        planes.append(total.astype(bf16))
    return planes


def send_line(planes, tensor, dp):
    return [swap(planes[z], 4 * z, 0, tensor, dp) for z in range(1, dp // 4)]


def pack_kernel(
    heads_ref, merge_ref, expand_ref, hb_ref, eb_ref, *refs
):
    small, (first_ref, later_ref) = refs[:-2], refs[-2:]
    _, part, own = heads_ref.shape
    for s in range(3):
        first_ref[:part, s * own : (s + 1) * own] = heads_ref[s]
    lines = [ref[...].astype(f32) for ref in small] + [jnp.zeros((8 - len(small), part), f32)]
    hb = hb_ref[...].astype(f32)
    hb = hb.reshape(hb.shape[0] * hb.shape[1], hb.shape[2])
    eb = eb_ref[...].astype(f32)
    pieces = []
    for piece in (jnp.concatenate(lines, axis=0), eb, hb):
        height, width = piece.shape
        if height < 8:
            piece = jnp.concatenate([piece, jnp.zeros((8 - height, width), f32)], axis=0)
        pieces.append(piece)
    used = sum(piece.shape[1] for piece in pieces)
    pieces.append(jnp.zeros((8, 128 - used), f32))
    first_ref[part:, :128] = jnp.concatenate(pieces, axis=1).astype(bf16)
    first_ref[part:, 128:] = jnp.zeros((8, 3 * own - 128), bf16)
    hidden = expand_ref.shape[1]
    later_ref[:, :hidden] = expand_ref[...]
    later_ref[:, hidden:] = merge_ref[...]


def gather_kernel(in_ref, out_ref, own_sem, send_sem, recv_sem):
    d, y = lax.axis_index("dp"), lax.axis_index("tensor")
    z, x, c = lax.div(d, 4), lax.rem(lax.div(d, 2), 2), lax.rem(d, 2)
    far_x, far_y, far_c = 1 - x, 1 - y, 1 - c
    barrier = pltpu.get_barrier_semaphore()

    def index(place):
        pz, px, pc, py = place
        return (pz * 2 + px) * 2 + pc, py

    lower, upper = (z - 1, x, c, y), (z + 1, x, c, y)
    to_x, to_y, to_c = (z, far_x, c, y), (z, x, c, far_y), (z, x, far_c, y)

    def greet(peer):
        pl.semaphore_signal(barrier, inc=1, device_id=index(peer), device_id_type=pl.DeviceIdType.MESH)

    for peer in (to_x, to_y, to_c):
        greet(peer)
    pl.when(z > 0)(lambda: greet(lower))
    pl.when(z < 3)(lambda: greet(upper))
    pl.semaphore_wait(barrier, 4 + lax.rem(lax.div(z + 1, 2), 2))

    sent = []

    def copy(owner, peer, slot, source=None):
        p, q = index(owner)
        return pltpu.make_async_remote_copy(
            src_ref=out_ref.at[q, p] if source is None else source,
            dst_ref=out_ref.at[q, p],
            send_sem=send_sem.at[slot],
            recv_sem=recv_sem.at[p * 2 + q],
            device_id=index(peer),
            device_id_type=pl.DeviceIdType.MESH,
        )

    def send(owner, peer, there, source=None):
        slot = len(sent)
        sent.append((owner, peer, slot, there))

        @pl.when(there)
        def _():
            copy(owner, peer, slot, source).start()

    def arrive(owner, there):
        @pl.when(there)
        def _():
            copy(owner, to_c, 0).wait_recv()

    own = (z, x, c, y)
    keep = pltpu.make_async_copy(in_ref, out_ref.at[y, d], own_sem)
    send(own, upper, z < 3, in_ref)
    send(own, lower, z > 0, in_ref)
    for peer in (to_x, to_y, to_c):
        send(own, peer, z >= 0, in_ref)
    keep.start()
    for far in range(1, 4):
        for sign, after, onward in ((-1, upper, z < 3), (1, lower, z > 0)):
            level = z + sign * far
            there = (level >= 0) & (level <= 3)
            block = (level, x, c, y)
            arrive(block, there)
            send(block, after, there & onward)
            for peer in (to_x, to_y, to_c):
                send(block, peer, there)
    for far in range(4):
        for sign in (-1, 1) if far else (1,):
            level = z + sign * far
            there = (level >= 0) & (level <= 3)
            odd = lax.rem(level + 4, 2)
            block = (level, far_x, c, y)
            arrive(block, there)
            send(block, to_y, there & (odd == 0))
            send(block, to_c, there)
            block = (level, x, c, far_y)
            arrive(block, there)
            send(block, to_x, there & (odd == 1))
            send(block, to_c, there)
    for far in range(4):
        for sign in (-1, 1) if far else (1,):
            level = z + sign * far
            there = (level >= 0) & (level <= 3)
            block = (level, far_x, c, far_y)
            arrive(block, there)
            send(block, to_c, there)
    for level in range(4):
        for px in range(2):
            for py in range(2):
                arrive((level, px, far_c, py), z >= 0)
    for owner, peer, slot, there in sent:
        pl.when(there)(lambda: copy(owner, peer, slot).wait_send())
    keep.wait()


def gather_first(shard, tensor, dp):
    shape = (tensor, dp) + shard.shape
    if (tensor, dp) != (2, 16):
        return lax.all_gather(shard, AXES, axis=0, tiled=True).reshape(shape)
    return call(
        gather_kernel,
        "gather",
        (),
        [pl.BlockSpec(memory_space=pltpu.VMEM)],
        [pl.BlockSpec(memory_space=pl.ANY)],
        [(shape, bf16)],
        (shard,),
        [pltpu.SemaphoreType.DMA, pltpu.SemaphoreType.DMA((64,)), pltpu.SemaphoreType.DMA((32,))],
        collective_id=1,
        has_side_effects=True,
    )[0]


def last_kernel(dp, tensor, act_ref, resid_ref, vec_ref, w_ref, *refs):
    count, depth = dp * tensor, dp // 4
    own_ref, others, refs = refs[0], refs[1 : 2 * tensor], refs[2 * tensor :]
    one_ref, two_ref, hb_ref, eb_ref, out_ref, heads_ref, sums_ref = refs[:7]
    packed, landed, line, arrived, send_sem, recv_sem, line_send, line_recv = refs[7:]
    step = pl.program_id(0)
    d, y = lax.axis_index("dp"), lax.axis_index("tensor")
    me = d * tensor + y
    part = own_ref.shape[1]
    barrier = pltpu.get_barrier_semaphore()

    def place(k):
        other = lax.rem(me + k, count)
        return other, (lax.div(other, tensor), lax.rem(other, tensor))

    def greet(k, carry):
        _, where = place(k)
        pl.semaphore_signal(barrier, inc=1, device_id=where, device_id_type=pl.DeviceIdType.MESH)
        return carry

    def plane(z):
        total = own_ref[z].astype(f32)
        for ref in others:
            total = total + ref[z].astype(f32)
        return total

    @pl.when(step == 0)
    def _():
        lax.fori_loop(1, count, greet, 0)
        for z in range(1, depth):
            line[z - 1] = plane(z).astype(bf16)
        heads = hb_ref.shape[1] // HEAD_DIM
        own_heads, hb_wide = heads // tensor, HEAD_DIM // dp
        eb_tall, eb_wide = eb_ref.shape[0] // tensor, eb_ref.shape[1] // dp
        hb = [
            hb_ref[k : k + 1, h * HEAD_DIM : (h + 1) * HEAD_DIM] for k in range(2) for h in range(heads)
        ]
        hb = jnp.concatenate(hb, axis=0).T
        eb = eb_ref[...].T
        sums = jnp.concatenate([one_ref[...], two_ref[3:4], two_ref[1:3], two_ref[0:1]], axis=0)
        for p in range(dp):
            piece = sums[:, p * part : (p + 1) * part]
            for q in range(tensor):
                packed[p * tensor + q, 0:6, 0:part] = piece
                packed[p * tensor + q, 0:eb_wide, part : part + eb_tall] = eb[
                    p * eb_wide : (p + 1) * eb_wide, q * eb_tall : (q + 1) * eb_tall
                ]
                for k in range(2):
                    lane = part + eb_tall + k * own_heads
                    packed[p * tensor + q, 0:hb_wide, lane : lane + own_heads] = hb[
                        p * hb_wide : (p + 1) * hb_wide,
                        k * heads + q * own_heads : k * heads + (q + 1) * own_heads,
                    ]

    copies = [
        pltpu.make_async_remote_copy(
            src_ref=line.at[z - 1],
            dst_ref=arrived.at[z - 1],
            send_sem=line_send.at[z - 1],
            recv_sem=line_recv.at[z - 1],
            device_id=(flip(d, 4 * z), y),
            device_id_type=pl.DeviceIdType.MESH,
        )
        for z in range(1, depth)
    ]

    def copy(k):
        other, where = place(k)
        return pltpu.make_async_remote_copy(
            src_ref=packed.at[other],
            dst_ref=landed.at[k],
            send_sem=send_sem.at[k],
            recv_sem=recv_sem.at[k],
            device_id=where,
            device_id_type=pl.DeviceIdType.MESH,
        )

    def start(k, carry):
        copy(k).start()
        return carry

    @pl.when(step == 0)
    def _():
        pl.semaphore_wait(barrier, count - 1)
        lax.fori_loop(1, count, start, 0)
        for item in copies:
            item.start()

    total = resid_ref[...] + vec_ref[5:6]
    width = w_ref.shape[3]
    for t in range(tensor):
        w = w_ref[t].reshape(dp * part, width)
        total = total + matmul(act_ref[:, t * width : (t + 1) * width], w, NT)
    out_ref[...] = total.astype(bf16)

    def finish(k, sums):
        copy(k).wait()
        return sums + landed[k]

    @pl.when(step == pl.num_programs(0) - 1)
    def _():
        sums_ref[...] = lax.fori_loop(1, count, finish, packed[me])
        total = plane(0)
        for item, z in zip(copies, range(1, depth)):
            item.wait()
            total = total + arrived[z - 1].astype(f32)
        own = heads_ref.shape[2]
        for s in range(3):
            heads_ref[s] = total[:, s * own : (s + 1) * own]


def finish_kernel(depth, *refs):
    given_ref, *refs = refs
    sums_ref, heads_ref, reduced_ref, *refs = refs
    planes, refs = refs[:depth], refs[depth:]
    copy_ref, *refs = refs
    copy_ref[...] = given_ref[...]
    reduce_ref, expand_ref, merge_ref, out_ref, hb_ref, eb_ref, *vectors = refs
    total = planes[0][...].astype(f32)
    for ref in planes[1:]:
        total = total + ref[...].astype(f32)
    hidden = expand_ref.shape[1]
    expand_ref[...] = total[:, :hidden]
    merge_ref[...] = total[:, hidden:]
    reduce_ref[...] = reduced_ref[...].astype(f32)
    out_ref[...] = heads_ref[...]
    part = vectors[0].shape[1]
    for r, ref in enumerate(vectors):
        ref[...] = sums_ref[r : r + 1, :part]
    wide, tall = eb_ref.shape
    eb_ref[...] = sums_ref[:wide, part : part + tall]
    wide, count = hb_ref.shape[1:]
    for k in range(2):
        lane = part + tall + k * count
        hb_ref[k] = sums_ref[:wide, lane : lane + count]


def shards(
    tensor,
    dp,
    activations,
    first_gain,
    first_shift,
    heads_weight,
    heads_bias,
    merge_weight,
    merge_bias,
    second_gain,
    second_shift,
    expand_weight,
    expand_bias,
    reduce_weight,
    reduce_bias,
    output_grad,
    real_images,
):
    rows, deep = activations.shape
    images = rows // SEQ
    part = deep // dp
    own = heads_weight.shape[2]
    hidden_own = expand_weight.shape[1]
    hidden = hidden_own * tensor
    heads = deep // HEAD_DIM
    least = (images - 1) * STRIDE + WINDOW
    blocks = -(-least // 512)
    block = -(-least // blocks // 16) * 16
    total_rows = block * blocks

    def gather(shard):
        out = lax.all_gather(shard, AXES, axis=0, tiled=True)
        return out.reshape(tensor, dp, *shard.shape)

    small = [first_gain, first_shift, merge_bias, second_gain, second_shift, reduce_bias]
    arrays = [
        heads_weight, merge_weight.T, expand_weight,
        heads_bias.transpose(0, 2, 1), expand_bias.T,
    ] + [v.reshape(1, part) for v in small]
    vmem = pl.BlockSpec(memory_space=pltpu.VMEM)
    first, later = call(
        pack_kernel, "pack", (), [vmem] * len(arrays), [vmem] * 2,
        [((part + 8, 3 * own), bf16), ((part, hidden_own + own), bf16)], arrays,
    )
    wide = gather(later)
    wide_heads = gather_first(first, tensor, dp)
    wide_heads, turned = lax.optimization_barrier((wide_heads, reduce_weight.T))
    wide_reduce = gather(turned)

    hbs, ebs = heads_bias.shape, expand_bias.shape
    small = wide_heads[:, :, part:, :128].astype(f32)
    vectors = small[0, :, :6, :part].transpose(1, 0, 2).reshape(6, deep)
    eb = small[:, :, : ebs[1], part : part + ebs[0]].transpose(0, 3, 1, 2).reshape(1, hidden)
    hb = small[:, :, : 2 * hbs[2], part + ebs[0] : part + ebs[0] + hbs[1]]
    hb = hb.reshape(tensor, dp, 2, hbs[2], hbs[1]).transpose(2, 0, 4, 1, 3).reshape(2, deep)
    live = jnp.clip(real_images - lax.axis_index("tensor") * images, 0, images) * SEQ

    def by_rows(width):
        return pl.BlockSpec((block, width), lambda i, *_: (i, 0))

    def columns(array, index, width):
        shape = array.shape[:3] + (width,)
        return pl.BlockSpec(shape, lambda *_: (0, 0, 0, index), pipeline_mode=pl.Buffered(1))

    vec = full((6, deep))
    expand_spec, merge_spec = columns(wide, 0, hidden_own), columns(wide, hidden_own // own, own)
    triple_spec = pl.BlockSpec((3, block, deep), lambda i: (0, i, 0))
    normed_one, triple = call(
        functools.partial(qkv_kernel, part, rows),
        "qkv",
        (blocks,),
        [by_rows(deep), vec, full((2, deep)), full(wide_heads.shape)],
        [by_rows(deep), triple_spec],
        [((total_rows, deep), bf16), ((3, total_rows, deep), bf16)],
        (activations, vectors, hb, wide_heads),
        flops=total_rows * deep * deep * 3,
    )

    group = 4
    groups = heads // group
    panel = group * HEAD_DIM
    head_spec = pl.BlockSpec((3, total_rows, panel), lambda g, i: (0, 0, g))
    ctx_spec = pl.BlockSpec((total_rows, panel), lambda g, i: (0, g))
    stat_spec = pl.BlockSpec((1, group, WINDOW), lambda g, i: (g * images + i, 0, 0))
    attend_flops = images * heads * WINDOW * 768 * 256 * 2
    context, stat = call(
        attend_kernel,
        "attend",
        (groups, images),
        [head_spec],
        [ctx_spec, stat_spec],
        [((total_rows, deep), bf16), ((images * groups, group, WINDOW), f32)],
        (triple,),
        flops=attend_flops,
    )

    resid, normed_two = call(
        functools.partial(merge_kernel, rows),
        "merge",
        (blocks,),
        [by_rows(deep), by_rows(deep), vec, merge_spec],
        [by_rows(deep), by_rows(deep)],
        [((total_rows, deep), f32), ((total_rows, deep), bf16)],
        (context, activations, vectors, wide),
        flops=total_rows * deep * deep,
    )

    chunk = min(512, hidden_own)
    per = hidden_own // chunk
    chunk_spec = pl.BlockSpec((total_rows, chunk), lambda c, *_: (0, c))
    shard_spec = pl.BlockSpec((1, dp, part, chunk), lambda c, *_: (c // per, 0, 0, c % per))
    active, slope, grad_reduce = call(
        expand_kernel,
        "expand",
        (hidden // chunk,),
        [
            full((total_rows, deep)), full((rows, deep)),
            pl.BlockSpec((1, chunk), lambda c, *_: (0, c)), shard_spec,
        ],
        [chunk_spec, chunk_spec, shard_spec],
        [
            ((total_rows, hidden), bf16), ((total_rows, hidden), bf16),
            ((tensor, dp, part, hidden_own), bf16),
        ],
        (live, normed_two, output_grad, eb, wide),
        [pltpu.VMEM((total_rows, deep), bf16)],
        flops=total_rows * deep * hidden * 2,
        prefetch=1,
    )
    grad_reduce = grad_reduce.reshape(tensor * dp * part, hidden_own)
    grad_reduce = lax.psum_scatter(grad_reduce, AXES, scatter_dimension=0, tiled=True)

    back_chunk = min(2048, hidden_own)
    pre_grad, resid_low, grad_context, sums_two, esum = call(
        functools.partial(mlp_back_kernel, back_chunk),
        "mlp_back",
        (blocks,),
        [
            by_rows(deep), by_rows(hidden), by_rows(deep), vec,
            expand_spec, full(wide_reduce.shape), merge_spec,
        ],
        [
            by_rows(hidden), by_rows(deep), by_rows(deep),
            pl.BlockSpec((4, deep), lambda *_: (0, 0)), pl.BlockSpec((hidden // 128, 128), lambda *_: (0, 0)),
        ],
        [
            ((total_rows, hidden), bf16), ((total_rows, deep), bf16), ((total_rows, deep), bf16),
            ((4, deep), f32), ((hidden // 128, 128), f32),
        ],
        (live, output_grad, slope, resid, vectors, wide, wide_reduce, wide),
        prefetch=1,
    )
    parts = slot_grads(
        "middle_grad", [(normed_two, pre_grad[None]), (resid_low, context[None])], tensor, dp, 512, 2
    )
    *parts, grad_context = lax.optimization_barrier((*parts, grad_context))
    landed = send_plane(parts, tensor, dp)
    grad_triple = call(
        attend_back_kernel,
        "attend_back",
        (groups, images),
        [head_spec, stat_spec, ctx_spec],
        [head_spec],
        [((3, total_rows, deep), bf16)],
        (triple, stat, grad_context),
    )[0]
    heads = slot_grads("heads_grad", [(normed_one, grad_triple)], tensor, dp, 512, 3)
    held = (tuple(heads), tuple(landed), parts[0], resid_low)
    heads, landed, part_own, resid_low = lax.optimization_barrier(held)
    last = send_plane(heads, tensor, dp)
    planes = sum_plane(part_own, landed, dp)
    planes, resid_low = lax.optimization_barrier((tuple(planes), resid_low))
    line = send_line(planes, tensor, dp)

    def whole(shape):
        return pl.BlockSpec(shape, lambda *_: (0,) * len(shape))

    shapes = [(2, deep), (2, deep)]
    input_grad, sums_one, bsum = call(
        functools.partial(qkv_back_kernel, part, rows),
        "qkv_back",
        (blocks,),
        [by_rows(deep), by_rows(deep), vec, triple_spec, full(wide_heads.shape)],
        [by_rows(deep)] + [whole(shape) for shape in shapes],
        [((rows, deep), bf16)] + [(shape, f32) for shape in shapes],
        (activations, resid_low, vectors, grad_triple, wide_heads),
        flops=total_rows * deep * deep * 3,
    )

    hbs, ebs = heads_bias.shape, expand_bias.shape
    depth = dp // 4
    arrays = [heads[0], *last, sums_one, sums_two, bsum, esum]
    output, heads_sum, sums = call(
        functools.partial(last_kernel, dp, tensor),
        "reduce",
        (blocks,),
        [by_rows(hidden), by_rows(deep), vec, full(wide_reduce.shape)] + [full(v.shape) for v in arrays],
        [by_rows(deep), whole((3, part, own)), whole((8, 128))],
        [((rows, deep), bf16), ((3, part, own), f32), ((8, 128), f32)],
        (active, resid, vectors, wide_reduce, *arrays),
        [
            pltpu.VMEM((tensor * dp, 8, 128), f32), pltpu.VMEM((tensor * dp, 8, 128), f32),
            pltpu.VMEM((depth - 1, part, 3 * own), bf16), pltpu.VMEM((depth - 1, part, 3 * own), bf16),
            pltpu.SemaphoreType.DMA((tensor * dp,)), pltpu.SemaphoreType.DMA((tensor * dp,)),
            pltpu.SemaphoreType.DMA((depth - 1,)), pltpu.SemaphoreType.DMA((depth - 1,)),
        ],
        flops=total_rows * deep * hidden,
        collective_id=0,
        has_side_effects=True,
    )
    shapes = [(part, hidden_own), (part, hidden_own), (part, own)]
    shapes += [heads_sum.shape, (2, hbs[2], hbs[1]), ebs[::-1]] + [(1, part)] * 6
    arrays = [sums, heads_sum, grad_reduce, planes[0], *line]
    piece = pl.BlockSpec((total_rows // 2, deep), lambda i: (i, 0))
    output, grad_reduce, grad_expand, grad_merge, grad_heads, hb_grad, eb_grad, *vector = call(
        functools.partial(finish_kernel, depth),
        "finish",
        (2,),
        [piece] + [full(v.shape) for v in arrays],
        [piece] + [whole(shape) for shape in shapes],
        [((rows, deep), bf16)] + [(shape, f32) for shape in shapes],
        [output] + arrays,
    )
    vector = [v.reshape(part) for v in vector]

    return (
        output,
        input_grad,
        vector[0],
        vector[1],
        grad_heads,
        hb_grad.transpose(0, 2, 1),
        grad_merge.T,
        vector[2],
        vector[3],
        vector[4],
        grad_expand,
        eb_grad.T,
        grad_reduce.T,
        vector[5],
    )


def solution(mesh):
    rows = P(("dp", "tensor"), None)
    specs = (
        P("dp"),
        P("dp"),
        P(None, "dp", "tensor"),
        P(None, "tensor", "dp"),
        P("tensor", "dp"),
        P("dp"),
        P("dp"),
        P("dp"),
        P("dp", "tensor"),
        P("tensor", "dp"),
        P("tensor", "dp"),
        P("dp"),
    )
    return jax.shard_map(
        functools.partial(shards, mesh.shape["tensor"], mesh.shape["dp"]),
        mesh=mesh,
        in_specs=(rows,) + specs + (rows, P("dp")),
        out_specs=(rows, rows) + specs,
        check_vma=False,
    )
```
